128 devices in a mesh: tm: 4 (over x), lat: 32 (over z, y, core).
Axes of the slice: x: 4, y: 4, z: 4, core: 2. Of those that a mesh axis runs over, the one named last changes fastest.
Arguments:
- sketch: bfloat16 [256, 3, 256, 1024], P('tm', None, 'lat'), may hold values from -6 to 6
- test_sketch: bfloat16 [256, 3, 256, 1024], P('tm', None, 'lat'), may hold values from -6 to 6
- checkpoints: bfloat16 [16, 3, 256, 1024], P('tm', None, 'lat'), may hold values from -2.5 to 2.5
- checkpoint_step: int32 [4], P('tm'), may hold values from 0 to 3
- station_row: int32 [4, 4096], P('tm', 'lat'), may hold values from 0 to 255, as said below
- station_column: int32 [4, 4096], P('tm', 'lat'), may hold values from 0 to 1023
- station_value: float32 [4, 4096], P('tm', 'lat'), may hold values from -6 to 6
Outputs:
- increment: float32 [4, 3, 256, 1024], P('tm', None, 'lat')
- reduced_adjoint: float32 [4, 64], P('tm')
- total_cost: float32 [], replicated
The draws below stay inside these ranges and needn't reach their ends.
Inputs may be any that keep to these rules, and one draw needn't show every extreme that they name: `station_row`: in each group's list, entries 128 * j to 128 * (j + 1) - 1 lie in latitude rows 8 * j to 8 * (j + 1) - 1.
All inputs are finite; a program needn't handle non-finite values.
Results may differ from the reference program's by a relative error of at most 0.0003.
Values may be sent and summed in bfloat16 or wider, within the bound.
No kernel may reach another device: no remote copies, remote signals or barrier semaphores. Data moves between devices by JAX's collectives and lax.ppermute only.
A program may use at most 128 MiB of HBM per device.

```python
import math
import jax
import jax.numpy as jnp
from jax import lax

K = 64
ROWS = 8
NLON = 1024
STEPS = 4
NCK = 4
OBS_DEV = 128
NLAT = 256
NOBS = 4096
N_TM = 4


def draw_station_row(key, part):
    band = jnp.arange(NOBS, dtype=jnp.int32) // OBS_DEV
    offset = jax.random.randint(key, (N_TM, NOBS), 0, ROWS, dtype=jnp.int32)
    return band[None, :] * ROWS + offset


def plant(values, key, least, top_value):
    longest = values.shape.index(max(values.shape))
    spots = []
    for shift in (0, 1):
        where = [jax.random.randint(jax.random.fold_in(key, axis), (), 0, length) for axis, length in enumerate(values.shape)]
        where[longest] = (where[longest] + shift) % values.shape[longest]
        spots.append(tuple(where))
    return values.at[spots[0]].set(least).at[spots[1]].set(top_value)


def block_levels(own_key, shape, cuts, low, top_value):
    def one(position, parts):
        draws = jax.random.uniform(jax.random.fold_in(jax.random.fold_in(own_key, 6), position), (parts,), jnp.float32, low / len(cuts), top_value / len(cuts))
        return jnp.repeat(jnp.exp(draws), shape[position] // parts).reshape((-1,) + (1,) * (len(shape) - position - 1))

    factor_of = one(*cuts[0])
    for cut in cuts[1:]:
        factor_of = factor_of * one(*cut)
    return factor_of


def gaussian(key, extent, spread, reach, split=(), kind=jnp.bfloat16):
    loudness = block_levels(key, extent, split, -0.22, 0.18) if split else 1.0
    drawn = jax.random.normal(key, extent, jnp.float32) * spread * loudness
    return jnp.minimum(jnp.maximum(drawn, -reach), reach).astype(kind)


def setup_inputs(seed: int = 0) -> dict:
    arg_keys = jax.random.split(jax.random.key(seed), 8)
    return {
        "sketch": gaussian(arg_keys[0], (N_TM * K, 3, NLAT, NLON), 1.0, 6.0, ((0, 4), (2, 32))),
        "test_sketch": gaussian(arg_keys[1], (N_TM * K, 3, NLAT, NLON), 1.0, 6.0, ((0, 4), (2, 32))),
        "checkpoints": gaussian(arg_keys[2], (N_TM * NCK, 3, NLAT, NLON), 1.0, 2.5, ((0, 4), (2, 32))),
        "checkpoint_step": plant(jax.random.randint(arg_keys[3], (N_TM,), 0, NCK), jax.random.fold_in(arg_keys[3], 1), 0, NCK - 1).astype(jnp.int32),
        "station_row": draw_station_row(jax.random.fold_in(arg_keys[7], 71), 0),
        "station_column": plant(jax.random.randint(arg_keys[5], (N_TM, NOBS), 0, NLON), jax.random.fold_in(arg_keys[5], 1), 0, NLON - 1).astype(jnp.int32),
        "station_value": gaussian(arg_keys[6], (N_TM, NOBS), 1.0, 6.0, ((0, 4), (1, 32)), jnp.float32),
    }


wave_coef = 0.5
flow_coef = 0.4
coriolis_coef = 0.5
map_scale = 0.5

def coefficients(base_rows, first_row, total_rows):
    values = base_rows.astype(jnp.float32)
    depth = 1.0 + 0.25 * values[0]
    east_flow = 0.4 * values[1]
    north_flow = 0.4 * values[2]
    latitude = (first_row + jnp.arange(values.shape[1], dtype=jnp.int32)).astype(jnp.float32)
    coriolis = coriolis_coef * (2.0 * (latitude + 0.5) / total_rows - 1.0)
    return (depth, east_flow, north_flow, coriolis[:, None])

def advance(padded, depth, east_flow, north_flow, coriolis):
    height = padded[:, 0]
    eastward = padded[:, 1]
    northward = padded[:, 2]

    def along_lon(field):
        middle = field[:, 1:-1]
        return 0.5 * (jnp.roll(middle, -1, -1) - jnp.roll(middle, 1, -1))

    def along_lat(field):
        return 0.5 * (field[:, 2:] - field[:, :-2])
    centre_height = height[:, 1:-1]
    centre_east = eastward[:, 1:-1]
    centre_north = northward[:, 1:-1]
    new_east = centre_east + wave_coef * (coriolis * centre_north - along_lon(height)) - flow_coef * (east_flow * along_lon(eastward) + north_flow * along_lat(eastward))
    new_north = centre_north + wave_coef * (-coriolis * centre_east - along_lat(height)) - flow_coef * (east_flow * along_lon(northward) + north_flow * along_lat(northward))
    new_height = centre_height - wave_coef * depth * (along_lon(eastward) + along_lat(northward)) - flow_coef * (east_flow * along_lon(height) + north_flow * along_lat(height))
    return jnp.stack([new_height, new_east, new_north], 1)

def one_group(inputs):
    basis, tests, stored, chosen, rows, columns, values = inputs
    base = lax.dynamic_index_in_dim(stored, chosen, 0, keepdims=False)
    depth, east_flow, north_flow, coriolis = coefficients(base, 0, NLAT)
    state = basis.astype(jnp.float32)
    for step_index in range(STEPS):
        padded = jnp.pad(state, ((0, 0), (0, 0), (1, 1), (0, 0)))
        state = advance(padded, depth, east_flow, north_flow, coriolis)
    propagator = lax.dot_general(tests.reshape(K, -1).astype(jnp.float32), state.reshape(K, -1), (((1,), (1,)), ((), ())), precision=lax.Precision.HIGHEST, preferred_element_type=jnp.float32) * (map_scale / math.sqrt(K * 3 * NLAT * NLON))
    flat = (rows * NLON + columns).astype(jnp.int32)
    heights = basis[:, 0].reshape(K, -1)
    sampled = jnp.take(heights, flat, axis=1).astype(jnp.float32)
    innovation = jnp.take(base[0].reshape(-1), flat).astype(jnp.float32) - values
    weight = 1.0 + 2.0 * rows.astype(jnp.float32) / NLAT
    forcing = jnp.dot(sampled, weight * innovation, precision=lax.Precision.HIGHEST) / (2.0 * math.sqrt(NOBS))
    cost = jnp.sum(weight * innovation * innovation) / (2.0 * N_TM * NOBS)
    return (state, propagator, forcing, cost)

def reference(sketch, test_sketch, checkpoints, checkpoint_step, station_row, station_column, station_value):
    inputs = (sketch.reshape(N_TM, K, 3, NLAT, NLON), test_sketch.reshape(N_TM, K, 3, NLAT, NLON), checkpoints.reshape(N_TM, NCK, 3, NLAT, NLON), checkpoint_step, station_row, station_column, station_value)
    states, propagators, forcings, costs = lax.map(one_group, inputs)
    following = jnp.zeros((K,), jnp.float32)
    adjoints = [None] * N_TM
    for group in reversed(range(N_TM)):
        adjoint = jnp.dot(propagators[group].T, following, precision=lax.Precision.HIGHEST) + forcings[group]
        adjoints[group] = adjoint
        following = adjoint
    adjoint_stack = jnp.stack(adjoints)
    increment = jnp.einsum('gk,gkfrc->gfrc', adjoint_stack, states, precision=lax.Precision.HIGHEST) / math.sqrt(K)
    return (increment, adjoint_stack, jnp.sum(costs))
```

```python
import functools
import math

import jax
import jax.numpy as jnp
from jax import lax
from jax.experimental import pallas as pl
from jax.experimental.pallas import tpu as pltpu
from jax.sharding import Mesh
from jax.sharding import PartitionSpec as P

STEPS = 4
LAT = ("lat_0", "lat_1", "lat_2")
KC = 16
HALO = STEPS

flow_coef = 0.4
coriolis_coef = 0.5
map_scale = 0.5
MIB = 1 << 20


def rows_first(block):
    columns, fields, rows, lon = block.shape
    parts = []
    for f in range(fields):
        part = block[:, f].astype(jnp.float32)
        parts.append(jnp.swapaxes(part, 0, 1))
    return parts


def pack_kernel(step_ref, sketch_ref, base_ref, low_ref, high_ref):
    chunk = pl.program_id(0)
    fields = sketch_ref.shape[1]
    size = fields * HALO
    for f, part in enumerate(rows_first(sketch_ref)):
        part = part.astype(low_ref.dtype)
        low_ref[pl.ds(chunk * size + f * HALO, HALO)] = part[:HALO]
        high_ref[pl.ds(chunk * size + f * HALO, HALO)] = part[HALO:]

    @pl.when(chunk == 0)
    def _():
        last = low_ref.shape[0] - 1
        values = base_ref[0].astype(jnp.float32)
        pad = jnp.zeros((KC - size, values.shape[-1]), jnp.float32)
        for ref, at in ((low_ref, 0), (high_ref, HALO)):
            rows = [values[f, at : at + HALO] for f in range(fields)]
            ref[last] = jnp.concatenate([*rows, pad], axis=0).astype(ref.dtype)


def pack(sketch, checkpoints, checkpoint_step):
    rank, fields, rows, lon = sketch.shape
    chunks = rank // KC
    out = jax.ShapeDtypeStruct((chunks * fields * HALO + 1, KC, lon), sketch.dtype)
    whole = pl.BlockSpec(out.shape, lambda c, s: (0, 0, 0))
    return pl.pallas_call(
        pack_kernel,
        out_shape=(out, out),
        grid_spec=pltpu.PrefetchScalarGridSpec(
            num_scalar_prefetch=1,
            grid=(chunks,),
            in_specs=[
                pl.BlockSpec((KC, fields, rows, lon), lambda c, s: (c, 0, 0, 0)),
                pl.BlockSpec((1, fields, rows, lon), lambda c, s: (s[0], 0, 0, 0)),
            ],
            out_specs=(whole, whole),
        ),
        compiler_params=pltpu.CompilerParams(vmem_limit_bytes=24 * MIB),
        name="pack",
    )(checkpoint_step, sketch, checkpoints)


def split3(x):
    high = x.astype(jnp.bfloat16)
    rest = x - high.astype(jnp.float32)
    middle = rest.astype(jnp.bfloat16)
    low = (rest - middle.astype(jnp.float32)).astype(jnp.bfloat16)
    return high, middle, low


def window_kernel(
    scales, step_ref, band_ref, test_ref, base_ref, row_ref, column_ref, value_ref, tests_ref, field_ref, cost_ref
):
    for f, part in enumerate(rows_first(test_ref)):
        tests_ref[f] = part.astype(tests_ref.dtype)

    @pl.when(pl.program_id(0) == 0)
    def _():
        total_rows, observed, groups = scales
        rows, lon = base_ref.shape[-2:]
        count = row_ref.shape[-1]
        station_row = row_ref[...]
        local = station_row - band_ref[0] * rows
        at_column = lax.broadcasted_iota(jnp.int32, (lon, count), 0) == column_ref[...]
        at_column = jnp.where(at_column, 1.0, 0.0).astype(jnp.bfloat16)
        at_row = lax.broadcasted_iota(jnp.int32, (rows, count), 0) == local
        found = lax.dot_general(
            base_ref[0, 0], at_column, (((1,), (0,)), ((), ())), preferred_element_type=jnp.float32
        )
        here = jnp.sum(jnp.where(at_row, found, 0.0), axis=0, keepdims=True)
        innovation = here - value_ref[...]
        weight = 1.0 + 2.0 * station_row.astype(jnp.float32) / total_rows
        weighted = weight * innovation
        cost = jnp.sum(weighted * innovation, axis=1, keepdims=True) / (2.0 * groups * observed)
        cost_ref[...] = jnp.broadcast_to(cost, cost_ref.shape)
        spread = jnp.where(at_row, weighted / (2.0 * math.sqrt(observed)), 0.0)
        field = jnp.zeros((rows, lon), jnp.float32)
        for piece in split3(spread):
            field += lax.dot_general(
                piece, at_column, (((1,), (1,)), ((), ())), preferred_element_type=jnp.float32
            )
        field_ref[...] = field


def window(test_sketch, checkpoints, checkpoint_step, band, station_row, station_column, station_value, scales):
    rank, fields, rows, lon = test_sketch.shape
    count = station_row.shape[-1]
    small = pl.BlockSpec((1, count), lambda c, s, b: (0, 0))
    return pl.pallas_call(
        functools.partial(window_kernel, scales),
        out_shape=(
            jax.ShapeDtypeStruct((fields, rows, rank, lon), test_sketch.dtype),
            jax.ShapeDtypeStruct((rows, lon), jnp.float32),
            jax.ShapeDtypeStruct((1, 128), jnp.float32),
        ),
        grid_spec=pltpu.PrefetchScalarGridSpec(
            num_scalar_prefetch=2,
            grid=(rank // KC,),
            in_specs=[
                pl.BlockSpec((KC, fields, rows, lon), lambda c, s, b: (c, 0, 0, 0)),
                pl.BlockSpec((1, 1, rows, lon), lambda c, s, b: (s[0], 0, 0, 0)),
                small,
                small,
                small,
            ],
            out_specs=(
                pl.BlockSpec((fields, rows, KC, lon), lambda c, s, b: (0, 0, c, 0)),
                pl.BlockSpec((rows, lon), lambda c, s, b: (0, 0)),
                pl.BlockSpec((1, 128), lambda c, s, b: (0, 0)),
            ),
        ),
        compiler_params=pltpu.CompilerParams(vmem_limit_bytes=24 * MIB),
        cost_estimate=pl.CostEstimate(flops=40_000_000, bytes_accessed=7_000_000, transcendentals=0),
        name="window",
    )(checkpoint_step, band, test_sketch, checkpoints, station_row, station_column, station_value)


def sweep_kernel(
    scale,
    bands,
    band_ref,
    turn_ref,
    below_ref,
    low_ref,
    high_ref,
    above_ref,
    below_base,
    low_base,
    high_base,
    above_base,
    tests_ref,
    field_ref,
    cost_ref,
    state_ref,
    share_ref,
    one,
    two,
    coef,
):
    chunk = pl.program_id(0)
    lon = one.shape[-1]
    rows = 2 * HALO
    fields = one.shape[1]
    band = band_ref[0]

    @pl.when(chunk == 0)
    def _():
        for q, ref in enumerate((below_base, low_base, high_base, above_base)):
            values = ref[0].astype(jnp.float32)
            for r in range(HALO):
                for f in range(fields):
                    line = values[f * HALO + r : f * HALO + r + 1]
                    line = 0.0625 + 0.015625 * line if f == 0 else (0.2 * flow_coef) * line
                    coef[f, q * HALO + r] = jnp.broadcast_to(line, (8, lon))

    forcing = jnp.zeros((KC, lon), jnp.float32)
    for q, ref in enumerate((below_ref, low_ref, high_ref, above_ref)):
        for r in range(HALO):
            for f in range(fields):
                value = ref[f * HALO + r].astype(jnp.float32)
                if f == 0:
                    if q in (1, 2):
                        at = (q - 1) * HALO + r
                        forcing += value * field_ref[at : at + 1]
                    value = 0.25 * value
                one[q * HALO + r, f] = value

    def advance(source, target, r):
        for half in range(KC // 8):
            at = pl.ds(half * 8, 8)
            turn = turn_ref[r]
            depth, east, north = (coef[f, r] for f in range(3))

            def lon_difference(x):
                return pltpu.roll(x, lon - 1, 1) - pltpu.roll(x, 1, 1)

            def lat_difference(f):
                return source[r + 1, f, at] - source[r - 1, f, at]

            h, u, v = (source[r, f, at] for f in range(3))
            dxh, dyh = lon_difference(h), lat_difference(0)
            dxu, dyu = lon_difference(u), lat_difference(1)
            new_u = (u + turn * v) - dxh - east * dxu - north * dyu
            target[r, 1, at] = new_u
            dxv, dyv = lon_difference(v), lat_difference(2)
            new_v = (v - turn * u) - dyh - east * dxv - north * dyv
            target[r, 2, at] = new_v
            new_h = h - depth * (dxu + dyv) - east * dxh - north * dyh
            target[r, 0, at] = new_h

    buffers = (one, two)
    for step in range(STEPS):
        source, target = buffers[step % 2], buffers[(step + 1) % 2]

        def body(r, carry, source=source, target=target):
            advance(source, target, r)
            return carry

        lax.fori_loop(1 + step, 2 * HALO + rows - 1 - step, body, 0)
        if step < STEPS - 1:
            outside = jnp.zeros((HALO - 1, *target.shape[1:]), jnp.float32)

            @pl.when(band == 0)
            def _(target=target):
                target[1:HALO] = outside

            @pl.when(band == bands - 1)
            def _(target=target):
                target[HALO + rows : 2 * HALO + rows - 1] = outside

    final = buffers[STEPS % 2]
    share = jnp.zeros((2 * KC, tests_ref.shape[2]), jnp.float32)
    for f in range(fields):
        for r in range(rows):
            value = final[HALO + r, f]
            if f == 0:
                value = 4.0 * value
            state_ref[f, r] = value
            upper = value.astype(jnp.bfloat16)
            lower = (value - upper.astype(jnp.float32)).astype(jnp.bfloat16)
            share += lax.dot_general(
                jnp.concatenate([upper, lower], axis=0),
                tests_ref[f, r],
                (((1,), (1,)), ((), ())),
                preferred_element_type=jnp.float32,
            )
    share = (share[:KC] + share[KC:]) * scale
    forced = jnp.sum(forcing, axis=1, keepdims=True)
    lane = lax.broadcasted_iota(jnp.int32, (KC, 128 - share.shape[1]), 1)
    tail = jnp.where(lane == 0, forced, jnp.where(lane == 1, cost_ref[0:1, 0:1], 0.0))
    share_ref[...] = jnp.concatenate([share, tail], axis=1)


def sweep(below, low, high, above, tests, field, cost, band, turn, scale, bands):
    fields, rows, rank, lon = tests.shape
    size = fields * HALO
    chunks = rank // KC
    quarter = pl.BlockSpec((size, KC, lon), lambda c, b, t: (c, 0, 0))
    base = pl.BlockSpec((1, KC, lon), lambda c, b, t: (chunks * size, 0, 0))
    return pl.pallas_call(
        functools.partial(sweep_kernel, scale, bands),
        out_shape=(
            jax.ShapeDtypeStruct((fields, rows, rank, lon), jnp.float32),
            jax.ShapeDtypeStruct((rank, 128), jnp.float32),
        ),
        grid_spec=pltpu.PrefetchScalarGridSpec(
            num_scalar_prefetch=2,
            grid=(chunks,),
            in_specs=[
                quarter,
                quarter,
                quarter,
                quarter,
                base,
                base,
                base,
                base,
                pl.BlockSpec((fields, rows, rank, lon), lambda c, b, t: (0, 0, 0, 0)),
                pl.BlockSpec((rows, lon), lambda c, b, t: (0, 0)),
                pl.BlockSpec((1, 128), lambda c, b, t: (0, 0)),
            ],
            out_specs=(
                pl.BlockSpec((fields, rows, KC, lon), lambda c, b, t: (0, 0, c, 0)),
                pl.BlockSpec((KC, 128), lambda c, b, t: (c, 0)),
            ),
            scratch_shapes=[
                pltpu.VMEM((rows + 2 * HALO, fields, KC, lon), jnp.float32),
                pltpu.VMEM((rows + 2 * HALO, fields, KC, lon), jnp.float32),
                pltpu.VMEM((fields, rows + 2 * HALO, 8, lon), jnp.float32),
            ],
        ),
        compiler_params=pltpu.CompilerParams(vmem_limit_bytes=40 * MIB),
        name="sweep",
    )(band, turn, below, low, high, above, below, low, high, above, tests, field, cost)


def combine_kernel(scale, groups, group_ref, *refs):
    shares = refs[:groups]
    state_ref, increment_ref, adjoint_ref, cost_ref, column = refs[groups:]
    rank = shares[0].shape[0]

    @pl.when(pl.program_id(0) == 0)
    def _():
        diagonal = lax.broadcasted_iota(jnp.int32, (rank, rank), 0) == lax.broadcasted_iota(
            jnp.int32, (rank, rank), 1
        )
        row = jnp.zeros((1, rank), jnp.float32)
        cost = jnp.zeros((1, 1), jnp.float32)
        for ahead in reversed(range(groups)):
            share = shares[ahead][...]
            cost += share[0:1, rank + 1 : rank + 2]
            values = jnp.sum(share[:, :rank] * row, axis=1, keepdims=True) + share[:, rank : rank + 1]
            if ahead:
                values = jnp.where(group_ref[0] + ahead < groups, values, 0.0)
            row = jnp.sum(jnp.where(diagonal, values, 0.0), axis=0, keepdims=True)
        adjoint_ref[...] = row
        cost_ref[...] = cost
        column[...] = jnp.broadcast_to(values * scale, column.shape)

    lon = state_ref.shape[-1]
    factor = column[...]
    for r in range(state_ref.shape[1]):
        for at in range(0, lon, 128):
            product = state_ref[0, r, :, at : at + 128] * factor
            increment_ref[0, 0, r : r + 1, at : at + 128] = jnp.sum(product, axis=0, keepdims=True)


def combine(shares, state, group, scale):
    fields, rows, rank, lon = state.shape
    groups = len(shares)
    share = pl.BlockSpec((rank, 128), lambda f, g: (0, 0))
    return pl.pallas_call(
        functools.partial(combine_kernel, scale, groups),
        out_shape=(
            jax.ShapeDtypeStruct((1, fields, rows, lon), jnp.float32),
            jax.ShapeDtypeStruct((1, rank), jnp.float32),
            jax.ShapeDtypeStruct((1, 1), jnp.float32),
        ),
        grid_spec=pltpu.PrefetchScalarGridSpec(
            num_scalar_prefetch=1,
            grid=(fields,),
            in_specs=[share] * groups + [pl.BlockSpec((1, rows, rank, lon), lambda f, g: (f, 0, 0, 0))],
            out_specs=(
                pl.BlockSpec((1, 1, rows, lon), lambda f, g: (0, f, 0, 0)),
                pl.BlockSpec((1, rank), lambda f, g: (0, 0)),
                pl.BlockSpec((1, 1), lambda f, g: (0, 0)),
            ),
            scratch_shapes=[pltpu.VMEM((rank, 128), jnp.float32)],
        ),
        compiler_params=pltpu.CompilerParams(vmem_limit_bytes=24 * MIB),
        name="combine",
    )(group, *shares, state)


def from_ahead(x, axis, by):
    count = lax.axis_size(axis)
    return lax.ppermute(x, axis, [((i + by) % count, i) for i in range(count)])


def added_over(x, axis):
    others = [from_ahead(x, axis, by) for by in range(1, lax.axis_size(axis))]
    return functools.reduce(jnp.add, others, x)


def body(
    sketch, test_sketch, checkpoints, checkpoint_step, station_row, station_column, station_value
):
    rank, fields, rows, lon = sketch.shape
    bands = lax.axis_size(LAT)
    groups = lax.axis_size("tm")
    total_rows = rows * bands
    observed = station_row.shape[1] * bands
    band = lax.axis_index(LAT).astype(jnp.int32).reshape(1)
    group = lax.axis_index("tm").astype(jnp.int32).reshape(1)

    low, high = pack(sketch, checkpoints, checkpoint_step)
    forward = [(i, i + 1) for i in range(bands - 1)]
    backward = [(target, source) for source, target in forward]
    below = lax.ppermute(high, LAT, forward)
    above = lax.ppermute(low, LAT, backward)
    tests, field, cost = window(
        test_sketch,
        checkpoints,
        checkpoint_step,
        band,
        station_row,
        station_column,
        station_value,
        (total_rows, observed, groups),
    )
    latitude = band * rows - HALO + jnp.arange(rows + 2 * HALO, dtype=jnp.int32)
    turn = 0.5 * coriolis_coef * (2.0 * (latitude.astype(jnp.float32) + 0.5) / total_rows - 1.0)
    scale = map_scale / math.sqrt(rank * fields * total_rows * lon)
    state, share = sweep(below, low, high, above, tests, field, cost, band, turn, scale, bands)
    for axis in ("lat_2", "lat_1", "lat_0"):
        share = added_over(share, axis)
    shares = [share] + [from_ahead(share, "tm", by) for by in range(1, groups)]
    increment, adjoint, total_cost = combine(shares, state, group, 1.0 / math.sqrt(rank))
    return (increment, adjoint, total_cost.reshape(()))


def solution(mesh):
    torus = Mesh(mesh.devices.reshape(mesh.shape["tm"], 4, 4, 2), ("tm", "lat_0", "lat_1", "lat_2"))
    in_specs = (
        P("tm", None, LAT, None),
        P("tm", None, LAT, None),
        P("tm", None, LAT, None),
        P("tm"),
        P("tm", LAT),
        P("tm", LAT),
        P("tm", LAT),
    )
    out_specs = (P("tm", None, LAT, None), P("tm", None), P())
    return jax.shard_map(body, mesh=torus, in_specs=in_specs, out_specs=out_specs, check_vma=False)
```

```python
import functools
import math

import jax
import jax.numpy as jnp
from jax import lax
from jax.experimental import pallas as pl
from jax.experimental.pallas import tpu as pltpu
from jax.sharding import Mesh
from jax.sharding import PartitionSpec as P

STEPS = 4
LAT = ("lat_0", "lat_1", "lat_2")
KC = 16
HALO = STEPS

flow_coef = 0.4
coriolis_coef = 0.5
map_scale = 0.5
MIB = 1 << 20

VMEM = pl.BlockSpec(memory_space=pltpu.VMEM)
SMEM = pl.BlockSpec(memory_space=pltpu.SMEM)
HBM = pl.BlockSpec(memory_space=pltpu.HBM)


def lon_difference(x):
    lon = x.shape[-1]
    return pltpu.roll(x, lon - 1, 1) - pltpu.roll(x, 1, 1)


def split3(x):
    high = x.astype(jnp.bfloat16)
    rest = x - high.astype(jnp.float32)
    middle = rest.astype(jnp.bfloat16)
    low = (rest - middle.astype(jnp.float32)).astype(jnp.bfloat16)
    return high, middle, low


def across(a, b):
    return lax.dot_general(a, b, (((1,), (1,)), ((), ())), preferred_element_type=jnp.float32)


def pack_kernel(
    step_ref, core_ref, sketch_hbm, base_hbm, outer_ref, inner_ref, outer_base, inner_base, base_ref, sketch, base, sems
):
    chunks = sketch.shape[0] // KC
    fields = sketch.shape[1]

    def copy(c):
        at = pl.ds(c * KC, KC)
        return pltpu.make_async_copy(sketch_hbm.at[at], sketch.at[at], sems.at[c])

    base_copy = pltpu.make_async_copy(base_hbm.at[step_ref[0]], base, sems.at[chunks])
    for c in range(chunks):
        copy(c).start()
    base_copy.start()
    for c in range(chunks):
        copy(c).wait()
        for core in range(2):
            low, high = (outer_ref, inner_ref) if core == 0 else (inner_ref, outer_ref)

            @pl.when(core_ref[0] == core)
            def _(c=c, low=low, high=high):
                for f in range(fields):
                    part = jnp.swapaxes(sketch[c * KC : (c + 1) * KC, f].astype(jnp.float32), 0, 1)
                    part = part.astype(jnp.bfloat16)
                    for ref, rows in ((low, part[:HALO]), (high, part[HALO:])):
                        ref[f * HALO : (f + 1) * HALO, c * KC : (c + 1) * KC] = rows

    base_copy.wait()
    values = base[...].astype(jnp.float32)
    base_ref[...] = values
    pad = jnp.zeros((16 - fields * HALO, values.shape[-1]), jnp.float32)
    for core in range(2):
        low, high = (outer_base, inner_base) if core == 0 else (inner_base, outer_base)

        @pl.when(core_ref[0] == core)
        def _(low=low, high=high):
            for ref, at in ((low, 0), (high, HALO)):
                rows = [values[f, at : at + HALO] for f in range(fields)]
                ref[...] = jnp.concatenate([*rows, pad], axis=0).astype(jnp.bfloat16)


def pack(sketch, checkpoints, checkpoint_step, core):
    rank, fields, rows, lon = sketch.shape
    half = jax.ShapeDtypeStruct((fields * HALO, rank, lon), jnp.bfloat16)
    lines = jax.ShapeDtypeStruct((16, lon), jnp.bfloat16)
    return pl.pallas_call(
        pack_kernel,
        out_shape=(half, half, lines, lines, jax.ShapeDtypeStruct((fields, rows, lon), jnp.float32)),
        in_specs=[SMEM, SMEM, HBM, HBM],
        out_specs=(VMEM,) * 5,
        scratch_shapes=[
            pltpu.VMEM(sketch.shape, jnp.bfloat16),
            pltpu.VMEM((fields, rows, lon), jnp.bfloat16),
            pltpu.SemaphoreType.DMA((rank // KC + 1,)),
        ],
        compiler_params=pltpu.CompilerParams(vmem_limit_bytes=12 * MIB),
        name="pack",
    )(checkpoint_step, core, sketch, checkpoints)


def observe_kernel(scales, band_ref, base_ref, row_ref, column_ref, value_ref, field_ref, cost_ref):
    total_rows, observed, groups = scales
    rows, lon = base_ref.shape[-2:]
    count = row_ref.shape[-1]
    station_row = row_ref[...]
    local = station_row - band_ref[0] * rows
    at_column = lax.broadcasted_iota(jnp.int32, (lon, count), 0) == column_ref[...]
    at_column = jnp.where(at_column, 1.0, 0.0).astype(jnp.bfloat16)
    at_row = lax.broadcasted_iota(jnp.int32, (rows, count), 0) == local
    found = lax.dot_general(
        base_ref[0].astype(jnp.bfloat16), at_column, (((1,), (0,)), ((), ())), preferred_element_type=jnp.float32
    )
    here = jnp.sum(jnp.where(at_row, found, 0.0), axis=0, keepdims=True)
    innovation = here - value_ref[...]
    weight = 1.0 + 2.0 * station_row.astype(jnp.float32) / total_rows
    weighted = weight * innovation
    cost = jnp.sum(weighted * innovation, axis=1, keepdims=True) / (2.0 * groups * observed)
    cost_ref[...] = jnp.broadcast_to(cost, cost_ref.shape)
    spread = jnp.where(at_row, weighted / (2.0 * math.sqrt(observed)), 0.0)
    field = jnp.zeros((rows, lon), jnp.float32)
    for piece in split3(spread):
        field += across(piece, at_column)
    for n, piece in enumerate(split3(field)):
        field_ref[n * rows : (n + 1) * rows] = piece.astype(jnp.float32)


def observe(band, base, station_row, station_column, station_value, scales):
    rows, lon = base.shape[-2:]
    return pl.pallas_call(
        functools.partial(observe_kernel, scales),
        out_shape=(
            jax.ShapeDtypeStruct((3 * rows, lon), jnp.float32),
            jax.ShapeDtypeStruct((1, 128), jnp.float32),
        ),
        in_specs=[SMEM] + [VMEM] * 4,
        out_specs=(VMEM, VMEM),
        compiler_params=pltpu.CompilerParams(vmem_limit_bytes=8 * MIB),
        cost_estimate=pl.CostEstimate(flops=20_000_000, bytes_accessed=1_000_000, transcendentals=0),
        name="observe",
    )(band, base, station_row, station_column, station_value)


def sweep_kernel(
    scale,
    bands,
    band_ref,
    core_ref,
    test_hbm,
    base_ref,
    outer_base,
    inner_base,
    outer_ref,
    inner_ref,
    field_ref,
    cost_ref,
    back_ref,
    coef_ref,
    share_ref,
    test,
    one,
    two,
    coef,
    sems,
):
    rank, fields, rows, lon = test.shape
    extended = rows + 2 * HALO
    band, core = band_ref[0], core_ref[0]

    def copy(c):
        at = pl.ds(c * KC, KC)
        return pltpu.make_async_copy(test_hbm.at[at], test.at[at], sems.at[c])

    for c in range(rank // KC):
        copy(c).start()

    def latitude(e):
        return band * rows - HALO + e

    def inside(e):
        at = latitude(e)
        return jnp.where((at >= 0) & (at < rows * bands), 1.0, 0.0)

    def put(f, e, line):
        line = 0.0625 + 0.015625 * line if f == 0 else (0.2 * flow_coef) * line
        line = line * inside(e)
        coef[f, e] = jnp.broadcast_to(line, (8, lon))
        coef_ref[f, pl.ds(e, 1)] = line

    for f in range(fields):
        for r in range(rows):
            put(f, HALO + r, base_ref[f, r : r + 1])
    for ref, first in ((outer_base, core), (inner_base, 1 - core)):
        values = ref[...].astype(jnp.float32)
        for f in range(fields):
            for r in range(HALO):
                put(f, first * (extended - HALO) + r, values[f * HALO + r : f * HALO + r + 1])

    turns = [
        0.5 * coriolis_coef * (2.0 * (latitude(e).astype(jnp.float32) + 0.5) / (rows * bands) - 1.0)
        for e in range(extended)
    ]
    insides = [inside(e) for e in range(extended)]

    def terms(source, e, at):
        depth, east, north = (coef[f, e] for f in range(3))
        h, u, v = (source[e, f, at] for f in range(3))
        deep = depth * h
        mine = (
            h + lon_difference(u + east * h),
            u - turns[e] * v + lon_difference(east * u + deep),
            v + turns[e] * u + lon_difference(east * v),
        )
        edge = v if HALO <= e < HALO + rows else insides[e] * v
        beside = (edge + north * h, north * u, north * v + deep)
        return mine, beside

    def backward_step(source, target, first, last, at):
        before = here = mine = None
        for e in range(first - 1, last + 2):
            after_mine, after = terms(source, e + 1, at) if e + 1 <= last else (None, None)
            for f in range(fields):
                total = mine[f] if mine is not None else None
                if after is not None:
                    total = after[f] if total is None else total + after[f]
                if before is not None:
                    total = -before[f] if total is None else total - before[f]
                target[e, f, at] = total
            before, here, mine = here, after, after_mine

    def chunk_body(c, carry):
        copy(c).wait()
        for half in range(KC // 8):
            at = pl.ds(half * 8, 8)
            for f in range(fields):
                part = test[pl.ds(c * KC + half * 8, 8), f].astype(jnp.float32)
                part = jnp.swapaxes(part, 0, 1)
                for r in range(rows):
                    one[HALO + r, f, at] = 4.0 * part[r] if f == 0 else part[r]
            source, target = one, two
            for step in range(STEPS):
                backward_step(source, target, HALO - step, HALO + rows - 1 + step, at)
                source, target = target, source
        for e in range(extended):
            for f in range(fields):
                value = one[e, f]
                if f == 0:
                    value = 0.25 * value
                upper = value.astype(jnp.bfloat16)
                lower = (value - upper.astype(jnp.float32)).astype(jnp.bfloat16)
                back_ref[f * extended + e, pl.ds(c * KC, KC)] = upper
                back_ref[f * extended + e, pl.ds(rank + c * KC, KC)] = lower
        return carry

    lax.fori_loop(0, rank // KC, chunk_body, 0)

    share = jnp.zeros((2 * rank, rank), jnp.float32)
    forced = jnp.zeros((3 * rows, rank), jnp.float32)
    line = lax.broadcasted_iota(jnp.int32, (3 * rows, rank), 0) % rows
    field = field_ref[...].astype(jnp.bfloat16)
    for ref, first in ((outer_ref, core), (inner_ref, 1 - core)):
        for f in range(fields):
            for r in range(HALO):
                columns = ref[f * HALO + r]
                share += across(back_ref[f * extended + HALO + first * HALO + r], columns)
                if f == 0:
                    forced += jnp.where(line == first * HALO + r, across(field, columns), 0.0)
    share = (share[:rank] + share[rank:]) * scale
    share_ref[:rank] = share
    lane = lax.broadcasted_iota(jnp.int32, (8, rank), 0)
    forced = jnp.sum(forced, axis=0, keepdims=True)
    share_ref[rank:] = jnp.where(lane == 0, forced, jnp.where(lane == 1, cost_ref[0:1, :rank], 0.0))


def sweep(band, core, test_sketch, base, outer_base, inner_base, outer, inner, field, cost, scale, bands):
    rank, fields, rows, lon = test_sketch.shape
    extended = rows + 2 * HALO
    return pl.pallas_call(
        functools.partial(sweep_kernel, scale, bands),
        out_shape=(
            jax.ShapeDtypeStruct((fields * extended, 2 * rank, lon), jnp.bfloat16),
            jax.ShapeDtypeStruct((fields, extended, lon), jnp.float32),
            jax.ShapeDtypeStruct((rank + 8, rank), jnp.float32),
        ),
        in_specs=[SMEM, SMEM, HBM] + [VMEM] * 7,
        out_specs=(VMEM,) * 3,
        scratch_shapes=[
            pltpu.VMEM(test_sketch.shape, jnp.bfloat16),
            pltpu.VMEM((extended, fields, KC, lon), jnp.float32),
            pltpu.VMEM((extended, fields, KC, lon), jnp.float32),
            pltpu.VMEM((fields, extended, 8, lon), jnp.float32),
            pltpu.SemaphoreType.DMA((rank // KC,)),
        ],
        compiler_params=pltpu.CompilerParams(vmem_limit_bytes=24 * MIB),
        cost_estimate=pl.CostEstimate(flops=2_000_000_000, bytes_accessed=30_000_000, transcendentals=0),
        name="sweep",
    )(band, core, test_sketch, base, outer_base, inner_base, outer, inner, field, cost)


def join_kernel(scale, core_ref, back_ref, own_ref, outer_hbm, inner_hbm, outer_ref, inner_ref, share_ref, sems):
    rank = own_ref.shape[1]
    extended = back_ref.shape[0] // 3
    core = core_ref[0]
    size = outer_ref.shape[0]
    pieces = 3
    step = size // pieces
    sides = ((inner_hbm, inner_ref, 1 - core), (outer_hbm, outer_ref, core))

    def copy(n, side):
        at = pl.ds(n * step, step)
        return pltpu.make_async_copy(side[0].at[at], side[1].at[at], sems.at[n])

    for s, side in enumerate(sides):
        for n in range(pieces):
            at = pl.ds(n * step, step)
            pltpu.make_async_copy(side[0].at[at], side[1].at[at], sems.at[s * pieces + n]).start()
    share = jnp.zeros((2 * rank, rank), jnp.float32)
    for s, side in enumerate(sides):
        for n in range(pieces):
            at = pl.ds(n * step, step)
            pltpu.make_async_copy(side[0].at[at], side[1].at[at], sems.at[s * pieces + n]).wait()
            for i in range(n * step, (n + 1) * step):
                f, r = i // HALO, i % HALO
                share += across(back_ref[f * extended + side[2] * (extended - HALO) + r], side[1][i])
    share = own_ref[:rank] + (share[:rank] + share[rank:]) * scale
    half = rank // 2
    share_ref[:half] = jnp.concatenate([share[:half], share[half:]], axis=1)
    tail = own_ref[rank:]
    share_ref[half:] = jnp.concatenate([tail, tail], axis=1)


def join(core, back, own, outer, inner, scale):
    rank = own.shape[1]
    received = jax.ShapeDtypeStruct(outer.shape, outer.dtype)
    return pl.pallas_call(
        functools.partial(join_kernel, scale),
        out_shape=(received, received, jax.ShapeDtypeStruct((rank // 2 + 8, 2 * rank), jnp.float32)),
        in_specs=[SMEM, VMEM, VMEM, HBM, HBM],
        out_specs=(VMEM,) * 3,
        scratch_shapes=[pltpu.SemaphoreType.DMA((6,))],
        compiler_params=pltpu.CompilerParams(vmem_limit_bytes=8 * MIB),
        name="join",
    )(core, back, own, outer, inner)


def combine_kernel(
    scale,
    groups,
    bands,
    group_ref,
    band_ref,
    core_ref,
    *refs,
):
    shares = refs[:groups]
    (
        outer_ref,
        inner_ref,
        far_outer_ref,
        far_inner_ref,
        coef_ref,
        increment_hbm,
        adjoint_hbm,
        cost_hbm,
        increment,
        adjoint,
        cost_out,
        combined,
        sems,
    ) = refs[groups:]
    half = shares[0].shape[0] - 8
    rank = 2 * half
    fields, extended, lon = coef_ref.shape
    rows = extended - 2 * HALO
    core = core_ref[0]

    line = lax.broadcasted_iota(jnp.int32, (half, 2 * rank), 0)
    lane = lax.broadcasted_iota(jnp.int32, (half, 2 * rank), 1)
    left = lane < rank
    row = jnp.zeros((1, 2 * rank), jnp.float32)
    cost = jnp.zeros((1, 2 * rank), jnp.float32)
    for ahead in reversed(range(groups)):
        share = shares[ahead][...]
        cost += share[half + 1 : half + 2]
        upper = jnp.sum(jnp.where(lane == line, row, 0.0), axis=1, keepdims=True)
        lower = jnp.sum(jnp.where(lane == line + half, row, 0.0), axis=1, keepdims=True)
        product = jnp.sum(share[:half] * jnp.where(left, upper, lower), axis=0, keepdims=True)
        row = product + pltpu.roll(product, rank, 1) + share[half : half + 1]
        if ahead:
            row = jnp.where(group_ref[0] + ahead < groups, row, 0.0)
    adjoint[...] = row[:, :rank]
    cost_out[...] = cost
    copies = [
        pltpu.make_async_copy(adjoint, adjoint_hbm, sems.at[0]),
        pltpu.make_async_copy(cost_out, cost_hbm, sems.at[1]),
    ]
    for copy in copies:
        copy.start()

    pick = lax.broadcasted_iota(jnp.int32, (8, rank), 0)
    factor = jnp.zeros((8, rank), jnp.float32)
    for n, piece in enumerate(split3(row[:, :rank] * scale)):
        factor = jnp.where(pick == n, piece.astype(jnp.float32), factor)
    factor = factor.astype(jnp.bfloat16)
    places = (
        (outer_ref, HALO + core * HALO),
        (inner_ref, 2 * HALO - core * HALO),
        (far_outer_ref, core * (extended - HALO)),
        (far_inner_ref, (1 - core) * (extended - HALO)),
    )
    for ref, first in places:
        for f in range(fields):
            for r in range(HALO):
                part = lax.dot_general(
                    factor, ref[f * HALO + r], (((1,), (0,)), ((), ())), preferred_element_type=jnp.float32
                )
                combined[f, pl.ds(first + r, 1)] = jnp.sum(part, axis=0, keepdims=True)

    latitude = band_ref[0] * rows - HALO + lax.broadcasted_iota(jnp.int32, (extended, lon), 0)
    present = (latitude >= 0) & (latitude < rows * bands)
    turn = 0.5 * coriolis_coef * (2.0 * (latitude.astype(jnp.float32) + 0.5) / (rows * bands) - 1.0)
    depth, east, north = (coef_ref[f] for f in range(3))
    h, u, v = 0.25 * combined[0], combined[1], combined[2]

    def lat_difference(x):
        return pltpu.roll(x, extended - 1, 0) - pltpu.roll(x, 1, 0)

    for _ in range(STEPS):
        dxh, dxu, dxv = (lon_difference(x) for x in (h, u, v))
        dyh, dyu, dyv = (lat_difference(x) for x in (h, u, v))
        new_u = (u + turn * v) - dxh - east * dxu - north * dyu
        new_v = (v - turn * u) - dyh - east * dxv - north * dyv
        new_h = h - depth * (dxu + dyv) - east * dxh - north * dyh
        h, u, v = (jnp.where(present, x, 0.0) for x in (new_h, new_u, new_v))
    own = slice(HALO, HALO + rows)
    for f, value in enumerate((4.0 * h, u, v)):
        increment[0, f] = value[own]
    copies.append(pltpu.make_async_copy(increment, increment_hbm, sems.at[2]))
    copies[-1].start()
    for copy in copies:
        copy.wait()


def combine(group, band, core, shares, halves, coef, scale, bands):
    fields, extended, lon = coef.shape
    rows = extended - 2 * HALO
    rank = halves[0].shape[1]
    return pl.pallas_call(
        functools.partial(combine_kernel, scale, len(shares), bands),
        out_shape=(
            jax.ShapeDtypeStruct((1, fields, rows, lon), jnp.float32),
            jax.ShapeDtypeStruct((1, rank), jnp.float32),
            jax.ShapeDtypeStruct((1, 2 * rank), jnp.float32),
        ),
        in_specs=[SMEM] * 3 + [VMEM] * (len(shares) + 5),
        out_specs=(HBM,) * 3,
        scratch_shapes=[
            pltpu.VMEM((1, fields, rows, lon), jnp.float32),
            pltpu.VMEM((1, rank), jnp.float32),
            pltpu.VMEM((1, 2 * rank), jnp.float32),
            pltpu.VMEM((fields, extended, lon), jnp.float32),
            pltpu.SemaphoreType.DMA((3,)),
        ],
        compiler_params=pltpu.CompilerParams(vmem_limit_bytes=8 * MIB),
        name="combine",
    )(group, band, core, *shares, *halves, coef)


def from_ahead(x, axis, by):
    count = lax.axis_size(axis)
    return lax.ppermute(x, axis, [((i + by) % count, i) for i in range(count)])


def added_over(x, axis):
    others = [from_ahead(x, axis, by) for by in range(1, lax.axis_size(axis))]
    return functools.reduce(jnp.add, others, x)


def body(
    sketch, test_sketch, checkpoints, checkpoint_step, station_row, station_column, station_value
):
    rank, fields, rows, lon = sketch.shape
    bands = lax.axis_size(LAT)
    groups = lax.axis_size("tm")
    total_rows = rows * bands
    observed = station_row.shape[1] * bands
    band = lax.axis_index(LAT).astype(jnp.int32).reshape(1)
    core = lax.axis_index("lat_2").astype(jnp.int32).reshape(1)
    group = lax.axis_index("tm").astype(jnp.int32).reshape(1)

    outer, inner, outer_base, inner_base, base = pack(sketch, checkpoints, checkpoint_step, core)
    across_chips = [pair for i in range(1, bands - 1, 2) for pair in ((i, i + 1), (i + 1, i))]
    inside_chip = [(0, 1), (1, 0)]
    far_outer = lax.ppermute(outer, LAT, across_chips)
    far_outer_base = lax.ppermute(outer_base, LAT, across_chips)
    far_inner_base = lax.ppermute(inner_base, "lat_2", inside_chip)
    far_inner = lax.ppermute(inner, "lat_2", inside_chip)
    field, cost = observe(
        band, base, station_row, station_column, station_value, (total_rows, observed, groups)
    )
    scale = map_scale / math.sqrt(rank * fields * total_rows * lon)
    back, coef, own = sweep(
        band, core, test_sketch, base, far_outer_base, far_inner_base, outer, inner, field, cost, scale, bands
    )
    far_outer, far_inner, share = join(core, back, own, far_outer, far_inner, scale)
    for axis in ("lat_2", "lat_1", "lat_0"):
        share = added_over(share, axis)
    shares = [share] + [from_ahead(share, "tm", by) for by in range(1, groups)]
    increment, adjoint, total_cost = combine(
        group, band, core, shares, (outer, inner, far_outer, far_inner), coef, 1.0 / math.sqrt(rank), bands
    )
    return (increment, adjoint, total_cost[0, 0])


def solution(mesh):
    torus = Mesh(mesh.devices.reshape(mesh.shape["tm"], 4, 4, 2), ("tm", "lat_0", "lat_1", "lat_2"))
    in_specs = (
        P("tm", None, LAT, None),
        P("tm", None, LAT, None),
        P("tm", None, LAT, None),
        P("tm"),
        P("tm", LAT),
        P("tm", LAT),
        P("tm", LAT),
    )
    out_specs = (P("tm", None, LAT, None), P("tm", None), P())
    return jax.shard_map(body, mesh=torus, in_specs=in_specs, out_specs=out_specs, check_vma=False)
```

```python
import functools
import math

import jax
import jax.numpy as jnp
from jax import lax
from jax.experimental import pallas as pl
from jax.experimental.pallas import tpu as pltpu
from jax.sharding import Mesh
from jax.sharding import PartitionSpec as P

STEPS = 4
LAT = ("lat_0", "lat_1", "lat_2")
KC = 16
HALO = STEPS

flow_coef = 0.4
coriolis_coef = 0.5
map_scale = 0.5
MIB = 1 << 20

VMEM = pl.BlockSpec(memory_space=pltpu.VMEM)
SMEM = pl.BlockSpec(memory_space=pltpu.SMEM)
HBM = pl.BlockSpec(memory_space=pltpu.HBM)


def lon_difference(x):
    lon = x.shape[-1]
    return pltpu.roll(x, lon - 1, 1) - pltpu.roll(x, 1, 1)


def split3(x):
    high = x.astype(jnp.bfloat16)
    rest = x - high.astype(jnp.float32)
    middle = rest.astype(jnp.bfloat16)
    low = (rest - middle.astype(jnp.float32)).astype(jnp.bfloat16)
    return high, middle, low


def across(a, b):
    return lax.dot_general(a, b, (((1,), (1,)), ((), ())), preferred_element_type=jnp.float32)


def on_hbm(x):
    return pltpu.with_memory_space_constraint(x, pltpu.HBM)


def pick_kernel(step_ref, core_ref, base_hbm, outer_base, inner_base, base_ref, base, sems):
    fields = base.shape[0]
    copy = pltpu.make_async_copy(base_hbm.at[step_ref[0]], base, sems.at[0])
    copy.start()
    copy.wait()
    values = base[...].astype(jnp.float32)
    base_ref[...] = values
    pad = jnp.zeros((16 - fields * HALO, values.shape[-1]), jnp.float32)
    for core in range(2):
        low, high = (outer_base, inner_base) if core == 0 else (inner_base, outer_base)

        @pl.when(core_ref[0] == core)
        def _(low=low, high=high):
            for ref, at in ((low, 0), (high, HALO)):
                rows = [values[f, at : at + HALO] for f in range(fields)]
                ref[...] = jnp.concatenate([*rows, pad], axis=0).astype(jnp.bfloat16)


def pick(checkpoints, checkpoint_step, core):
    _, fields, rows, lon = checkpoints.shape
    lines = jax.ShapeDtypeStruct((16, lon), jnp.bfloat16)
    return pl.pallas_call(
        pick_kernel,
        out_shape=(lines, lines, jax.ShapeDtypeStruct((fields, rows, lon), jnp.float32)),
        in_specs=[SMEM, SMEM, HBM],
        out_specs=(VMEM,) * 3,
        scratch_shapes=[pltpu.VMEM((fields, rows, lon), jnp.bfloat16), pltpu.SemaphoreType.DMA((1,))],
        compiler_params=pltpu.CompilerParams(vmem_limit_bytes=8 * MIB),
        name="pick",
    )(checkpoint_step, core, on_hbm(checkpoints))


def pack_kernel(core_ref, sketch, first, second, outer_ref, inner_ref):
    fields = sketch.shape[1]
    for core in range(2):
        low, high = (outer_ref, inner_ref) if core == 0 else (inner_ref, outer_ref)

        @pl.when(core_ref[0] == core)
        def _(low=low, high=high):
            for c in range(sketch.shape[0] // KC):
                for f in range(fields):
                    part = jnp.swapaxes(sketch[c * KC : (c + 1) * KC, f].astype(jnp.float32), 0, 1)
                    part = part.astype(jnp.bfloat16)
                    for ref, rows in ((low, part[:HALO]), (high, part[HALO:])):
                        ref[f * HALO : (f + 1) * HALO, c * KC : (c + 1) * KC] = rows


def pack(sketch, core, *first):
    rank, fields, rows, lon = sketch.shape
    half = jax.ShapeDtypeStruct((fields * HALO, rank, lon), jnp.bfloat16)
    return pl.pallas_call(
        pack_kernel,
        out_shape=(half, half),
        in_specs=[SMEM, VMEM, VMEM, VMEM],
        out_specs=(VMEM,) * 2,
        compiler_params=pltpu.CompilerParams(vmem_limit_bytes=8 * MIB),
        name="pack",
    )(core, sketch, *first)


def observe_kernel(scales, band_ref, base_ref, row_ref, column_ref, value_ref, field_ref, cost_ref):
    total_rows, observed, groups = scales
    rows, lon = base_ref.shape[-2:]
    count = row_ref.shape[-1]
    station_row = row_ref[...]
    local = station_row - band_ref[0] * rows
    at_column = lax.broadcasted_iota(jnp.int32, (lon, count), 0) == column_ref[...]
    at_column = jnp.where(at_column, 1.0, 0.0).astype(jnp.bfloat16)
    at_row = lax.broadcasted_iota(jnp.int32, (rows, count), 0) == local
    found = lax.dot_general(
        base_ref[0].astype(jnp.bfloat16), at_column, (((1,), (0,)), ((), ())), preferred_element_type=jnp.float32
    )
    here = jnp.sum(jnp.where(at_row, found, 0.0), axis=0, keepdims=True)
    innovation = here - value_ref[...]
    weight = 1.0 + 2.0 * station_row.astype(jnp.float32) / total_rows
    weighted = weight * innovation
    cost = jnp.sum(weighted * innovation, axis=1, keepdims=True) / (2.0 * groups * observed)
    cost_ref[...] = jnp.broadcast_to(cost, cost_ref.shape)
    spread = jnp.where(at_row, weighted / (2.0 * math.sqrt(observed)), 0.0)
    field = jnp.zeros((rows, lon), jnp.float32)
    for piece in split3(spread):
        field += across(piece, at_column)
    for n, piece in enumerate(split3(field)):
        field_ref[n * rows : (n + 1) * rows] = piece.astype(jnp.float32)


def observe(band, base, station_row, station_column, station_value, scales):
    rows, lon = base.shape[-2:]
    return pl.pallas_call(
        functools.partial(observe_kernel, scales),
        out_shape=(
            jax.ShapeDtypeStruct((3 * rows, lon), jnp.float32),
            jax.ShapeDtypeStruct((1, 128), jnp.float32),
        ),
        in_specs=[SMEM] + [VMEM] * 4,
        out_specs=(VMEM, VMEM),
        compiler_params=pltpu.CompilerParams(vmem_limit_bytes=8 * MIB),
        cost_estimate=pl.CostEstimate(flops=20_000_000, bytes_accessed=1_000_000, transcendentals=0),
        name="observe",
    )(band, base, station_row, station_column, station_value)


def sweep_kernel(
    scale,
    bands,
    band_ref,
    core_ref,
    test_hbm,
    base_ref,
    outer_base,
    inner_base,
    outer_ref,
    inner_ref,
    field_ref,
    cost_ref,
    back_ref,
    coef_ref,
    share_ref,
    test,
    one,
    two,
    coef,
    sems,
):
    rank, fields, rows, lon = test.shape
    extended = rows + 2 * HALO
    band, core = band_ref[0], core_ref[0]

    def copy(c):
        at = pl.ds(c * KC, KC)
        return pltpu.make_async_copy(test_hbm.at[at], test.at[at], sems.at[c])

    for c in range(rank // KC):
        copy(c).start()

    def latitude(e):
        return band * rows - HALO + e

    def inside(e):
        at = latitude(e)
        return jnp.where((at >= 0) & (at < rows * bands), 1.0, 0.0)

    def put(f, e, line):
        line = 0.0625 + 0.015625 * line if f == 0 else (0.2 * flow_coef) * line
        line = line * inside(e)
        coef[f, e] = jnp.broadcast_to(line, (8, lon))
        coef_ref[f, pl.ds(e, 1)] = line

    for f in range(fields):
        for r in range(rows):
            put(f, HALO + r, base_ref[f, r : r + 1])
    for ref, first in ((outer_base, core), (inner_base, 1 - core)):
        values = ref[...].astype(jnp.float32)
        for f in range(fields):
            for r in range(HALO):
                put(f, first * (extended - HALO) + r, values[f * HALO + r : f * HALO + r + 1])

    turns = [
        0.5 * coriolis_coef * (2.0 * (latitude(e).astype(jnp.float32) + 0.5) / (rows * bands) - 1.0)
        for e in range(extended)
    ]
    insides = [inside(e) for e in range(extended)]

    def terms(source, e, at):
        depth, east, north = (coef[f, e] for f in range(3))
        h, u, v = (source[e, f, at] for f in range(3))
        deep = depth * h
        mine = (
            h + lon_difference(u + east * h),
            u - turns[e] * v + lon_difference(east * u + deep),
            v + turns[e] * u + lon_difference(east * v),
        )
        edge = v if HALO <= e < HALO + rows else insides[e] * v
        beside = (edge + north * h, north * u, north * v + deep)
        return mine, beside

    def backward_step(source, target, first, last, at):
        before = here = mine = None
        for e in range(first - 1, last + 2):
            after_mine, after = terms(source, e + 1, at) if e + 1 <= last else (None, None)
            for f in range(fields):
                total = mine[f] if mine is not None else None
                if after is not None:
                    total = after[f] if total is None else total + after[f]
                if before is not None:
                    total = -before[f] if total is None else total - before[f]
                target[e, f, at] = total
            before, here, mine = here, after, after_mine

    def chunk_body(c, carry):
        copy(c).wait()
        for half in range(KC // 8):
            at = pl.ds(half * 8, 8)
            for f in range(fields):
                part = test[pl.ds(c * KC + half * 8, 8), f].astype(jnp.float32)
                part = jnp.swapaxes(part, 0, 1)
                for r in range(rows):
                    one[HALO + r, f, at] = 4.0 * part[r] if f == 0 else part[r]
            source, target = one, two
            for step in range(STEPS):
                backward_step(source, target, HALO - step, HALO + rows - 1 + step, at)
                source, target = target, source
        for e in range(extended):
            for f in range(fields):
                value = one[e, f]
                if f == 0:
                    value = 0.25 * value
                upper = value.astype(jnp.bfloat16)
                lower = (value - upper.astype(jnp.float32)).astype(jnp.bfloat16)
                back_ref[f * extended + e, pl.ds(c * KC, KC)] = upper
                back_ref[f * extended + e, pl.ds(rank + c * KC, KC)] = lower
        return carry

    lax.fori_loop(0, rank // KC, chunk_body, 0)

    share = jnp.zeros((2 * rank, rank), jnp.float32)
    forced = jnp.zeros((3 * rows, rank), jnp.float32)
    line = lax.broadcasted_iota(jnp.int32, (3 * rows, rank), 0) % rows
    field = field_ref[...].astype(jnp.bfloat16)
    for ref, first in ((outer_ref, core), (inner_ref, 1 - core)):
        for f in range(fields):
            for r in range(HALO):
                columns = ref[f * HALO + r]
                share += across(back_ref[f * extended + HALO + first * HALO + r], columns)
                if f == 0:
                    forced += jnp.where(line == first * HALO + r, across(field, columns), 0.0)
    share = (share[:rank] + share[rank:]) * scale
    share_ref[:rank] = share
    lane = lax.broadcasted_iota(jnp.int32, (8, rank), 0)
    forced = jnp.sum(forced, axis=0, keepdims=True)
    share_ref[rank:] = jnp.where(lane == 0, forced, jnp.where(lane == 1, cost_ref[0:1, :rank], 0.0))


def sweep(band, core, test_sketch, base, outer_base, inner_base, outer, inner, field, cost, scale, bands):
    rank, fields, rows, lon = test_sketch.shape
    extended = rows + 2 * HALO
    return pl.pallas_call(
        functools.partial(sweep_kernel, scale, bands),
        out_shape=(
            jax.ShapeDtypeStruct((fields * extended, 2 * rank, lon), jnp.bfloat16),
            jax.ShapeDtypeStruct((fields, extended, lon), jnp.float32),
            jax.ShapeDtypeStruct((rank + 8, rank), jnp.float32),
        ),
        in_specs=[SMEM, SMEM, HBM] + [VMEM] * 7,
        out_specs=(VMEM,) * 3,
        scratch_shapes=[
            pltpu.VMEM(test_sketch.shape, jnp.bfloat16),
            pltpu.VMEM((extended, fields, KC, lon), jnp.float32),
            pltpu.VMEM((extended, fields, KC, lon), jnp.float32),
            pltpu.VMEM((fields, extended, 8, lon), jnp.float32),
            pltpu.SemaphoreType.DMA((rank // KC,)),
        ],
        compiler_params=pltpu.CompilerParams(vmem_limit_bytes=24 * MIB),
        cost_estimate=pl.CostEstimate(flops=2_000_000_000, bytes_accessed=30_000_000, transcendentals=0),
        name="sweep",
    )(band, core, on_hbm(test_sketch), base, outer_base, inner_base, outer, inner, field, cost)


def join_kernel(scale, core_ref, back_ref, own_ref, outer_hbm, inner_hbm, share_ref, outer, inner, sems):
    rank = own_ref.shape[1]
    extended = back_ref.shape[0] // 3
    core = core_ref[0]
    pieces = 3
    step = outer.shape[0] // pieces
    sides = ((inner_hbm, inner, 1 - core), (outer_hbm, outer, core))

    def copy(s, n):
        at = pl.ds(n * step, step)
        return pltpu.make_async_copy(sides[s][0].at[at], sides[s][1].at[at], sems.at[s * pieces + n])

    for s in range(2):
        for n in range(pieces):
            copy(s, n).start()
    share = jnp.zeros((2 * rank, rank), jnp.float32)
    for s, side in enumerate(sides):
        for n in range(pieces):
            copy(s, n).wait()
            for i in range(n * step, (n + 1) * step):
                f, r = i // HALO, i % HALO
                share += across(back_ref[f * extended + side[2] * (extended - HALO) + r], side[1][i])
    share = own_ref[:rank] + (share[:rank] + share[rank:]) * scale
    half = rank // 2
    share_ref[:half] = jnp.concatenate([share[:half], share[half:]], axis=1)
    tail = own_ref[rank:]
    share_ref[half:] = jnp.concatenate([tail, tail], axis=1)


def join(core, back, own, outer, inner, scale):
    rank = own.shape[1]
    return pl.pallas_call(
        functools.partial(join_kernel, scale),
        out_shape=jax.ShapeDtypeStruct((rank // 2 + 8, 2 * rank), jnp.float32),
        in_specs=[SMEM, VMEM, VMEM, HBM, HBM],
        out_specs=VMEM,
        scratch_shapes=[
            pltpu.VMEM(outer.shape, outer.dtype),
            pltpu.VMEM(inner.shape, inner.dtype),
            pltpu.SemaphoreType.DMA((6,)),
        ],
        compiler_params=pltpu.CompilerParams(vmem_limit_bytes=8 * MIB),
        name="join",
    )(core, back, own, on_hbm(outer), on_hbm(inner))


def combine_kernel(
    scale,
    groups,
    bands,
    group_ref,
    band_ref,
    core_ref,
    *refs,
):
    shares = refs[:groups]
    (
        outer_ref,
        inner_ref,
        far_outer_hbm,
        far_inner_hbm,
        coef_ref,
        increment_hbm,
        adjoint_hbm,
        cost_hbm,
        increment,
        adjoint,
        cost_out,
        combined,
        far_outer_ref,
        far_inner_ref,
        sems,
    ) = refs[groups:]
    arrivals = [
        pltpu.make_async_copy(far_outer_hbm, far_outer_ref, sems.at[3]),
        pltpu.make_async_copy(far_inner_hbm, far_inner_ref, sems.at[4]),
    ]
    for copy in arrivals:
        copy.start()
    half = shares[0].shape[0] - 8
    rank = 2 * half
    fields, extended, lon = coef_ref.shape
    rows = extended - 2 * HALO
    core = core_ref[0]

    line = lax.broadcasted_iota(jnp.int32, (half, 2 * rank), 0)
    lane = lax.broadcasted_iota(jnp.int32, (half, 2 * rank), 1)
    left = lane < rank
    row = jnp.zeros((1, 2 * rank), jnp.float32)
    cost = jnp.zeros((1, 2 * rank), jnp.float32)
    for ahead in reversed(range(groups)):
        share = shares[ahead][...]
        cost += share[half + 1 : half + 2]
        upper = jnp.sum(jnp.where(lane == line, row, 0.0), axis=1, keepdims=True)
        lower = jnp.sum(jnp.where(lane == line + half, row, 0.0), axis=1, keepdims=True)
        product = jnp.sum(share[:half] * jnp.where(left, upper, lower), axis=0, keepdims=True)
        row = product + pltpu.roll(product, rank, 1) + share[half : half + 1]
        if ahead:
            row = jnp.where(group_ref[0] + ahead < groups, row, 0.0)
    adjoint[...] = row[:, :rank]
    cost_out[...] = cost
    copies = [
        pltpu.make_async_copy(adjoint, adjoint_hbm, sems.at[0]),
        pltpu.make_async_copy(cost_out, cost_hbm, sems.at[1]),
    ]
    for copy in copies:
        copy.start()

    pick = lax.broadcasted_iota(jnp.int32, (8, rank), 0)
    factor = jnp.zeros((8, rank), jnp.float32)
    for n, piece in enumerate(split3(row[:, :rank] * scale)):
        factor = jnp.where(pick == n, piece.astype(jnp.float32), factor)
    factor = factor.astype(jnp.bfloat16)
    places = (
        (outer_ref, HALO + core * HALO),
        (inner_ref, 2 * HALO - core * HALO),
        (far_outer_ref, core * (extended - HALO)),
        (far_inner_ref, (1 - core) * (extended - HALO)),
    )
    for n, (ref, first) in enumerate(places):
        if n >= 2:
            arrivals[n - 2].wait()
        for f in range(fields):
            for r in range(HALO):
                part = lax.dot_general(
                    factor, ref[f * HALO + r], (((1,), (0,)), ((), ())), preferred_element_type=jnp.float32
                )
                combined[f, pl.ds(first + r, 1)] = jnp.sum(part, axis=0, keepdims=True)

    latitude = band_ref[0] * rows - HALO + lax.broadcasted_iota(jnp.int32, (extended, lon), 0)
    present = (latitude >= 0) & (latitude < rows * bands)
    turn = 0.5 * coriolis_coef * (2.0 * (latitude.astype(jnp.float32) + 0.5) / (rows * bands) - 1.0)
    depth, east, north = (coef_ref[f] for f in range(3))
    h, u, v = 0.25 * combined[0], combined[1], combined[2]

    def lat_difference(x):
        return pltpu.roll(x, extended - 1, 0) - pltpu.roll(x, 1, 0)

    for _ in range(STEPS):
        dxh, dxu, dxv = (lon_difference(x) for x in (h, u, v))
        dyh, dyu, dyv = (lat_difference(x) for x in (h, u, v))
        new_u = (u + turn * v) - dxh - east * dxu - north * dyu
        new_v = (v - turn * u) - dyh - east * dxv - north * dyv
        new_h = h - depth * (dxu + dyv) - east * dxh - north * dyh
        h, u, v = (jnp.where(present, x, 0.0) for x in (new_h, new_u, new_v))
    own = slice(HALO, HALO + rows)
    for f, value in enumerate((4.0 * h, u, v)):
        increment[0, f] = value[own]
    copies.append(pltpu.make_async_copy(increment, increment_hbm, sems.at[2]))
    copies[-1].start()
    for copy in copies:
        copy.wait()


def combine(group, band, core, shares, halves, coef, scale, bands):
    fields, extended, lon = coef.shape
    rows = extended - 2 * HALO
    rank = halves[0].shape[1]
    return pl.pallas_call(
        functools.partial(combine_kernel, scale, len(shares), bands),
        out_shape=(
            jax.ShapeDtypeStruct((1, fields, rows, lon), jnp.float32),
            jax.ShapeDtypeStruct((1, rank), jnp.float32),
            jax.ShapeDtypeStruct((1, 2 * rank), jnp.float32),
        ),
        in_specs=[SMEM] * 3 + [VMEM] * (len(shares) + 2) + [HBM] * 2 + [VMEM],
        out_specs=(HBM,) * 3,
        scratch_shapes=[
            pltpu.VMEM((1, fields, rows, lon), jnp.float32),
            pltpu.VMEM((1, rank), jnp.float32),
            pltpu.VMEM((1, 2 * rank), jnp.float32),
            pltpu.VMEM((fields, extended, lon), jnp.float32),
            pltpu.VMEM(halves[2].shape, halves[2].dtype),
            pltpu.VMEM(halves[3].shape, halves[3].dtype),
            pltpu.SemaphoreType.DMA((5,)),
        ],
        compiler_params=pltpu.CompilerParams(vmem_limit_bytes=8 * MIB),
        name="combine",
    )(group, band, core, *shares, *halves[:2], *(on_hbm(x) for x in halves[2:]), coef)


def from_ahead(x, axis, by):
    count = lax.axis_size(axis)
    return lax.ppermute(x, axis, [((i + by) % count, i) for i in range(count)])


def added_over(x, axis):
    others = [from_ahead(x, axis, by) for by in range(1, lax.axis_size(axis))]
    return functools.reduce(jnp.add, others, x)


def body(
    sketch, test_sketch, checkpoints, checkpoint_step, station_row, station_column, station_value
):
    rank, fields, rows, lon = sketch.shape
    bands = lax.axis_size(LAT)
    groups = lax.axis_size("tm")
    total_rows = rows * bands
    observed = station_row.shape[1] * bands
    band = lax.axis_index(LAT).astype(jnp.int32).reshape(1)
    core = lax.axis_index("lat_2").astype(jnp.int32).reshape(1)
    group = lax.axis_index("tm").astype(jnp.int32).reshape(1)

    outer_base, inner_base, base = pick(checkpoints, checkpoint_step, core)
    across_chips = [pair for i in range(1, bands - 1, 2) for pair in ((i, i + 1), (i + 1, i))]
    inside_chip = [(0, 1), (1, 0)]
    far_outer_base = lax.ppermute(outer_base, LAT, across_chips)
    far_inner_base = lax.ppermute(inner_base, "lat_2", inside_chip)
    outer, inner = pack(sketch, core, far_outer_base, far_inner_base)
    far_outer = lax.ppermute(outer, LAT, across_chips)
    far_inner = lax.ppermute(inner, "lat_2", inside_chip)
    field, cost = observe(
        band, base, station_row, station_column, station_value, (total_rows, observed, groups)
    )
    scale = map_scale / math.sqrt(rank * fields * total_rows * lon)
    back, coef, own = sweep(
        band, core, test_sketch, base, far_outer_base, far_inner_base, outer, inner, field, cost, scale, bands
    )
    share = join(core, back, own, far_outer, far_inner, scale)
    for axis in ("lat_2", "lat_1", "lat_0"):
        share = added_over(share, axis)
    shares = [share] + [from_ahead(share, "tm", by) for by in range(1, groups)]
    increment, adjoint, total_cost = combine(
        group, band, core, shares, (outer, inner, far_outer, far_inner), coef, 1.0 / math.sqrt(rank), bands
    )
    return (increment, adjoint, total_cost[0, 0])


def solution(mesh):
    torus = Mesh(mesh.devices.reshape(mesh.shape["tm"], 4, 4, 2), ("tm", "lat_0", "lat_1", "lat_2"))
    in_specs = (
        P("tm", None, LAT, None),
        P("tm", None, LAT, None),
        P("tm", None, LAT, None),
        P("tm"),
        P("tm", LAT),
        P("tm", LAT),
        P("tm", LAT),
    )
    out_specs = (P("tm", None, LAT, None), P("tm", None), P())
    return jax.shard_map(body, mesh=torus, in_specs=in_specs, out_specs=out_specs, check_vma=False)
```

```python
import functools
import math

import jax
import jax.numpy as jnp
from jax import lax
from jax.experimental import pallas as pl
from jax.experimental.pallas import tpu as pltpu
from jax.sharding import Mesh
from jax.sharding import PartitionSpec as P

STEPS = 4
LAT = ("lat_0", "lat_1", "lat_2")
KC = 16
HALO = STEPS

flow_coef = 0.4
coriolis_coef = 0.5
map_scale = 0.5
MIB = 1 << 20

VMEM = pl.BlockSpec(memory_space=pltpu.VMEM)
SMEM = pl.BlockSpec(memory_space=pltpu.SMEM)
HBM = pl.BlockSpec(memory_space=pltpu.HBM)


def lon_difference(x):
    lon = x.shape[-1]
    return pltpu.roll(x, lon - 1, 1) - pltpu.roll(x, 1, 1)


def split3(x):
    high = x.astype(jnp.bfloat16)
    rest = x - high.astype(jnp.float32)
    middle = rest.astype(jnp.bfloat16)
    low = (rest - middle.astype(jnp.float32)).astype(jnp.bfloat16)
    return high, middle, low


def across(a, b):
    return lax.dot_general(a, b, (((1,), (1,)), ((), ())), preferred_element_type=jnp.float32)


def on_hbm(x):
    return pltpu.with_memory_space_constraint(x, pltpu.HBM)


def pick_kernel(step_ref, core_ref, base_hbm, outer_base, inner_base, base_ref, base, sems):
    fields = base.shape[0]
    copy = pltpu.make_async_copy(base_hbm.at[step_ref[0]], base, sems.at[0])
    copy.start()
    copy.wait()
    values = base[...].astype(jnp.float32)
    base_ref[...] = values
    pad = jnp.zeros((16 - fields * HALO, values.shape[-1]), jnp.float32)
    for core in range(2):
        low, high = (outer_base, inner_base) if core == 0 else (inner_base, outer_base)

        @pl.when(core_ref[0] == core)
        def _(low=low, high=high):
            for ref, at in ((low, 0), (high, HALO)):
                rows = [values[f, at : at + HALO] for f in range(fields)]
                ref[...] = jnp.concatenate([*rows, pad], axis=0).astype(jnp.bfloat16)


def pick(checkpoints, checkpoint_step, core):
    _, fields, rows, lon = checkpoints.shape
    lines = jax.ShapeDtypeStruct((16, lon), jnp.bfloat16)
    return pl.pallas_call(
        pick_kernel,
        out_shape=(lines, lines, jax.ShapeDtypeStruct((fields, rows, lon), jnp.float32)),
        in_specs=[SMEM, SMEM, HBM],
        out_specs=(VMEM,) * 3,
        scratch_shapes=[pltpu.VMEM((fields, rows, lon), jnp.bfloat16), pltpu.SemaphoreType.DMA((1,))],
        compiler_params=pltpu.CompilerParams(vmem_limit_bytes=8 * MIB),
        name="pick",
    )(checkpoint_step, core, on_hbm(checkpoints))


def pack_kernel(core_ref, sketch_hbm, outer_ref, inner_ref, sketch, sems):
    chunks = sketch.shape[0] // KC
    fields = sketch.shape[1]

    def copy(c):
        at = pl.ds(c * KC, KC)
        return pltpu.make_async_copy(sketch_hbm.at[at], sketch.at[at], sems.at[c])

    for c in range(chunks):
        copy(c).start()
    for c in range(chunks):
        copy(c).wait()
        for core in range(2):
            low, high = (outer_ref, inner_ref) if core == 0 else (inner_ref, outer_ref)

            @pl.when(core_ref[0] == core)
            def _(c=c, low=low, high=high):
                for f in range(fields):
                    part = jnp.swapaxes(sketch[c * KC : (c + 1) * KC, f].astype(jnp.float32), 0, 1)
                    part = part.astype(jnp.bfloat16)
                    for ref, rows in ((low, part[:HALO]), (high, part[HALO:])):
                        ref[f * HALO : (f + 1) * HALO, c * KC : (c + 1) * KC] = rows


def pack(sketch, core):
    rank, fields, rows, lon = sketch.shape
    half = jax.ShapeDtypeStruct((fields * HALO, rank, lon), jnp.bfloat16)
    return pl.pallas_call(
        pack_kernel,
        out_shape=(half, half),
        in_specs=[SMEM, HBM],
        out_specs=(VMEM,) * 2,
        scratch_shapes=[pltpu.VMEM(sketch.shape, sketch.dtype), pltpu.SemaphoreType.DMA((rank // KC,))],
        compiler_params=pltpu.CompilerParams(vmem_limit_bytes=8 * MIB),
        name="pack",
    )(core, on_hbm(sketch))


def observe_kernel(scales, band_ref, base_ref, row_ref, column_ref, value_ref, field_ref, cost_ref):
    total_rows, observed, groups = scales
    rows, lon = base_ref.shape[-2:]
    count = row_ref.shape[-1]
    station_row = row_ref[...]
    local = station_row - band_ref[0] * rows
    at_column = lax.broadcasted_iota(jnp.int32, (lon, count), 0) == column_ref[...]
    at_column = jnp.where(at_column, 1.0, 0.0).astype(jnp.bfloat16)
    at_row = lax.broadcasted_iota(jnp.int32, (rows, count), 0) == local
    found = lax.dot_general(
        base_ref[0].astype(jnp.bfloat16), at_column, (((1,), (0,)), ((), ())), preferred_element_type=jnp.float32
    )
    here = jnp.sum(jnp.where(at_row, found, 0.0), axis=0, keepdims=True)
    innovation = here - value_ref[...]
    weight = 1.0 + 2.0 * station_row.astype(jnp.float32) / total_rows
    weighted = weight * innovation
    cost = jnp.sum(weighted * innovation, axis=1, keepdims=True) / (2.0 * groups * observed)
    cost_ref[...] = jnp.broadcast_to(cost, cost_ref.shape)
    spread = jnp.where(at_row, weighted / (2.0 * math.sqrt(observed)), 0.0)
    field = jnp.zeros((rows, lon), jnp.float32)
    for piece in split3(spread):
        field += across(piece, at_column)
    for n, piece in enumerate(split3(field)):
        field_ref[n * rows : (n + 1) * rows] = piece.astype(jnp.float32)


def observe(band, base, station_row, station_column, station_value, scales):
    rows, lon = base.shape[-2:]
    return pl.pallas_call(
        functools.partial(observe_kernel, scales),
        out_shape=(
            jax.ShapeDtypeStruct((3 * rows, lon), jnp.float32),
            jax.ShapeDtypeStruct((1, 128), jnp.float32),
        ),
        in_specs=[SMEM] + [VMEM] * 4,
        out_specs=(VMEM, VMEM),
        compiler_params=pltpu.CompilerParams(vmem_limit_bytes=8 * MIB),
        cost_estimate=pl.CostEstimate(flops=20_000_000, bytes_accessed=1_000_000, transcendentals=0),
        name="observe",
    )(band, base, station_row, station_column, station_value)


def sweep_kernel(
    bands,
    band_ref,
    core_ref,
    test_hbm,
    base_ref,
    outer_base,
    inner_base,
    outer_ref,
    inner_ref,
    field_ref,
    cost_ref,
    back_ref,
    coef_ref,
    tail_ref,
    test,
    one,
    two,
    coef,
    sems,
):
    rank, fields, rows, lon = test.shape
    extended = rows + 2 * HALO
    band, core = band_ref[0], core_ref[0]

    def copy(c):
        at = pl.ds(c * KC, KC)
        return pltpu.make_async_copy(test_hbm.at[at], test.at[at], sems.at[c])

    for c in range(rank // KC):
        copy(c).start()

    def latitude(e):
        return band * rows - HALO + e

    def inside(e):
        at = latitude(e)
        return jnp.where((at >= 0) & (at < rows * bands), 1.0, 0.0)

    def put(f, e, line):
        line = 0.0625 + 0.015625 * line if f == 0 else (0.2 * flow_coef) * line
        line = line * inside(e)
        coef[f, e] = jnp.broadcast_to(line, (8, lon))
        coef_ref[f, pl.ds(e, 1)] = line

    for f in range(fields):
        for r in range(rows):
            put(f, HALO + r, base_ref[f, r : r + 1])
    for ref, first in ((outer_base, core), (inner_base, 1 - core)):
        values = ref[...].astype(jnp.float32)
        for f in range(fields):
            for r in range(HALO):
                put(f, first * (extended - HALO) + r, values[f * HALO + r : f * HALO + r + 1])

    turns = [
        0.5 * coriolis_coef * (2.0 * (latitude(e).astype(jnp.float32) + 0.5) / (rows * bands) - 1.0)
        for e in range(extended)
    ]
    insides = [inside(e) for e in range(extended)]

    def terms(source, e, at):
        depth, east, north = (coef[f, e] for f in range(3))
        h, u, v = (source[e, f, at] for f in range(3))
        deep = depth * h
        mine = (
            h + lon_difference(u + east * h),
            u - turns[e] * v + lon_difference(east * u + deep),
            v + turns[e] * u + lon_difference(east * v),
        )
        edge = v if HALO <= e < HALO + rows else insides[e] * v
        beside = (edge + north * h, north * u, north * v + deep)
        return mine, beside

    def keep(target, c, e, f, half, total):
        target[e, f, pl.ds(half * 8, 8)] = total

    def keep_parts(target, c, e, f, half, total):
        if f == 0:
            total = 0.25 * total
        upper = total.astype(jnp.bfloat16)
        lower = (total - upper.astype(jnp.float32)).astype(jnp.bfloat16)
        at = c * KC + half * 8
        back_ref[f * extended + e, pl.ds(at, 8)] = upper
        back_ref[f * extended + e, pl.ds(rank + at, 8)] = lower

    def backward_step(source, target, first, last, c, half, store):
        at = pl.ds(half * 8, 8)
        before = here = mine = None
        for e in range(first - 1, last + 2):
            after_mine, after = terms(source, e + 1, at) if e + 1 <= last else (None, None)
            for f in range(fields):
                total = mine[f] if mine is not None else None
                if after is not None:
                    total = after[f] if total is None else total + after[f]
                if before is not None:
                    total = -before[f] if total is None else total - before[f]
                store(target, c, e, f, half, total)
            before, here, mine = here, after, after_mine

    def chunk_body(c, carry):
        copy(c).wait()
        for half in range(KC // 8):
            at = pl.ds(half * 8, 8)
            for f in range(fields):
                part = test[pl.ds(c * KC + half * 8, 8), f].astype(jnp.float32)
                part = jnp.swapaxes(part, 0, 1)
                for r in range(rows):
                    one[HALO + r, f, at] = 4.0 * part[r] if f == 0 else part[r]
            source, target = one, two
            for step in range(STEPS):
                store = keep if step < STEPS - 1 else keep_parts
                backward_step(source, target, HALO - step, HALO + rows - 1 + step, c, half, store)
                source, target = target, source
        return carry

    lax.fori_loop(0, rank // KC, chunk_body, 0)

    forced = jnp.zeros((3 * rows, rank), jnp.float32)
    line = lax.broadcasted_iota(jnp.int32, (3 * rows, rank), 0) % rows
    field = field_ref[...].astype(jnp.bfloat16)
    for ref, first in ((outer_ref, core), (inner_ref, 1 - core)):
        for r in range(HALO):
            forced += jnp.where(line == first * HALO + r, across(field, ref[r]), 0.0)
    lane = lax.broadcasted_iota(jnp.int32, (8, rank), 0)
    forced = jnp.sum(forced, axis=0, keepdims=True)
    tail_ref[...] = jnp.where(lane == 0, forced, jnp.where(lane == 1, cost_ref[0:1, :rank], 0.0))


def sweep(band, core, test_sketch, base, outer_base, inner_base, outer, inner, field, cost, bands):
    rank, fields, rows, lon = test_sketch.shape
    extended = rows + 2 * HALO
    return pl.pallas_call(
        functools.partial(sweep_kernel, bands),
        out_shape=(
            jax.ShapeDtypeStruct((fields * extended, 2 * rank, lon), jnp.bfloat16),
            jax.ShapeDtypeStruct((fields, extended, lon), jnp.float32),
            jax.ShapeDtypeStruct((8, rank), jnp.float32),
        ),
        in_specs=[SMEM, SMEM, HBM] + [VMEM] * 7,
        out_specs=(VMEM,) * 3,
        scratch_shapes=[
            pltpu.VMEM(test_sketch.shape, jnp.bfloat16),
            pltpu.VMEM((extended, fields, KC, lon), jnp.float32),
            pltpu.VMEM((extended, fields, KC, lon), jnp.float32),
            pltpu.VMEM((fields, extended, 8, lon), jnp.float32),
            pltpu.SemaphoreType.DMA((rank // KC,)),
        ],
        compiler_params=pltpu.CompilerParams(vmem_limit_bytes=24 * MIB),
        cost_estimate=pl.CostEstimate(flops=2_000_000_000, bytes_accessed=30_000_000, transcendentals=0),
        name="sweep",
    )(band, core, on_hbm(test_sketch), base, outer_base, inner_base, outer, inner, field, cost)


def join_kernel(
    scale, core_ref, back_ref, tail_ref, outer_ref, inner_ref, outer_hbm, inner_hbm, share_ref, outer, inner, sems
):
    rank = tail_ref.shape[1]
    extended = back_ref.shape[0] // 3
    core = core_ref[0]
    pieces = 3
    step = outer.shape[0] // pieces
    sides = ((inner_hbm, inner, 1 - core), (outer_hbm, outer, core))

    def copy(s, n):
        at = pl.ds(n * step, step)
        return pltpu.make_async_copy(sides[s][0].at[at], sides[s][1].at[at], sems.at[s * pieces + n])

    for s in range(2):
        for n in range(pieces):
            copy(s, n).start()
    share = jnp.zeros((2 * rank, rank), jnp.float32)
    for ref, first in ((outer_ref, core), (inner_ref, 1 - core)):
        for i in range(outer.shape[0]):
            f, r = i // HALO, i % HALO
            share += across(back_ref[f * extended + HALO + first * HALO + r], ref[i])
    for s, side in enumerate(sides):
        for n in range(pieces):
            copy(s, n).wait()
            for i in range(n * step, (n + 1) * step):
                f, r = i // HALO, i % HALO
                share += across(back_ref[f * extended + side[2] * (extended - HALO) + r], side[1][i])
    share = (share[:rank] + share[rank:]) * scale
    half = rank // 2
    share_ref[:half] = jnp.concatenate([share[:half], share[half:]], axis=1)
    tail = tail_ref[...]
    share_ref[half:] = jnp.concatenate([tail, tail], axis=1)


def join(core, back, tail, outer, inner, far_outer, far_inner, scale):
    rank = tail.shape[1]
    return pl.pallas_call(
        functools.partial(join_kernel, scale),
        out_shape=jax.ShapeDtypeStruct((rank // 2 + 8, 2 * rank), jnp.float32),
        in_specs=[SMEM, VMEM, VMEM, VMEM, VMEM, HBM, HBM],
        out_specs=VMEM,
        scratch_shapes=[
            pltpu.VMEM(outer.shape, outer.dtype),
            pltpu.VMEM(inner.shape, inner.dtype),
            pltpu.SemaphoreType.DMA((6,)),
        ],
        compiler_params=pltpu.CompilerParams(vmem_limit_bytes=8 * MIB),
        name="join",
    )(core, back, tail, outer, inner, on_hbm(far_outer), on_hbm(far_inner))


def combine_kernel(
    scale,
    groups,
    bands,
    group_ref,
    band_ref,
    core_ref,
    *refs,
):
    shares = refs[:groups]
    (
        outer_ref,
        inner_ref,
        far_outer_hbm,
        far_inner_hbm,
        coef_ref,
        increment_hbm,
        adjoint_hbm,
        cost_hbm,
        increment,
        adjoint,
        cost_out,
        combined,
        far_outer_ref,
        far_inner_ref,
        sems,
    ) = refs[groups:]
    arrivals = [
        pltpu.make_async_copy(far_outer_hbm, far_outer_ref, sems.at[3]),
        pltpu.make_async_copy(far_inner_hbm, far_inner_ref, sems.at[4]),
    ]
    for copy in arrivals:
        copy.start()
    half = shares[0].shape[0] - 8
    rank = 2 * half
    fields, extended, lon = coef_ref.shape
    rows = extended - 2 * HALO
    core = core_ref[0]

    line = lax.broadcasted_iota(jnp.int32, (half, 2 * rank), 0)
    lane = lax.broadcasted_iota(jnp.int32, (half, 2 * rank), 1)
    left = lane < rank
    row = jnp.zeros((1, 2 * rank), jnp.float32)
    cost = jnp.zeros((1, 2 * rank), jnp.float32)
    for ahead in reversed(range(groups)):
        share = shares[ahead][...]
        cost += share[half + 1 : half + 2]
        upper = jnp.sum(jnp.where(lane == line, row, 0.0), axis=1, keepdims=True)
        lower = jnp.sum(jnp.where(lane == line + half, row, 0.0), axis=1, keepdims=True)
        product = jnp.sum(share[:half] * jnp.where(left, upper, lower), axis=0, keepdims=True)
        row = product + pltpu.roll(product, rank, 1) + share[half : half + 1]
        if ahead:
            row = jnp.where(group_ref[0] + ahead < groups, row, 0.0)
    adjoint[...] = row[:, :rank]
    cost_out[...] = cost
    copies = [
        pltpu.make_async_copy(adjoint, adjoint_hbm, sems.at[0]),
        pltpu.make_async_copy(cost_out, cost_hbm, sems.at[1]),
    ]
    for copy in copies:
        copy.start()

    pick = lax.broadcasted_iota(jnp.int32, (8, rank), 0)
    factor = jnp.zeros((8, rank), jnp.float32)
    for n, piece in enumerate(split3(row[:, :rank] * scale)):
        factor = jnp.where(pick == n, piece.astype(jnp.float32), factor)
    factor = factor.astype(jnp.bfloat16)
    places = (
        (outer_ref, HALO + core * HALO),
        (inner_ref, 2 * HALO - core * HALO),
        (far_outer_ref, core * (extended - HALO)),
        (far_inner_ref, (1 - core) * (extended - HALO)),
    )
    for n, (ref, first) in enumerate(places):
        if n >= 2:
            arrivals[n - 2].wait()
        for f in range(fields):
            for r in range(HALO):
                part = lax.dot_general(
                    factor, ref[f * HALO + r], (((1,), (0,)), ((), ())), preferred_element_type=jnp.float32
                )
                combined[f, pl.ds(first + r, 1)] = jnp.sum(part, axis=0, keepdims=True)

    latitude = band_ref[0] * rows - HALO + lax.broadcasted_iota(jnp.int32, (extended, lon), 0)
    present = (latitude >= 0) & (latitude < rows * bands)
    turn = 0.5 * coriolis_coef * (2.0 * (latitude.astype(jnp.float32) + 0.5) / (rows * bands) - 1.0)
    depth, east, north = (coef_ref[f] for f in range(3))
    h, u, v = 0.25 * combined[0], combined[1], combined[2]

    def lat_difference(x):
        return pltpu.roll(x, extended - 1, 0) - pltpu.roll(x, 1, 0)

    for _ in range(STEPS):
        dxh, dxu, dxv = (lon_difference(x) for x in (h, u, v))
        dyh, dyu, dyv = (lat_difference(x) for x in (h, u, v))
        new_u = (u + turn * v) - dxh - east * dxu - north * dyu
        new_v = (v - turn * u) - dyh - east * dxv - north * dyv
        new_h = h - depth * (dxu + dyv) - east * dxh - north * dyh
        h, u, v = (jnp.where(present, x, 0.0) for x in (new_h, new_u, new_v))
    own = slice(HALO, HALO + rows)
    for f, value in enumerate((4.0 * h, u, v)):
        increment[0, f] = value[own]
    copies.append(pltpu.make_async_copy(increment, increment_hbm, sems.at[2]))
    copies[-1].start()
    for copy in copies:
        copy.wait()


def combine(group, band, core, shares, halves, coef, scale, bands):
    fields, extended, lon = coef.shape
    rows = extended - 2 * HALO
    rank = halves[0].shape[1]
    return pl.pallas_call(
        functools.partial(combine_kernel, scale, len(shares), bands),
        out_shape=(
            jax.ShapeDtypeStruct((1, fields, rows, lon), jnp.float32),
            jax.ShapeDtypeStruct((1, rank), jnp.float32),
            jax.ShapeDtypeStruct((1, 2 * rank), jnp.float32),
        ),
        in_specs=[SMEM] * 3 + [VMEM] * (len(shares) + 2) + [HBM] * 2 + [VMEM],
        out_specs=(HBM,) * 3,
        scratch_shapes=[
            pltpu.VMEM((1, fields, rows, lon), jnp.float32),
            pltpu.VMEM((1, rank), jnp.float32),
            pltpu.VMEM((1, 2 * rank), jnp.float32),
            pltpu.VMEM((fields, extended, lon), jnp.float32),
            pltpu.VMEM(halves[2].shape, halves[2].dtype),
            pltpu.VMEM(halves[3].shape, halves[3].dtype),
            pltpu.SemaphoreType.DMA((5,)),
        ],
        compiler_params=pltpu.CompilerParams(vmem_limit_bytes=8 * MIB),
        name="combine",
    )(group, band, core, *shares, *halves[:2], *(on_hbm(x) for x in halves[2:]), coef)


def from_ahead(x, axis, by):
    count = lax.axis_size(axis)
    return lax.ppermute(x, axis, [((i + by) % count, i) for i in range(count)])


def added_over(x, axis):
    others = [from_ahead(x, axis, by) for by in range(1, lax.axis_size(axis))]
    return functools.reduce(jnp.add, others, x)


def body(
    sketch, test_sketch, checkpoints, checkpoint_step, station_row, station_column, station_value
):
    rank, fields, rows, lon = sketch.shape
    bands = lax.axis_size(LAT)
    groups = lax.axis_size("tm")
    total_rows = rows * bands
    observed = station_row.shape[1] * bands
    band = lax.axis_index(LAT).astype(jnp.int32).reshape(1)
    core = lax.axis_index("lat_2").astype(jnp.int32).reshape(1)
    group = lax.axis_index("tm").astype(jnp.int32).reshape(1)

    outer_base, inner_base, base = pick(checkpoints, checkpoint_step, core)
    across_chips = [pair for i in range(1, bands - 1, 2) for pair in ((i, i + 1), (i + 1, i))]
    inside_chip = [(0, 1), (1, 0)]
    far_outer_base = lax.ppermute(outer_base, LAT, across_chips)
    far_inner_base = lax.ppermute(inner_base, "lat_2", inside_chip)
    outer, inner = pack(sketch, core)
    outer, inner, far_outer_base, far_inner_base = lax.optimization_barrier(
        (outer, inner, far_outer_base, far_inner_base)
    )
    far_outer = lax.ppermute(outer, LAT, across_chips)
    far_inner = lax.ppermute(inner, "lat_2", inside_chip)
    field, cost = observe(
        band, base, station_row, station_column, station_value, (total_rows, observed, groups)
    )
    scale = map_scale / math.sqrt(rank * fields * total_rows * lon)
    back, coef, tail = sweep(
        band, core, test_sketch, base, far_outer_base, far_inner_base, outer, inner, field, cost, bands
    )
    share = join(core, back, tail, outer, inner, far_outer, far_inner, scale)
    for axis in ("lat_2", "lat_1", "lat_0"):
        share = added_over(share, axis)
    shares = [share] + [from_ahead(share, "tm", by) for by in range(1, groups)]
    increment, adjoint, total_cost = combine(
        group, band, core, shares, (outer, inner, far_outer, far_inner), coef, 1.0 / math.sqrt(rank), bands
    )
    return (increment, adjoint, total_cost[0, 0])


def solution(mesh):
    torus = Mesh(mesh.devices.reshape(mesh.shape["tm"], 4, 4, 2), ("tm", "lat_0", "lat_1", "lat_2"))
    in_specs = (
        P("tm", None, LAT, None),
        P("tm", None, LAT, None),
        P("tm", None, LAT, None),
        P("tm"),
        P("tm", LAT),
        P("tm", LAT),
        P("tm", LAT),
    )
    out_specs = (P("tm", None, LAT, None), P("tm", None), P())
    return jax.shard_map(body, mesh=torus, in_specs=in_specs, out_specs=out_specs, check_vma=False)
```

```python
import functools
import math

import jax
import jax.numpy as jnp
from jax import lax
from jax.experimental import pallas as pl
from jax.experimental.pallas import tpu as pltpu
from jax.sharding import Mesh
from jax.sharding import PartitionSpec as P

STEPS = 4
LAT = ("lat_0", "lat_1", "lat_2")
KC = 16
HALO = STEPS

flow_coef = 0.4
coriolis_coef = 0.5
map_scale = 0.5
MIB = 1 << 20

VMEM = pl.BlockSpec(memory_space=pltpu.VMEM)
SMEM = pl.BlockSpec(memory_space=pltpu.SMEM)
HBM = pl.BlockSpec(memory_space=pltpu.HBM)


def lon_difference(x):
    lon = x.shape[-1]
    return pltpu.roll(x, lon - 1, 1) - pltpu.roll(x, 1, 1)


def split3(x):
    high = x.astype(jnp.bfloat16)
    rest = x - high.astype(jnp.float32)
    middle = rest.astype(jnp.bfloat16)
    low = (rest - middle.astype(jnp.float32)).astype(jnp.bfloat16)
    return high, middle, low


def across(a, b):
    return lax.dot_general(a, b, (((1,), (1,)), ((), ())), preferred_element_type=jnp.float32)


def on_hbm(x):
    return pltpu.with_memory_space_constraint(x, pltpu.HBM)


def pick_kernel(step_ref, core_ref, base_hbm, outer_base, inner_base, base_ref, base, sems):
    fields = base.shape[0]
    copy = pltpu.make_async_copy(base_hbm.at[step_ref[0]], base, sems.at[0])
    copy.start()
    copy.wait()
    values = base[...].astype(jnp.float32)
    base_ref[...] = values
    pad = jnp.zeros((16 - fields * HALO, values.shape[-1]), jnp.float32)
    for core in range(2):
        low, high = (outer_base, inner_base) if core == 0 else (inner_base, outer_base)

        @pl.when(core_ref[0] == core)
        def _(low=low, high=high):
            for ref, at in ((low, 0), (high, HALO)):
                rows = [values[f, at : at + HALO] for f in range(fields)]
                ref[...] = jnp.concatenate([*rows, pad], axis=0).astype(jnp.bfloat16)


def pick(checkpoints, checkpoint_step, core):
    _, fields, rows, lon = checkpoints.shape
    lines = jax.ShapeDtypeStruct((16, lon), jnp.bfloat16)
    return pl.pallas_call(
        pick_kernel,
        out_shape=(lines, lines, jax.ShapeDtypeStruct((fields, rows, lon), jnp.float32)),
        in_specs=[SMEM, SMEM, HBM],
        out_specs=(VMEM,) * 3,
        scratch_shapes=[pltpu.VMEM((fields, rows, lon), jnp.bfloat16), pltpu.SemaphoreType.DMA((1,))],
        compiler_params=pltpu.CompilerParams(vmem_limit_bytes=8 * MIB),
        name="pick",
    )(checkpoint_step, core, on_hbm(checkpoints))


def pack_kernel(core_ref, sketch_hbm, outer_ref, inner_ref, sketch, sems):
    chunks = sketch.shape[0] // KC
    fields = sketch.shape[1]

    def copy(c):
        at = pl.ds(c * KC, KC)
        return pltpu.make_async_copy(sketch_hbm.at[at], sketch.at[at], sems.at[c])

    for c in range(chunks):
        copy(c).start()
    def chunk_body(c, carry):
        copy(c).wait()
        at = pl.ds(c * KC, KC)
        for core in range(2):
            low, high = (outer_ref, inner_ref) if core == 0 else (inner_ref, outer_ref)

            @pl.when(core_ref[0] == core)
            def _(low=low, high=high):
                for f in range(fields):
                    part = jnp.swapaxes(sketch[at, f].astype(jnp.float32), 0, 1)
                    part = part.astype(jnp.bfloat16)
                    for ref, rows in ((low, part[:HALO]), (high, part[HALO:])):
                        ref[f * HALO : (f + 1) * HALO, at] = rows

        return carry

    lax.fori_loop(0, chunks, chunk_body, 0)


def pack(sketch, core):
    rank, fields, rows, lon = sketch.shape
    half = jax.ShapeDtypeStruct((fields * HALO, rank, lon), jnp.bfloat16)
    return pl.pallas_call(
        pack_kernel,
        out_shape=(half, half),
        in_specs=[SMEM, HBM],
        out_specs=(VMEM,) * 2,
        scratch_shapes=[pltpu.VMEM(sketch.shape, sketch.dtype), pltpu.SemaphoreType.DMA((rank // KC,))],
        compiler_params=pltpu.CompilerParams(vmem_limit_bytes=8 * MIB),
        name="pack",
    )(core, on_hbm(sketch))


def observe_kernel(scales, band_ref, base_ref, row_ref, column_ref, value_ref, field_ref, cost_ref):
    total_rows, observed, groups = scales
    rows, lon = base_ref.shape[-2:]
    count = row_ref.shape[-1]
    station_row = row_ref[...]
    local = station_row - band_ref[0] * rows
    at_column = lax.broadcasted_iota(jnp.int32, (lon, count), 0) == column_ref[...]
    at_column = jnp.where(at_column, 1.0, 0.0).astype(jnp.bfloat16)
    at_row = lax.broadcasted_iota(jnp.int32, (rows, count), 0) == local
    found = lax.dot_general(
        base_ref[0].astype(jnp.bfloat16), at_column, (((1,), (0,)), ((), ())), preferred_element_type=jnp.float32
    )
    here = jnp.sum(jnp.where(at_row, found, 0.0), axis=0, keepdims=True)
    innovation = here - value_ref[...]
    weight = 1.0 + 2.0 * station_row.astype(jnp.float32) / total_rows
    weighted = weight * innovation
    cost = jnp.sum(weighted * innovation, axis=1, keepdims=True) / (2.0 * groups * observed)
    cost_ref[...] = jnp.broadcast_to(cost, cost_ref.shape)
    spread = jnp.where(at_row, weighted / (2.0 * math.sqrt(observed)), 0.0)
    field = jnp.zeros((rows, lon), jnp.float32)
    for piece in split3(spread):
        field += across(piece, at_column)
    for n, piece in enumerate(split3(field)):
        field_ref[n * rows : (n + 1) * rows] = piece.astype(jnp.float32)


def observe(band, base, station_row, station_column, station_value, scales):
    rows, lon = base.shape[-2:]
    return pl.pallas_call(
        functools.partial(observe_kernel, scales),
        out_shape=(
            jax.ShapeDtypeStruct((3 * rows, lon), jnp.float32),
            jax.ShapeDtypeStruct((1, 128), jnp.float32),
        ),
        in_specs=[SMEM] + [VMEM] * 4,
        out_specs=(VMEM, VMEM),
        compiler_params=pltpu.CompilerParams(vmem_limit_bytes=8 * MIB),
        cost_estimate=pl.CostEstimate(flops=20_000_000, bytes_accessed=1_000_000, transcendentals=0),
        name="observe",
    )(band, base, station_row, station_column, station_value)


def sweep_kernel(
    bands,
    band_ref,
    core_ref,
    test_hbm,
    base_ref,
    outer_base,
    inner_base,
    outer_ref,
    inner_ref,
    field_ref,
    cost_ref,
    back_ref,
    coef_ref,
    tail_ref,
    test,
    one,
    two,
    coef,
    sems,
):
    rank, fields, rows, lon = test.shape
    extended = rows + 2 * HALO
    band, core = band_ref[0], core_ref[0]

    def copy(c):
        at = pl.ds(c * KC, KC)
        return pltpu.make_async_copy(test_hbm.at[at], test.at[at], sems.at[c])

    for c in range(rank // KC):
        copy(c).start()

    def latitude(e):
        return band * rows - HALO + e

    def inside(e):
        at = latitude(e)
        return jnp.where((at >= 0) & (at < rows * bands), 1.0, 0.0)

    def put(f, e, line):
        line = 0.0625 + 0.015625 * line if f == 0 else (0.2 * flow_coef) * line
        line = line * inside(e)
        coef[f, e] = jnp.broadcast_to(line, (8, lon))
        coef_ref[f, pl.ds(e, 1)] = line

    def own_row(r, carry):
        for f in range(fields):
            put(f, HALO + r, base_ref[f, pl.ds(r, 1)])
        return carry

    lax.fori_loop(0, rows, own_row, 0)
    for ref, first in ((outer_base, core), (inner_base, 1 - core)):
        values = ref[...].astype(jnp.float32)
        for f in range(fields):
            for r in range(HALO):
                put(f, first * (extended - HALO) + r, values[f * HALO + r : f * HALO + r + 1])

    turns = [
        0.5 * coriolis_coef * (2.0 * (latitude(e).astype(jnp.float32) + 0.5) / (rows * bands) - 1.0)
        for e in range(extended)
    ]
    insides = [inside(e) for e in range(extended)]

    def terms(source, e, at):
        depth, east, north = (coef[f, e] for f in range(3))
        h, u, v = (source[e, f, at] for f in range(3))
        deep = depth * h
        mine = (
            h + lon_difference(u + east * h),
            u - turns[e] * v + lon_difference(east * u + deep),
            v + turns[e] * u + lon_difference(east * v),
        )
        edge = v if HALO <= e < HALO + rows else insides[e] * v
        beside = (edge + north * h, north * u, north * v + deep)
        return mine, beside

    def keep(target, c, e, f, half, total):
        target[e, f, pl.ds(half * 8, 8)] = total

    def keep_parts(target, c, e, f, half, total):
        if f == 0:
            total = 0.25 * total
        upper = total.astype(jnp.bfloat16)
        lower = (total - upper.astype(jnp.float32)).astype(jnp.bfloat16)
        at = c * KC + half * 8
        back_ref[f * extended + e, pl.ds(at, 8)] = upper
        back_ref[f * extended + e, pl.ds(rank + at, 8)] = lower

    def backward_step(source, target, first, last, c, half, store):
        at = pl.ds(half * 8, 8)
        before = here = mine = None
        for e in range(first - 1, last + 2):
            after_mine, after = terms(source, e + 1, at) if e + 1 <= last else (None, None)
            for f in range(fields):
                total = mine[f] if mine is not None else None
                if after is not None:
                    total = after[f] if total is None else total + after[f]
                if before is not None:
                    total = -before[f] if total is None else total - before[f]
                store(target, c, e, f, half, total)
            before, here, mine = here, after, after_mine

    def chunk_body(c, carry):
        copy(c).wait()
        for half in range(KC // 8):
            at = pl.ds(half * 8, 8)
            for f in range(fields):
                part = test[pl.ds(c * KC + half * 8, 8), f].astype(jnp.float32)
                part = jnp.swapaxes(part, 0, 1)
                for r in range(rows):
                    one[HALO + r, f, at] = 4.0 * part[r] if f == 0 else part[r]
            source, target = one, two
            for step in range(STEPS):
                store = keep if step < STEPS - 1 else keep_parts
                backward_step(source, target, HALO - step, HALO + rows - 1 + step, c, half, store)
                source, target = target, source
        return carry

    lax.fori_loop(0, rank // KC, chunk_body, 0)

    forced = jnp.zeros((3 * rows, rank), jnp.float32)
    line = lax.broadcasted_iota(jnp.int32, (3 * rows, rank), 0) % rows
    field = field_ref[...].astype(jnp.bfloat16)
    for ref, first in ((outer_ref, core), (inner_ref, 1 - core)):
        for r in range(HALO):
            forced += jnp.where(line == first * HALO + r, across(field, ref[r]), 0.0)
    lane = lax.broadcasted_iota(jnp.int32, (8, rank), 0)
    forced = jnp.sum(forced, axis=0, keepdims=True)
    tail_ref[...] = jnp.where(lane == 0, forced, jnp.where(lane == 1, cost_ref[0:1, :rank], 0.0))


def sweep(band, core, test_sketch, base, outer_base, inner_base, outer, inner, field, cost, bands):
    rank, fields, rows, lon = test_sketch.shape
    extended = rows + 2 * HALO
    return pl.pallas_call(
        functools.partial(sweep_kernel, bands),
        out_shape=(
            jax.ShapeDtypeStruct((fields * extended, 2 * rank, lon), jnp.bfloat16),
            jax.ShapeDtypeStruct((fields, extended, lon), jnp.float32),
            jax.ShapeDtypeStruct((8, rank), jnp.float32),
        ),
        in_specs=[SMEM, SMEM, HBM] + [VMEM] * 7,
        out_specs=(VMEM,) * 3,
        scratch_shapes=[
            pltpu.VMEM(test_sketch.shape, jnp.bfloat16),
            pltpu.VMEM((extended, fields, KC, lon), jnp.float32),
            pltpu.VMEM((extended, fields, KC, lon), jnp.float32),
            pltpu.VMEM((fields, extended, 8, lon), jnp.float32),
            pltpu.SemaphoreType.DMA((rank // KC,)),
        ],
        compiler_params=pltpu.CompilerParams(vmem_limit_bytes=24 * MIB),
        cost_estimate=pl.CostEstimate(flops=2_000_000_000, bytes_accessed=30_000_000, transcendentals=0),
        name="sweep",
    )(band, core, on_hbm(test_sketch), base, outer_base, inner_base, outer, inner, field, cost)


def join_kernel(
    scale, core_ref, back_ref, tail_ref, outer_ref, inner_ref, outer_hbm, inner_hbm, share_ref, outer, inner, sems
):
    rank = tail_ref.shape[1]
    extended = back_ref.shape[0] // 3
    core = core_ref[0]
    pieces = 3
    step = outer.shape[0] // pieces
    sides = ((inner_hbm, inner, 1 - core), (outer_hbm, outer, core))

    def copy(s, n):
        at = pl.ds(n * step, step)
        return pltpu.make_async_copy(sides[s][0].at[at], sides[s][1].at[at], sems.at[s * pieces + n])

    for s in range(2):
        for n in range(pieces):
            copy(s, n).start()
    share = jnp.zeros((2 * rank, rank), jnp.float32)

    def products(places, share):
        def one_field(f, share):
            for ref, first in places:
                for r in range(HALO):
                    share += across(back_ref[f * extended + first + r], ref[f * HALO + r])
            return share

        return lax.fori_loop(0, back_ref.shape[0] // extended, one_field, share)

    share = products(((outer_ref, HALO + core * HALO), (inner_ref, 2 * HALO - core * HALO)), share)
    for s, side in enumerate(sides):
        for n in range(pieces):
            copy(s, n).wait()
        share = products(((side[1], side[2] * (extended - HALO)),), share)
    share = (share[:rank] + share[rank:]) * scale
    half = rank // 2
    share_ref[:half] = jnp.concatenate([share[:half], share[half:]], axis=1)
    tail = tail_ref[...]
    share_ref[half:] = jnp.concatenate([tail, tail], axis=1)


def join(core, back, tail, outer, inner, far_outer, far_inner, scale):
    rank = tail.shape[1]
    return pl.pallas_call(
        functools.partial(join_kernel, scale),
        out_shape=jax.ShapeDtypeStruct((rank // 2 + 8, 2 * rank), jnp.float32),
        in_specs=[SMEM, VMEM, VMEM, VMEM, VMEM, HBM, HBM],
        out_specs=VMEM,
        scratch_shapes=[
            pltpu.VMEM(outer.shape, outer.dtype),
            pltpu.VMEM(inner.shape, inner.dtype),
            pltpu.SemaphoreType.DMA((6,)),
        ],
        compiler_params=pltpu.CompilerParams(vmem_limit_bytes=8 * MIB),
        name="join",
    )(core, back, tail, outer, inner, on_hbm(far_outer), on_hbm(far_inner))


def fetch_kernel(outer_hbm, inner_hbm, share_ref, outer_ref, inner_ref, sems):
    copies = [
        pltpu.make_async_copy(outer_hbm, outer_ref, sems.at[0]),
        pltpu.make_async_copy(inner_hbm, inner_ref, sems.at[1]),
    ]
    for copy in copies:
        copy.start()
    for copy in copies:
        copy.wait()


def fetch(outer, inner, share):
    received = jax.ShapeDtypeStruct(outer.shape, outer.dtype)
    return pl.pallas_call(
        fetch_kernel,
        out_shape=(received, received),
        in_specs=[HBM, HBM, VMEM],
        out_specs=(VMEM, VMEM),
        scratch_shapes=[pltpu.SemaphoreType.DMA((2,))],
        compiler_params=pltpu.CompilerParams(vmem_limit_bytes=4 * MIB),
        cost_estimate=pl.CostEstimate(flops=0, bytes_accessed=6_300_000, transcendentals=0),
        name="fetch",
    )(on_hbm(outer), on_hbm(inner), share)


def combine_kernel(
    scale,
    groups,
    bands,
    group_ref,
    band_ref,
    core_ref,
    *refs,
):
    shares = refs[:groups]
    (
        outer_ref,
        inner_ref,
        far_outer_ref,
        far_inner_ref,
        coef_ref,
        increment_hbm,
        adjoint_hbm,
        cost_hbm,
        increment,
        adjoint,
        cost_out,
        combined,
        sems,
    ) = refs[groups:]
    half = shares[0].shape[0] - 8
    rank = 2 * half
    fields, extended, lon = coef_ref.shape
    rows = extended - 2 * HALO
    core = core_ref[0]

    line = lax.broadcasted_iota(jnp.int32, (half, 2 * rank), 0)
    lane = lax.broadcasted_iota(jnp.int32, (half, 2 * rank), 1)
    left = lane < rank
    row = jnp.zeros((1, 2 * rank), jnp.float32)
    cost = jnp.zeros((1, 2 * rank), jnp.float32)
    for ahead in reversed(range(groups)):
        share = shares[ahead][...]
        cost += share[half + 1 : half + 2]
        upper = jnp.sum(jnp.where(lane == line, row, 0.0), axis=1, keepdims=True)
        lower = jnp.sum(jnp.where(lane == line + half, row, 0.0), axis=1, keepdims=True)
        product = jnp.sum(share[:half] * jnp.where(left, upper, lower), axis=0, keepdims=True)
        row = product + pltpu.roll(product, rank, 1) + share[half : half + 1]
        if ahead:
            row = jnp.where(group_ref[0] + ahead < groups, row, 0.0)
    adjoint[...] = row[:, :rank]
    cost_out[...] = cost
    copies = [
        pltpu.make_async_copy(adjoint, adjoint_hbm, sems.at[0]),
        pltpu.make_async_copy(cost_out, cost_hbm, sems.at[1]),
    ]
    for copy in copies:
        copy.start()

    pick = lax.broadcasted_iota(jnp.int32, (8, rank), 0)
    factor = jnp.zeros((8, rank), jnp.float32)
    for n, piece in enumerate(split3(row[:, :rank] * scale)):
        factor = jnp.where(pick == n, piece.astype(jnp.float32), factor)
    factor = factor.astype(jnp.bfloat16)
    places = (
        (outer_ref, HALO + core * HALO),
        (inner_ref, 2 * HALO - core * HALO),
        (far_outer_ref, core * (extended - HALO)),
        (far_inner_ref, (1 - core) * (extended - HALO)),
    )

    def one_field(f, carry):
        for ref, first in places:
            for r in range(HALO):
                part = lax.dot_general(
                    factor, ref[f * HALO + r], (((1,), (0,)), ((), ())), preferred_element_type=jnp.float32
                )
                combined[f, pl.ds(first + r, 1)] = jnp.sum(part, axis=0, keepdims=True)
        return carry

    lax.fori_loop(0, fields, one_field, 0)

    latitude = band_ref[0] * rows - HALO + lax.broadcasted_iota(jnp.int32, (extended, lon), 0)
    present = (latitude >= 0) & (latitude < rows * bands)
    turn = 0.5 * coriolis_coef * (2.0 * (latitude.astype(jnp.float32) + 0.5) / (rows * bands) - 1.0)
    combined[0] = 0.25 * combined[0]

    def lat_difference(x):
        return pltpu.roll(x, extended - 1, 0) - pltpu.roll(x, 1, 0)

    def step(_, carry):
        depth, east, north = (coef_ref[f] for f in range(3))
        h, u, v = (combined[f] for f in range(3))
        dxh, dxu, dxv = (lon_difference(x) for x in (h, u, v))
        dyh, dyu, dyv = (lat_difference(x) for x in (h, u, v))
        new_u = (u + turn * v) - dxh - east * dxu - north * dyu
        new_v = (v - turn * u) - dyh - east * dxv - north * dyv
        new_h = h - depth * (dxu + dyv) - east * dxh - north * dyh
        for f, x in enumerate((new_h, new_u, new_v)):
            combined[f] = jnp.where(present, x, 0.0)
        return carry

    lax.fori_loop(0, STEPS, step, 0)
    for f in range(fields):
        value = combined[f, HALO : HALO + rows]
        increment[0, f] = 4.0 * value if f == 0 else value
    copies.append(pltpu.make_async_copy(increment, increment_hbm, sems.at[2]))
    copies[-1].start()
    for copy in copies:
        copy.wait()


def combine(group, band, core, shares, halves, coef, scale, bands):
    fields, extended, lon = coef.shape
    rows = extended - 2 * HALO
    rank = halves[0].shape[1]
    return pl.pallas_call(
        functools.partial(combine_kernel, scale, len(shares), bands),
        out_shape=(
            jax.ShapeDtypeStruct((1, fields, rows, lon), jnp.float32),
            jax.ShapeDtypeStruct((1, rank), jnp.float32),
            jax.ShapeDtypeStruct((1, 2 * rank), jnp.float32),
        ),
        in_specs=[SMEM] * 3 + [VMEM] * (len(shares) + 5),
        out_specs=(HBM,) * 3,
        scratch_shapes=[
            pltpu.VMEM((1, fields, rows, lon), jnp.float32),
            pltpu.VMEM((1, rank), jnp.float32),
            pltpu.VMEM((1, 2 * rank), jnp.float32),
            pltpu.VMEM((fields, extended, lon), jnp.float32),
            pltpu.SemaphoreType.DMA((3,)),
        ],
        compiler_params=pltpu.CompilerParams(vmem_limit_bytes=8 * MIB),
        name="combine",
    )(group, band, core, *shares, *halves, coef)


def from_ahead(x, axis, by):
    count = lax.axis_size(axis)
    return lax.ppermute(x, axis, [((i + by) % count, i) for i in range(count)])


def added_over(x, axis):
    others = [from_ahead(x, axis, by) for by in range(1, lax.axis_size(axis))]
    return functools.reduce(jnp.add, others, x)


def body(
    sketch, test_sketch, checkpoints, checkpoint_step, station_row, station_column, station_value
):
    rank, fields, rows, lon = sketch.shape
    bands = lax.axis_size(LAT)
    groups = lax.axis_size("tm")
    total_rows = rows * bands
    observed = station_row.shape[1] * bands
    band = lax.axis_index(LAT).astype(jnp.int32).reshape(1)
    core = lax.axis_index("lat_2").astype(jnp.int32).reshape(1)
    group = lax.axis_index("tm").astype(jnp.int32).reshape(1)

    outer_base, inner_base, base = pick(checkpoints, checkpoint_step, core)
    across_chips = [pair for i in range(1, bands - 1, 2) for pair in ((i, i + 1), (i + 1, i))]
    inside_chip = [(0, 1), (1, 0)]
    far_outer_base = lax.ppermute(outer_base, LAT, across_chips)
    far_inner_base = lax.ppermute(inner_base, "lat_2", inside_chip)
    outer, inner = pack(sketch, core)
    outer, inner, far_outer_base, far_inner_base = lax.optimization_barrier(
        (outer, inner, far_outer_base, far_inner_base)
    )
    far_outer = lax.ppermute(outer, LAT, across_chips)
    far_inner = lax.ppermute(inner, "lat_2", inside_chip)
    field, cost = observe(
        band, base, station_row, station_column, station_value, (total_rows, observed, groups)
    )
    scale = map_scale / math.sqrt(rank * fields * total_rows * lon)
    back, coef, tail = sweep(
        band, core, test_sketch, base, far_outer_base, far_inner_base, outer, inner, field, cost, bands
    )
    share = join(core, back, tail, outer, inner, far_outer, far_inner, scale)
    for axis in ("lat_2", "lat_1", "lat_0"):
        share = added_over(share, axis)
    far_outer, far_inner = fetch(far_outer, far_inner, share)
    shares = [share] + [from_ahead(share, "tm", by) for by in range(1, groups)]
    increment, adjoint, total_cost = combine(
        group, band, core, shares, (outer, inner, far_outer, far_inner), coef, 1.0 / math.sqrt(rank), bands
    )
    return (increment, adjoint, total_cost[0, 0])


def solution(mesh):
    torus = Mesh(mesh.devices.reshape(mesh.shape["tm"], 4, 4, 2), ("tm", "lat_0", "lat_1", "lat_2"))
    in_specs = (
        P("tm", None, LAT, None),
        P("tm", None, LAT, None),
        P("tm", None, LAT, None),
        P("tm"),
        P("tm", LAT),
        P("tm", LAT),
        P("tm", LAT),
    )
    out_specs = (P("tm", None, LAT, None), P("tm", None), P())
    return jax.shard_map(body, mesh=torus, in_specs=in_specs, out_specs=out_specs, check_vma=False)
```

```python
import functools
import math

import jax
import jax.numpy as jnp
from jax import lax
from jax.experimental import pallas as pl
from jax.experimental.pallas import tpu as pltpu
from jax.sharding import Mesh
from jax.sharding import PartitionSpec as P

STEPS = 4
LAT = ("lat_0", "lat_1", "lat_2")
KC = 16
HALO = STEPS

flow_coef = 0.4
coriolis_coef = 0.5
map_scale = 0.5
MIB = 1 << 20

VMEM = pl.BlockSpec(memory_space=pltpu.VMEM)
SMEM = pl.BlockSpec(memory_space=pltpu.SMEM)
HBM = pl.BlockSpec(memory_space=pltpu.HBM)


def lon_difference(x):
    lon = x.shape[-1]
    return pltpu.roll(x, lon - 1, 1) - pltpu.roll(x, 1, 1)


def split3(x):
    high = x.astype(jnp.bfloat16)
    rest = x - high.astype(jnp.float32)
    middle = rest.astype(jnp.bfloat16)
    low = (rest - middle.astype(jnp.float32)).astype(jnp.bfloat16)
    return high, middle, low


def across(a, b):
    return lax.dot_general(a, b, (((1,), (1,)), ((), ())), preferred_element_type=jnp.float32)


def on_hbm(x):
    return pltpu.with_memory_space_constraint(x, pltpu.HBM)


def pick_kernel(step_ref, core_ref, base_hbm, outer_base, inner_base, base_ref, base, sems):
    fields = base.shape[0]
    copy = pltpu.make_async_copy(base_hbm.at[step_ref[0]], base, sems.at[0])
    copy.start()
    copy.wait()
    values = base[...].astype(jnp.float32)
    base_ref[...] = values
    pad = jnp.zeros((16 - fields * HALO, values.shape[-1]), jnp.float32)
    for core in range(2):
        low, high = (outer_base, inner_base) if core == 0 else (inner_base, outer_base)

        @pl.when(core_ref[0] == core)
        def _(low=low, high=high):
            for ref, at in ((low, 0), (high, HALO)):
                rows = [values[f, at : at + HALO] for f in range(fields)]
                ref[...] = jnp.concatenate([*rows, pad], axis=0).astype(jnp.bfloat16)


def pick(checkpoints, checkpoint_step, core):
    _, fields, rows, lon = checkpoints.shape
    lines = jax.ShapeDtypeStruct((16, lon), jnp.bfloat16)
    return pl.pallas_call(
        pick_kernel,
        out_shape=(lines, lines, jax.ShapeDtypeStruct((fields, rows, lon), jnp.float32)),
        in_specs=[SMEM, SMEM, HBM],
        out_specs=(VMEM,) * 3,
        scratch_shapes=[pltpu.VMEM((fields, rows, lon), jnp.bfloat16), pltpu.SemaphoreType.DMA((1,))],
        compiler_params=pltpu.CompilerParams(vmem_limit_bytes=8 * MIB),
        name="pick",
    )(checkpoint_step, core, on_hbm(checkpoints))


def pack_kernel(core_ref, sketch_hbm, outer_ref, inner_ref, sketch, sems):
    chunks = sketch.shape[0] // KC
    fields = sketch.shape[1]

    def copy(c):
        at = pl.ds(c * KC, KC)
        return pltpu.make_async_copy(sketch_hbm.at[at], sketch.at[at], sems.at[c])

    for c in range(chunks):
        copy(c).start()
    def chunk_body(c, carry):
        copy(c).wait()
        at = pl.ds(c * KC, KC)
        for core in range(2):
            low, high = (outer_ref, inner_ref) if core == 0 else (inner_ref, outer_ref)

            @pl.when(core_ref[0] == core)
            def _(low=low, high=high):
                for f in range(fields):
                    part = jnp.swapaxes(sketch[at, f].astype(jnp.float32), 0, 1)
                    part = part.astype(jnp.bfloat16)
                    for ref, rows in ((low, part[:HALO]), (high, part[HALO:])):
                        ref[f * HALO : (f + 1) * HALO, at] = rows

        return carry

    lax.fori_loop(0, chunks, chunk_body, 0)


def pack(sketch, core):
    rank, fields, rows, lon = sketch.shape
    half = jax.ShapeDtypeStruct((fields * HALO, rank, lon), jnp.bfloat16)
    return pl.pallas_call(
        pack_kernel,
        out_shape=(half, half),
        in_specs=[SMEM, HBM],
        out_specs=(VMEM,) * 2,
        scratch_shapes=[pltpu.VMEM(sketch.shape, sketch.dtype), pltpu.SemaphoreType.DMA((rank // KC,))],
        compiler_params=pltpu.CompilerParams(vmem_limit_bytes=8 * MIB),
        name="pack",
    )(core, on_hbm(sketch))


def observed(scales, band, height, station_row, station_column, station_value):
    total_rows, observations, groups = scales
    rows, lon = height.shape
    count = station_row.shape[-1]
    local = station_row - band * rows
    at_column = lax.broadcasted_iota(jnp.int32, (lon, count), 0) == station_column
    at_column = jnp.where(at_column, 1.0, 0.0).astype(jnp.bfloat16)
    at_row = lax.broadcasted_iota(jnp.int32, (rows, count), 0) == local
    found = lax.dot_general(
        height.astype(jnp.bfloat16), at_column, (((1,), (0,)), ((), ())), preferred_element_type=jnp.float32
    )
    here = jnp.sum(jnp.where(at_row, found, 0.0), axis=0, keepdims=True)
    innovation = here - station_value
    weight = 1.0 + 2.0 * station_row.astype(jnp.float32) / total_rows
    weighted = weight * innovation
    cost = jnp.sum(weighted * innovation, axis=1, keepdims=True) / (2.0 * groups * observations)
    spread = jnp.where(at_row, weighted / (2.0 * math.sqrt(observations)), 0.0)
    field = jnp.zeros((rows, lon), jnp.float32)
    for piece in split3(spread):
        field += across(piece, at_column)
    pieces = [piece.astype(jnp.float32) for piece in split3(field)]
    return jnp.concatenate(pieces, axis=0).astype(jnp.bfloat16), cost


def sweep_kernel(
    scales,
    bands,
    band_ref,
    core_ref,
    test_hbm,
    base_ref,
    outer_base,
    inner_base,
    outer_ref,
    inner_ref,
    station_row_ref,
    station_column_ref,
    station_value_ref,
    back_ref,
    coef_ref,
    tail_ref,
    test,
    one,
    two,
    coef,
    sems,
):
    rank, fields, rows, lon = test.shape
    extended = rows + 2 * HALO
    band, core = band_ref[0], core_ref[0]

    def copy(c):
        at = pl.ds(c * KC, KC)
        return pltpu.make_async_copy(test_hbm.at[at], test.at[at], sems.at[c])

    for c in range(rank // KC):
        copy(c).start()

    def latitude(e):
        return band * rows - HALO + e

    def inside(e):
        at = latitude(e)
        return jnp.where((at >= 0) & (at < rows * bands), 1.0, 0.0)

    def put(f, e, line):
        line = 0.0625 + 0.015625 * line if f == 0 else (0.2 * flow_coef) * line
        line = line * inside(e)
        coef[f, e] = jnp.broadcast_to(line, (8, lon))
        coef_ref[f, pl.ds(e, 1)] = line

    def own_row(r, carry):
        for f in range(fields):
            put(f, HALO + r, base_ref[f, pl.ds(r, 1)])
        return carry

    lax.fori_loop(0, rows, own_row, 0)
    for ref, first in ((outer_base, core), (inner_base, 1 - core)):
        values = ref[...].astype(jnp.float32)
        for f in range(fields):
            for r in range(HALO):
                put(f, first * (extended - HALO) + r, values[f * HALO + r : f * HALO + r + 1])

    forced = jnp.zeros((3 * rows, rank), jnp.float32)
    line = lax.broadcasted_iota(jnp.int32, (3 * rows, rank), 0) % rows
    field, cost = observed(
        scales, band, base_ref[0], station_row_ref[...], station_column_ref[...], station_value_ref[...]
    )
    for ref, first in ((outer_ref, core), (inner_ref, 1 - core)):
        for r in range(HALO):
            forced += jnp.where(line == first * HALO + r, across(field, ref[r]), 0.0)
    lane = lax.broadcasted_iota(jnp.int32, (8, rank), 0)
    forced = jnp.sum(forced, axis=0, keepdims=True)
    tail_ref[...] = jnp.where(lane == 0, forced, jnp.where(lane == 1, cost, 0.0))

    turns = [
        0.5 * coriolis_coef * (2.0 * (latitude(e).astype(jnp.float32) + 0.5) / (rows * bands) - 1.0)
        for e in range(extended)
    ]
    insides = [inside(e) for e in range(extended)]

    def terms(source, e, at):
        depth, east, north = (coef[f, e] for f in range(3))
        h, u, v = (source[e, f, at] for f in range(3))
        deep = depth * h
        mine = (
            h + lon_difference(u + east * h),
            u - turns[e] * v + lon_difference(east * u + deep),
            v + turns[e] * u + lon_difference(east * v),
        )
        edge = v if HALO <= e < HALO + rows else insides[e] * v
        beside = (edge + north * h, north * u, north * v + deep)
        return mine, beside

    def keep(target, c, e, f, half, total):
        target[e, f, pl.ds(half * 8, 8)] = total

    def keep_parts(target, c, e, f, half, total):
        if f == 0:
            total = 0.25 * total
        upper = total.astype(jnp.bfloat16)
        lower = (total - upper.astype(jnp.float32)).astype(jnp.bfloat16)
        at = c * KC + half * 8
        back_ref[f * extended + e, pl.ds(at, 8)] = upper
        back_ref[f * extended + e, pl.ds(rank + at, 8)] = lower

    def backward_step(source, target, first, last, c, half, store):
        at = pl.ds(half * 8, 8)
        before = here = mine = None
        for e in range(first - 1, last + 2):
            after_mine, after = terms(source, e + 1, at) if e + 1 <= last else (None, None)
            for f in range(fields):
                total = mine[f] if mine is not None else None
                if after is not None:
                    total = after[f] if total is None else total + after[f]
                if before is not None:
                    total = -before[f] if total is None else total - before[f]
                store(target, c, e, f, half, total)
            before, here, mine = here, after, after_mine

    def chunk_body(c, carry):
        copy(c).wait()
        for half in range(KC // 8):
            at = pl.ds(half * 8, 8)
            for f in range(fields):
                part = test[pl.ds(c * KC + half * 8, 8), f].astype(jnp.float32)
                part = jnp.swapaxes(part, 0, 1)
                for r in range(rows):
                    one[HALO + r, f, at] = 4.0 * part[r] if f == 0 else part[r]
            source, target = one, two
            for step in range(STEPS):
                store = keep if step < STEPS - 1 else keep_parts
                backward_step(source, target, HALO - step, HALO + rows - 1 + step, c, half, store)
                source, target = target, source
        return carry

    lax.fori_loop(0, rank // KC, chunk_body, 0)


def sweep(band, core, test_sketch, base, outer_base, inner_base, outer, inner, stations, scales, bands):
    rank, fields, rows, lon = test_sketch.shape
    extended = rows + 2 * HALO
    return pl.pallas_call(
        functools.partial(sweep_kernel, scales, bands),
        out_shape=(
            jax.ShapeDtypeStruct((fields * extended, 2 * rank, lon), jnp.bfloat16),
            jax.ShapeDtypeStruct((fields, extended, lon), jnp.float32),
            jax.ShapeDtypeStruct((8, rank), jnp.float32),
        ),
        in_specs=[SMEM, SMEM, HBM] + [VMEM] * 8,
        out_specs=(VMEM,) * 3,
        scratch_shapes=[
            pltpu.VMEM(test_sketch.shape, jnp.bfloat16),
            pltpu.VMEM((extended, fields, KC, lon), jnp.float32),
            pltpu.VMEM((extended, fields, KC, lon), jnp.float32),
            pltpu.VMEM((fields, extended, 8, lon), jnp.float32),
            pltpu.SemaphoreType.DMA((rank // KC,)),
        ],
        compiler_params=pltpu.CompilerParams(vmem_limit_bytes=24 * MIB),
        cost_estimate=pl.CostEstimate(flops=2_000_000_000, bytes_accessed=30_000_000, transcendentals=0),
        name="sweep",
    )(band, core, on_hbm(test_sketch), base, outer_base, inner_base, outer, inner, *stations)


def join_kernel(
    scale, core_ref, back_ref, tail_ref, outer_ref, inner_ref, outer_hbm, inner_hbm, share_ref, outer, inner, sums, sems
):
    rank = tail_ref.shape[1]
    extended = back_ref.shape[0] // 3
    core = core_ref[0]
    pieces = 3
    step = outer.shape[0] // pieces
    sides = ((inner_hbm, inner, 1 - core), (outer_hbm, outer, core))

    def copy(s, n):
        at = pl.ds(n * step, step)
        return pltpu.make_async_copy(sides[s][0].at[at], sides[s][1].at[at], sems.at[s * pieces + n])

    for s in range(2):
        for n in range(pieces):
            copy(s, n).start()
    def products(places):
        total = jnp.zeros((2 * rank, rank), jnp.float32)
        for ref, first in places:
            for i in range(ref.shape[0]):
                total += across(back_ref[i // HALO * extended + first + i % HALO], ref[i])
        return total

    for at in range(2):

        @pl.when(core == at)
        def _(at=at):
            sums[...] = products(((outer_ref, HALO + at * HALO), (inner_ref, 2 * HALO - at * HALO)))

    for s in range(2):
        for n in range(pieces):
            copy(s, n).wait()
    for at in range(2):

        @pl.when(core == at)
        def _(at=at):
            sums[...] += products(
                ((inner, (1 - at) * (extended - HALO)), (outer, at * (extended - HALO)))
            )

    share = sums[...]
    share = (share[:rank] + share[rank:]) * scale
    half = rank // 2
    share_ref[:half] = jnp.concatenate([share[:half], share[half:]], axis=1)
    tail = tail_ref[...]
    share_ref[half:] = jnp.concatenate([tail, tail], axis=1)


def join(core, back, tail, outer, inner, far_outer, far_inner, scale):
    rank = tail.shape[1]
    return pl.pallas_call(
        functools.partial(join_kernel, scale),
        out_shape=jax.ShapeDtypeStruct((rank // 2 + 8, 2 * rank), jnp.float32),
        in_specs=[SMEM, VMEM, VMEM, VMEM, VMEM, HBM, HBM],
        out_specs=VMEM,
        scratch_shapes=[
            pltpu.VMEM(outer.shape, outer.dtype),
            pltpu.VMEM(inner.shape, inner.dtype),
            pltpu.VMEM((2 * rank, rank), jnp.float32),
            pltpu.SemaphoreType.DMA((6,)),
        ],
        compiler_params=pltpu.CompilerParams(vmem_limit_bytes=8 * MIB),
        name="join",
    )(core, back, tail, outer, inner, on_hbm(far_outer), on_hbm(far_inner))


def fetch_kernel(outer_hbm, inner_hbm, share_ref, outer_ref, inner_ref, sems):
    copies = [
        pltpu.make_async_copy(outer_hbm, outer_ref, sems.at[0]),
        pltpu.make_async_copy(inner_hbm, inner_ref, sems.at[1]),
    ]
    for copy in copies:
        copy.start()
    for copy in copies:
        copy.wait()


def fetch(outer, inner, share):
    received = jax.ShapeDtypeStruct(outer.shape, outer.dtype)
    return pl.pallas_call(
        fetch_kernel,
        out_shape=(received, received),
        in_specs=[HBM, HBM, VMEM],
        out_specs=(VMEM, VMEM),
        scratch_shapes=[pltpu.SemaphoreType.DMA((2,))],
        compiler_params=pltpu.CompilerParams(vmem_limit_bytes=4 * MIB),
        cost_estimate=pl.CostEstimate(flops=0, bytes_accessed=6_300_000, transcendentals=0),
        name="fetch",
    )(on_hbm(outer), on_hbm(inner), share)


def combine_kernel(
    scale,
    groups,
    bands,
    group_ref,
    band_ref,
    core_ref,
    *refs,
):
    shares = refs[:groups]
    (
        outer_ref,
        inner_ref,
        far_outer_ref,
        far_inner_ref,
        coef_ref,
        increment_hbm,
        adjoint_hbm,
        cost_hbm,
        increment,
        adjoint,
        cost_out,
        combined,
        sems,
    ) = refs[groups:]
    half = shares[0].shape[0] - 8
    rank = 2 * half
    fields, extended, lon = coef_ref.shape
    rows = extended - 2 * HALO
    core = core_ref[0]

    line = lax.broadcasted_iota(jnp.int32, (half, 2 * rank), 0)
    lane = lax.broadcasted_iota(jnp.int32, (half, 2 * rank), 1)
    left = lane < rank
    row = jnp.zeros((1, 2 * rank), jnp.float32)
    cost = jnp.zeros((1, 2 * rank), jnp.float32)
    for ahead in reversed(range(groups)):
        share = shares[ahead][...]
        cost += share[half + 1 : half + 2]
        upper = jnp.sum(jnp.where(lane == line, row, 0.0), axis=1, keepdims=True)
        lower = jnp.sum(jnp.where(lane == line + half, row, 0.0), axis=1, keepdims=True)
        product = jnp.sum(share[:half] * jnp.where(left, upper, lower), axis=0, keepdims=True)
        row = product + pltpu.roll(product, rank, 1) + share[half : half + 1]
        if ahead:
            row = jnp.where(group_ref[0] + ahead < groups, row, 0.0)
    adjoint[...] = row[:, :rank]
    cost_out[...] = cost
    copies = [
        pltpu.make_async_copy(adjoint, adjoint_hbm, sems.at[0]),
        pltpu.make_async_copy(cost_out, cost_hbm, sems.at[1]),
    ]
    for copy in copies:
        copy.start()

    pick = lax.broadcasted_iota(jnp.int32, (8, rank), 0)
    factor = jnp.zeros((8, rank), jnp.float32)
    for n, piece in enumerate(split3(row[:, :rank] * scale)):
        factor = jnp.where(pick == n, piece.astype(jnp.float32), factor)
    factor = factor.astype(jnp.bfloat16)
    places = (
        (outer_ref, HALO + core * HALO),
        (inner_ref, 2 * HALO - core * HALO),
        (far_outer_ref, core * (extended - HALO)),
        (far_inner_ref, (1 - core) * (extended - HALO)),
    )

    def one_field(f, carry):
        for ref, first in places:
            for r in range(HALO):
                part = lax.dot_general(
                    factor, ref[f * HALO + r], (((1,), (0,)), ((), ())), preferred_element_type=jnp.float32
                )
                combined[f, pl.ds(first + r, 1)] = jnp.sum(part, axis=0, keepdims=True)
        return carry

    lax.fori_loop(0, fields, one_field, 0)

    latitude = band_ref[0] * rows - HALO + lax.broadcasted_iota(jnp.int32, (extended, lon), 0)
    present = (latitude >= 0) & (latitude < rows * bands)
    turn = 0.5 * coriolis_coef * (2.0 * (latitude.astype(jnp.float32) + 0.5) / (rows * bands) - 1.0)
    combined[0] = 0.25 * combined[0]

    def lat_difference(x):
        return pltpu.roll(x, extended - 1, 0) - pltpu.roll(x, 1, 0)

    def step(_, carry):
        depth, east, north = (coef_ref[f] for f in range(3))
        h, u, v = (combined[f] for f in range(3))
        dxh, dxu, dxv = (lon_difference(x) for x in (h, u, v))
        dyh, dyu, dyv = (lat_difference(x) for x in (h, u, v))
        new_u = (u + turn * v) - dxh - east * dxu - north * dyu
        new_v = (v - turn * u) - dyh - east * dxv - north * dyv
        new_h = h - depth * (dxu + dyv) - east * dxh - north * dyh
        for f, x in enumerate((new_h, new_u, new_v)):
            combined[f] = jnp.where(present, x, 0.0)
        return carry

    lax.fori_loop(0, STEPS, step, 0)
    for f in range(fields):
        value = combined[f, HALO : HALO + rows]
        increment[0, f] = 4.0 * value if f == 0 else value
    copies.append(pltpu.make_async_copy(increment, increment_hbm, sems.at[2]))
    copies[-1].start()
    for copy in copies:
        copy.wait()


def combine(group, band, core, shares, halves, coef, scale, bands):
    fields, extended, lon = coef.shape
    rows = extended - 2 * HALO
    rank = halves[0].shape[1]
    return pl.pallas_call(
        functools.partial(combine_kernel, scale, len(shares), bands),
        out_shape=(
            jax.ShapeDtypeStruct((1, fields, rows, lon), jnp.float32),
            jax.ShapeDtypeStruct((1, rank), jnp.float32),
            jax.ShapeDtypeStruct((1, 2 * rank), jnp.float32),
        ),
        in_specs=[SMEM] * 3 + [VMEM] * (len(shares) + 5),
        out_specs=(HBM,) * 3,
        scratch_shapes=[
            pltpu.VMEM((1, fields, rows, lon), jnp.float32),
            pltpu.VMEM((1, rank), jnp.float32),
            pltpu.VMEM((1, 2 * rank), jnp.float32),
            pltpu.VMEM((fields, extended, lon), jnp.float32),
            pltpu.SemaphoreType.DMA((3,)),
        ],
        compiler_params=pltpu.CompilerParams(vmem_limit_bytes=8 * MIB),
        name="combine",
    )(group, band, core, *shares, *halves, coef)


def from_ahead(x, axis, by):
    count = lax.axis_size(axis)
    return lax.ppermute(x, axis, [((i + by) % count, i) for i in range(count)])


def added_over(x, axis):
    others = [from_ahead(x, axis, by) for by in range(1, lax.axis_size(axis))]
    return functools.reduce(jnp.add, others, x)


def body(
    sketch, test_sketch, checkpoints, checkpoint_step, station_row, station_column, station_value
):
    rank, fields, rows, lon = sketch.shape
    bands = lax.axis_size(LAT)
    groups = lax.axis_size("tm")
    total_rows = rows * bands
    band = lax.axis_index(LAT).astype(jnp.int32).reshape(1)
    core = lax.axis_index("lat_2").astype(jnp.int32).reshape(1)
    group = lax.axis_index("tm").astype(jnp.int32).reshape(1)

    outer_base, inner_base, base = pick(checkpoints, checkpoint_step, core)
    across_chips = [pair for i in range(1, bands - 1, 2) for pair in ((i, i + 1), (i + 1, i))]
    inside_chip = [(0, 1), (1, 0)]
    far_outer_base = lax.ppermute(outer_base, LAT, across_chips)
    far_inner_base = lax.ppermute(inner_base, "lat_2", inside_chip)
    outer, inner = pack(sketch, core)
    outer, inner, far_outer_base, far_inner_base = lax.optimization_barrier(
        (outer, inner, far_outer_base, far_inner_base)
    )
    far_outer = lax.ppermute(outer, LAT, across_chips)
    far_inner = lax.ppermute(inner, "lat_2", inside_chip)
    stations = (station_row, station_column, station_value)
    scales = (total_rows, station_row.shape[1] * bands, groups)
    scale = map_scale / math.sqrt(rank * fields * total_rows * lon)
    back, coef, tail = sweep(
        band, core, test_sketch, base, far_outer_base, far_inner_base, outer, inner, stations, scales, bands
    )
    share = join(core, back, tail, outer, inner, far_outer, far_inner, scale)
    for axis in ("lat_2", "lat_1", "lat_0"):
        share = added_over(share, axis)
    far_outer, far_inner = fetch(far_outer, far_inner, share)
    shares = [share] + [from_ahead(share, "tm", by) for by in range(1, groups)]
    increment, adjoint, total_cost = combine(
        group, band, core, shares, (outer, inner, far_outer, far_inner), coef, 1.0 / math.sqrt(rank), bands
    )
    return (increment, adjoint, total_cost[0, 0])


def solution(mesh):
    torus = Mesh(mesh.devices.reshape(mesh.shape["tm"], 4, 4, 2), ("tm", "lat_0", "lat_1", "lat_2"))
    in_specs = (
        P("tm", None, LAT, None),
        P("tm", None, LAT, None),
        P("tm", None, LAT, None),
        P("tm"),
        P("tm", LAT),
        P("tm", LAT),
        P("tm", LAT),
    )
    out_specs = (P("tm", None, LAT, None), P("tm", None), P())
    return jax.shard_map(body, mesh=torus, in_specs=in_specs, out_specs=out_specs, check_vma=False)
```

```python
import functools
import math

import jax
import jax.numpy as jnp
from jax import lax
from jax.experimental import pallas as pl
from jax.experimental.pallas import tpu as pltpu
from jax.sharding import Mesh
from jax.sharding import PartitionSpec as P

STEPS = 4
LAT = ("lat_0", "lat_1", "lat_2")
KC = 16
HALO = STEPS

flow_coef = 0.4
coriolis_coef = 0.5
map_scale = 0.5
MIB = 1 << 20

VMEM = pl.BlockSpec(memory_space=pltpu.VMEM)
SMEM = pl.BlockSpec(memory_space=pltpu.SMEM)
HBM = pl.BlockSpec(memory_space=pltpu.HBM)


def lon_difference(x):
    lon = x.shape[-1]
    return pltpu.roll(x, lon - 1, 1) - pltpu.roll(x, 1, 1)


def split3(x):
    high = x.astype(jnp.bfloat16)
    rest = x - high.astype(jnp.float32)
    middle = rest.astype(jnp.bfloat16)
    low = (rest - middle.astype(jnp.float32)).astype(jnp.bfloat16)
    return high, middle, low


def across(a, b):
    return lax.dot_general(a, b, (((1,), (1,)), ((), ())), preferred_element_type=jnp.float32)


def on_hbm(x):
    return pltpu.with_memory_space_constraint(x, pltpu.HBM)


def pick_kernel(step_ref, core_ref, base_hbm, outer_base, inner_base, base_ref, base, sems):
    fields = base.shape[0]
    copy = pltpu.make_async_copy(base_hbm.at[step_ref[0]], base, sems.at[0])
    copy.start()
    copy.wait()
    values = base[...].astype(jnp.float32)
    base_ref[...] = values
    pad = jnp.zeros((16 - fields * HALO, values.shape[-1]), jnp.float32)
    for core in range(2):
        low, high = (outer_base, inner_base) if core == 0 else (inner_base, outer_base)

        @pl.when(core_ref[0] == core)
        def _(low=low, high=high):
            for ref, at in ((low, 0), (high, HALO)):
                rows = [values[f, at : at + HALO] for f in range(fields)]
                ref[...] = jnp.concatenate([*rows, pad], axis=0).astype(jnp.bfloat16)


def pick(checkpoints, checkpoint_step, core):
    _, fields, rows, lon = checkpoints.shape
    lines = jax.ShapeDtypeStruct((16, lon), jnp.bfloat16)
    return pl.pallas_call(
        pick_kernel,
        out_shape=(lines, lines, jax.ShapeDtypeStruct((fields, rows, lon), jnp.float32)),
        in_specs=[SMEM, SMEM, HBM],
        out_specs=(VMEM,) * 3,
        scratch_shapes=[pltpu.VMEM((fields, rows, lon), jnp.bfloat16), pltpu.SemaphoreType.DMA((1,))],
        compiler_params=pltpu.CompilerParams(vmem_limit_bytes=8 * MIB),
        name="pick",
    )(checkpoint_step, core, on_hbm(checkpoints))


def pack_kernel(core_ref, sketch_hbm, outer_ref, inner_ref, sketch, sems):
    chunks = sketch.shape[0] // KC
    fields = sketch.shape[1]

    def copy(c):
        at = pl.ds(c * KC, KC)
        return pltpu.make_async_copy(sketch_hbm.at[at], sketch.at[at], sems.at[c])

    for c in range(chunks):
        copy(c).start()
    def chunk_body(c, carry):
        copy(c).wait()
        at = pl.ds(c * KC, KC)
        for core in range(2):
            low, high = (outer_ref, inner_ref) if core == 0 else (inner_ref, outer_ref)

            @pl.when(core_ref[0] == core)
            def _(low=low, high=high):
                for f in range(fields):
                    part = jnp.swapaxes(sketch[at, f].astype(jnp.float32), 0, 1)
                    part = part.astype(jnp.bfloat16)
                    for ref, rows in ((low, part[:HALO]), (high, part[HALO:])):
                        ref[f * HALO : (f + 1) * HALO, at] = rows

        return carry

    lax.fori_loop(0, chunks, chunk_body, 0)


def pack(sketch, core):
    rank, fields, rows, lon = sketch.shape
    half = jax.ShapeDtypeStruct((fields * HALO, rank, lon), jnp.bfloat16)
    return pl.pallas_call(
        pack_kernel,
        out_shape=(half, half),
        in_specs=[SMEM, HBM],
        out_specs=(VMEM,) * 2,
        scratch_shapes=[pltpu.VMEM(sketch.shape, sketch.dtype), pltpu.SemaphoreType.DMA((rank // KC,))],
        compiler_params=pltpu.CompilerParams(vmem_limit_bytes=8 * MIB),
        name="pack",
    )(core, on_hbm(sketch))


def observed(scales, band, height, station_row, station_column, station_value):
    total_rows, observations, groups = scales
    rows, lon = height.shape
    count = station_row.shape[-1]
    local = station_row - band * rows
    at_column = lax.broadcasted_iota(jnp.int32, (lon, count), 0) == station_column
    at_column = jnp.where(at_column, 1.0, 0.0).astype(jnp.bfloat16)
    at_row = lax.broadcasted_iota(jnp.int32, (rows, count), 0) == local
    found = lax.dot_general(
        height.astype(jnp.bfloat16), at_column, (((1,), (0,)), ((), ())), preferred_element_type=jnp.float32
    )
    here = jnp.sum(jnp.where(at_row, found, 0.0), axis=0, keepdims=True)
    innovation = here - station_value
    weight = 1.0 + 2.0 * station_row.astype(jnp.float32) / total_rows
    weighted = weight * innovation
    cost = jnp.sum(weighted * innovation, axis=1, keepdims=True) / (2.0 * groups * observations)
    spread = jnp.where(at_row, weighted / (2.0 * math.sqrt(observations)), 0.0)
    field = jnp.zeros((rows, lon), jnp.float32)
    for piece in split3(spread):
        field += across(piece, at_column)
    pieces = [piece.astype(jnp.float32) for piece in split3(field)]
    return jnp.concatenate(pieces, axis=0).astype(jnp.bfloat16), cost


def sweep_kernel(
    scales,
    bands,
    band_ref,
    core_ref,
    test_hbm,
    base_ref,
    outer_base,
    inner_base,
    outer_ref,
    inner_ref,
    station_row_ref,
    station_column_ref,
    station_value_ref,
    back_ref,
    coef_ref,
    tail_ref,
    test,
    one,
    two,
    coef,
    sems,
):
    rank, fields, rows, lon = test.shape
    extended = rows + 2 * HALO
    band, core = band_ref[0], core_ref[0]

    def copy(c):
        at = pl.ds(c * KC, KC)
        return pltpu.make_async_copy(test_hbm.at[at], test.at[at], sems.at[c])

    for c in range(rank // KC):
        copy(c).start()

    def latitude(e):
        return band * rows - HALO + e

    def inside(e):
        at = latitude(e)
        return jnp.where((at >= 0) & (at < rows * bands), 1.0, 0.0)

    def put(f, e, line):
        line = 0.0625 + 0.015625 * line if f == 0 else (0.2 * flow_coef) * line
        line = line * inside(e)
        coef[f, e] = jnp.broadcast_to(line, (8, lon))
        coef_ref[f, pl.ds(e, 1)] = line

    def own_row(r, carry):
        for f in range(fields):
            put(f, HALO + r, base_ref[f, pl.ds(r, 1)])
        return carry

    lax.fori_loop(0, rows, own_row, 0)
    for ref, first in ((outer_base, core), (inner_base, 1 - core)):
        values = ref[...].astype(jnp.float32)
        for f in range(fields):
            for r in range(HALO):
                put(f, first * (extended - HALO) + r, values[f * HALO + r : f * HALO + r + 1])

    forced = jnp.zeros((3 * rows, rank), jnp.float32)
    line = lax.broadcasted_iota(jnp.int32, (3 * rows, rank), 0) % rows
    field, cost = observed(
        scales, band, base_ref[0], station_row_ref[...], station_column_ref[...], station_value_ref[...]
    )
    for ref, first in ((outer_ref, core), (inner_ref, 1 - core)):
        for r in range(HALO):
            forced += jnp.where(line == first * HALO + r, across(field, ref[r]), 0.0)
    lane = lax.broadcasted_iota(jnp.int32, (8, rank), 0)
    forced = jnp.sum(forced, axis=0, keepdims=True)
    tail_ref[...] = jnp.where(lane == 0, forced, jnp.where(lane == 1, cost, 0.0))

    turns = [
        0.5 * coriolis_coef * (2.0 * (latitude(e).astype(jnp.float32) + 0.5) / (rows * bands) - 1.0)
        for e in range(extended)
    ]
    insides = [inside(e) for e in range(extended)]

    def terms(source, e, at):
        depth, east, north = (coef[f, e] for f in range(3))
        h, u, v = (source[e, f, at] for f in range(3))
        deep = depth * h
        mine = (
            h + lon_difference(u + east * h),
            u - turns[e] * v + lon_difference(east * u + deep),
            v + turns[e] * u + lon_difference(east * v),
        )
        edge = v if HALO <= e < HALO + rows else insides[e] * v
        beside = (edge + north * h, north * u, north * v + deep)
        return mine, beside

    def keep(target, c, e, f, half, total):
        target[e, f, pl.ds(half * 8, 8)] = total

    def keep_parts(target, c, e, f, half, total):
        if f == 0:
            total = 0.25 * total
        upper = total.astype(jnp.bfloat16)
        lower = (total - upper.astype(jnp.float32)).astype(jnp.bfloat16)
        at = c * KC + half * 8
        back_ref[f * extended + e, pl.ds(at, 8)] = upper
        back_ref[f * extended + e, pl.ds(rank + at, 8)] = lower

    def backward_step(source, target, first, last, c, half, store):
        at = pl.ds(half * 8, 8)
        before = here = mine = None
        for e in range(first - 1, last + 2):
            after_mine, after = terms(source, e + 1, at) if e + 1 <= last else (None, None)
            for f in range(fields):
                total = mine[f] if mine is not None else None
                if after is not None:
                    total = after[f] if total is None else total + after[f]
                if before is not None:
                    total = -before[f] if total is None else total - before[f]
                store(target, c, e, f, half, total)
            before, here, mine = here, after, after_mine

    def chunk_body(c, carry):
        copy(c).wait()
        for half in range(KC // 8):
            at = pl.ds(half * 8, 8)
            for f in range(fields):
                part = test[pl.ds(c * KC + half * 8, 8), f].astype(jnp.float32)
                part = jnp.swapaxes(part, 0, 1)
                for r in range(rows):
                    one[HALO + r, f, at] = 4.0 * part[r] if f == 0 else part[r]
            source, target = one, two
            for step in range(STEPS):
                store = keep if step < STEPS - 1 else keep_parts
                backward_step(source, target, HALO - step, HALO + rows - 1 + step, c, half, store)
                source, target = target, source
        return carry

    lax.fori_loop(0, rank // KC, chunk_body, 0)


def sweep(band, core, test_sketch, base, outer_base, inner_base, outer, inner, stations, scales, bands):
    rank, fields, rows, lon = test_sketch.shape
    extended = rows + 2 * HALO
    return pl.pallas_call(
        functools.partial(sweep_kernel, scales, bands),
        out_shape=(
            jax.ShapeDtypeStruct((fields * extended, 2 * rank, lon), jnp.bfloat16),
            jax.ShapeDtypeStruct((fields, extended, lon), jnp.float32),
            jax.ShapeDtypeStruct((8, rank), jnp.float32),
        ),
        in_specs=[SMEM, SMEM, HBM] + [VMEM] * 8,
        out_specs=(VMEM,) * 3,
        scratch_shapes=[
            pltpu.VMEM(test_sketch.shape, jnp.bfloat16),
            pltpu.VMEM((extended, fields, KC, lon), jnp.float32),
            pltpu.VMEM((extended, fields, KC, lon), jnp.float32),
            pltpu.VMEM((fields, extended, 8, lon), jnp.float32),
            pltpu.SemaphoreType.DMA((rank // KC,)),
        ],
        compiler_params=pltpu.CompilerParams(vmem_limit_bytes=24 * MIB),
        cost_estimate=pl.CostEstimate(flops=2_000_000_000, bytes_accessed=30_000_000, transcendentals=0),
        name="sweep",
    )(band, core, on_hbm(test_sketch), base, outer_base, inner_base, outer, inner, *stations)


def join_kernel(
    scale, core_ref, back_ref, tail_ref, outer_ref, inner_ref, outer_hbm, inner_hbm, share_ref, outer, inner, sums, sems
):
    rank = tail_ref.shape[1]
    extended = back_ref.shape[0] // 3
    core = core_ref[0]
    pieces = 3
    step = outer.shape[0] // pieces
    sides = ((inner_hbm, inner, 1 - core), (outer_hbm, outer, core))

    def copy(s, n):
        at = pl.ds(n * step, step)
        return pltpu.make_async_copy(sides[s][0].at[at], sides[s][1].at[at], sems.at[s * pieces + n])

    for s in range(2):
        for n in range(pieces):
            copy(s, n).start()
    def products(places):
        total = jnp.zeros((2 * rank, rank), jnp.float32)
        for ref, first in places:
            for i in range(ref.shape[0]):
                total += across(back_ref[i // HALO * extended + first + i % HALO], ref[i])
        return total

    for at in range(2):

        @pl.when(core == at)
        def _(at=at):
            sums[...] = products(((outer_ref, HALO + at * HALO), (inner_ref, 2 * HALO - at * HALO)))

    for s in range(2):
        for n in range(pieces):
            copy(s, n).wait()
    for at in range(2):

        @pl.when(core == at)
        def _(at=at):
            sums[...] += products(
                ((inner, (1 - at) * (extended - HALO)), (outer, at * (extended - HALO)))
            )

    share = sums[...]
    share = (share[:rank] + share[rank:]) * scale
    half = rank // 2
    share_ref[:half] = jnp.concatenate([share[:half], share[half:]], axis=1)
    tail = tail_ref[...]
    share_ref[half:] = jnp.concatenate([tail, tail], axis=1)


def join(core, back, tail, outer, inner, far_outer, far_inner, scale):
    rank = tail.shape[1]
    return pl.pallas_call(
        functools.partial(join_kernel, scale),
        out_shape=jax.ShapeDtypeStruct((rank // 2 + 8, 2 * rank), jnp.float32),
        in_specs=[SMEM, VMEM, VMEM, VMEM, VMEM, HBM, HBM],
        out_specs=VMEM,
        scratch_shapes=[
            pltpu.VMEM(outer.shape, outer.dtype),
            pltpu.VMEM(inner.shape, inner.dtype),
            pltpu.VMEM((2 * rank, rank), jnp.float32),
            pltpu.SemaphoreType.DMA((6,)),
        ],
        compiler_params=pltpu.CompilerParams(vmem_limit_bytes=8 * MIB),
        name="join",
    )(core, back, tail, outer, inner, on_hbm(far_outer), on_hbm(far_inner))


def fetch_kernel(outer_hbm, inner_hbm, share_ref, outer_ref, inner_ref, sems):
    copies = [
        pltpu.make_async_copy(outer_hbm, outer_ref, sems.at[0]),
        pltpu.make_async_copy(inner_hbm, inner_ref, sems.at[1]),
    ]
    for copy in copies:
        copy.start()
    for copy in copies:
        copy.wait()


def fetch(outer, inner, share):
    received = jax.ShapeDtypeStruct(outer.shape, outer.dtype)
    return pl.pallas_call(
        fetch_kernel,
        out_shape=(received, received),
        in_specs=[HBM, HBM, VMEM],
        out_specs=(VMEM, VMEM),
        scratch_shapes=[pltpu.SemaphoreType.DMA((2,))],
        compiler_params=pltpu.CompilerParams(vmem_limit_bytes=4 * MIB),
        cost_estimate=pl.CostEstimate(flops=0, bytes_accessed=6_300_000, transcendentals=0),
        name="fetch",
    )(on_hbm(outer), on_hbm(inner), share)


def combine_kernel(
    scale,
    groups,
    bands,
    group_ref,
    band_ref,
    core_ref,
    *refs,
):
    shares = refs[:groups]
    (
        outer_ref,
        inner_ref,
        far_outer_ref,
        far_inner_ref,
        coef_ref,
        increment_hbm,
        adjoint_hbm,
        cost_hbm,
        increment,
        adjoint,
        cost_out,
        combined,
        sems,
    ) = refs[groups:]
    half = shares[0].shape[0] - 8
    rank = 2 * half
    fields, extended, lon = coef_ref.shape
    rows = extended - 2 * HALO
    core = core_ref[0]

    line = lax.broadcasted_iota(jnp.int32, (half, 2 * rank), 0)
    lane = lax.broadcasted_iota(jnp.int32, (half, 2 * rank), 1)
    left = lane < rank
    row = jnp.zeros((1, 2 * rank), jnp.float32)
    cost = jnp.zeros((1, 2 * rank), jnp.float32)
    places = dict(zip((0, *farthest_first(groups)), shares))
    for ahead in reversed(range(groups)):
        share = places[ahead][...]
        cost += share[half + 1 : half + 2]
        upper = jnp.sum(jnp.where(lane == line, row, 0.0), axis=1, keepdims=True)
        lower = jnp.sum(jnp.where(lane == line + half, row, 0.0), axis=1, keepdims=True)
        product = jnp.sum(share[:half] * jnp.where(left, upper, lower), axis=0, keepdims=True)
        row = product + pltpu.roll(product, rank, 1) + share[half : half + 1]
        if ahead:
            row = jnp.where(group_ref[0] + ahead < groups, row, 0.0)
    adjoint[...] = row[:, :rank]
    cost_out[...] = cost
    copies = [
        pltpu.make_async_copy(adjoint, adjoint_hbm, sems.at[0]),
        pltpu.make_async_copy(cost_out, cost_hbm, sems.at[1]),
    ]
    for copy in copies:
        copy.start()

    pick = lax.broadcasted_iota(jnp.int32, (8, rank), 0)
    factor = jnp.zeros((8, rank), jnp.float32)
    for n, piece in enumerate(split3(row[:, :rank] * scale)):
        factor = jnp.where(pick == n, piece.astype(jnp.float32), factor)
    factor = factor.astype(jnp.bfloat16)
    places = (
        (outer_ref, HALO + core * HALO),
        (inner_ref, 2 * HALO - core * HALO),
        (far_outer_ref, core * (extended - HALO)),
        (far_inner_ref, (1 - core) * (extended - HALO)),
    )

    def one_field(f, carry):
        for ref, first in places:
            for r in range(HALO):
                part = lax.dot_general(
                    factor, ref[f * HALO + r], (((1,), (0,)), ((), ())), preferred_element_type=jnp.float32
                )
                combined[f, pl.ds(first + r, 1)] = jnp.sum(part, axis=0, keepdims=True)
        return carry

    lax.fori_loop(0, fields, one_field, 0)

    latitude = band_ref[0] * rows - HALO + lax.broadcasted_iota(jnp.int32, (extended, lon), 0)
    present = (latitude >= 0) & (latitude < rows * bands)
    turn = 0.5 * coriolis_coef * (2.0 * (latitude.astype(jnp.float32) + 0.5) / (rows * bands) - 1.0)
    combined[0] = 0.25 * combined[0]

    def lat_difference(x):
        return pltpu.roll(x, extended - 1, 0) - pltpu.roll(x, 1, 0)

    def step(_, carry):
        depth, east, north = (coef_ref[f] for f in range(3))
        h, u, v = (combined[f] for f in range(3))
        dxh, dxu, dxv = (lon_difference(x) for x in (h, u, v))
        dyh, dyu, dyv = (lat_difference(x) for x in (h, u, v))
        new_u = (u + turn * v) - dxh - east * dxu - north * dyu
        new_v = (v - turn * u) - dyh - east * dxv - north * dyv
        new_h = h - depth * (dxu + dyv) - east * dxh - north * dyh
        for f, x in enumerate((new_h, new_u, new_v)):
            combined[f] = jnp.where(present, x, 0.0)
        return carry

    lax.fori_loop(0, STEPS, step, 0)
    for f in range(fields):
        value = combined[f, HALO : HALO + rows]
        increment[0, f] = 4.0 * value if f == 0 else value
    copies.append(pltpu.make_async_copy(increment, increment_hbm, sems.at[2]))
    copies[-1].start()
    for copy in copies:
        copy.wait()


def combine(group, band, core, shares, halves, coef, scale, bands):
    fields, extended, lon = coef.shape
    rows = extended - 2 * HALO
    rank = halves[0].shape[1]
    return pl.pallas_call(
        functools.partial(combine_kernel, scale, len(shares), bands),
        out_shape=(
            jax.ShapeDtypeStruct((1, fields, rows, lon), jnp.float32),
            jax.ShapeDtypeStruct((1, rank), jnp.float32),
            jax.ShapeDtypeStruct((1, 2 * rank), jnp.float32),
        ),
        in_specs=[SMEM] * 3 + [VMEM] * (len(shares) + 5),
        out_specs=(HBM,) * 3,
        scratch_shapes=[
            pltpu.VMEM((1, fields, rows, lon), jnp.float32),
            pltpu.VMEM((1, rank), jnp.float32),
            pltpu.VMEM((1, 2 * rank), jnp.float32),
            pltpu.VMEM((fields, extended, lon), jnp.float32),
            pltpu.SemaphoreType.DMA((3,)),
        ],
        compiler_params=pltpu.CompilerParams(vmem_limit_bytes=8 * MIB),
        name="combine",
    )(group, band, core, *shares, *halves, coef)


def from_ahead(x, axis, by):
    count = lax.axis_size(axis)
    return lax.ppermute(x, axis, [((i + by) % count, i) for i in range(count)])


def farthest_first(count):
    return sorted(range(1, count), key=lambda by: -min(by, count - by))


def added_over(x, axis):
    others = [from_ahead(x, axis, by) for by in farthest_first(lax.axis_size(axis))]
    return functools.reduce(jnp.add, others, x)


def body(
    sketch, test_sketch, checkpoints, checkpoint_step, station_row, station_column, station_value
):
    rank, fields, rows, lon = sketch.shape
    bands = lax.axis_size(LAT)
    groups = lax.axis_size("tm")
    total_rows = rows * bands
    band = lax.axis_index(LAT).astype(jnp.int32).reshape(1)
    core = lax.axis_index("lat_2").astype(jnp.int32).reshape(1)
    group = lax.axis_index("tm").astype(jnp.int32).reshape(1)

    outer_base, inner_base, base = pick(checkpoints, checkpoint_step, core)
    across_chips = [pair for i in range(1, bands - 1, 2) for pair in ((i, i + 1), (i + 1, i))]
    inside_chip = [(0, 1), (1, 0)]
    far_outer_base = lax.ppermute(outer_base, LAT, across_chips)
    far_inner_base = lax.ppermute(inner_base, "lat_2", inside_chip)
    outer, inner = pack(sketch, core)
    outer, inner, far_outer_base, far_inner_base = lax.optimization_barrier(
        (outer, inner, far_outer_base, far_inner_base)
    )
    far_outer = lax.ppermute(outer, LAT, across_chips)
    far_inner = lax.ppermute(inner, "lat_2", inside_chip)
    stations = (station_row, station_column, station_value)
    scales = (total_rows, station_row.shape[1] * bands, groups)
    scale = map_scale / math.sqrt(rank * fields * total_rows * lon)
    back, coef, tail = sweep(
        band, core, test_sketch, base, far_outer_base, far_inner_base, outer, inner, stations, scales, bands
    )
    share = join(core, back, tail, outer, inner, far_outer, far_inner, scale)
    for axis in ("lat_2", "lat_1", "lat_0"):
        share = added_over(share, axis)
    far_outer, far_inner = fetch(far_outer, far_inner, share)
    order = farthest_first(groups)
    shares = [share] + [from_ahead(share, "tm", by) for by in order]
    increment, adjoint, total_cost = combine(
        group, band, core, shares, (outer, inner, far_outer, far_inner), coef, 1.0 / math.sqrt(rank), bands
    )
    return (increment, adjoint, total_cost[0, 0])


def solution(mesh):
    torus = Mesh(mesh.devices.reshape(mesh.shape["tm"], 4, 4, 2), ("tm", "lat_0", "lat_1", "lat_2"))
    in_specs = (
        P("tm", None, LAT, None),
        P("tm", None, LAT, None),
        P("tm", None, LAT, None),
        P("tm"),
        P("tm", LAT),
        P("tm", LAT),
        P("tm", LAT),
    )
    out_specs = (P("tm", None, LAT, None), P("tm", None), P())
    return jax.shard_map(body, mesh=torus, in_specs=in_specs, out_specs=out_specs, check_vma=False)
```

```python
import functools
import math

import jax
import jax.numpy as jnp
from jax import lax
from jax.experimental import pallas as pl
from jax.experimental.pallas import tpu as pltpu
from jax.sharding import Mesh
from jax.sharding import PartitionSpec as P

STEPS = 4
LAT = ("lat_0", "lat_1", "lat_2")
KC = 16
HALO = STEPS

flow_coef = 0.4
coriolis_coef = 0.5
map_scale = 0.5
MIB = 1 << 20

VMEM = pl.BlockSpec(memory_space=pltpu.VMEM)
SMEM = pl.BlockSpec(memory_space=pltpu.SMEM)
HBM = pl.BlockSpec(memory_space=pltpu.HBM)


def lon_difference(x):
    lon = x.shape[-1]
    return pltpu.roll(x, lon - 1, 1) - pltpu.roll(x, 1, 1)


def split3(x):
    high = x.astype(jnp.bfloat16)
    rest = x - high.astype(jnp.float32)
    middle = rest.astype(jnp.bfloat16)
    low = (rest - middle.astype(jnp.float32)).astype(jnp.bfloat16)
    return high, middle, low


def across(a, b):
    return lax.dot_general(a, b, (((1,), (1,)), ((), ())), preferred_element_type=jnp.float32)


def on_hbm(x):
    return pltpu.with_memory_space_constraint(x, pltpu.HBM)


def pick_kernel(step_ref, core_ref, base_hbm, outer_base, inner_base, base_ref, base, sems):
    fields = base.shape[0]
    copy = pltpu.make_async_copy(base_hbm.at[step_ref[0]], base, sems.at[0])
    copy.start()
    copy.wait()
    values = base[...].astype(jnp.float32)
    base_ref[...] = values
    pad = jnp.zeros((16 - fields * HALO, values.shape[-1]), jnp.float32)
    for core in range(2):
        low, high = (outer_base, inner_base) if core == 0 else (inner_base, outer_base)

        @pl.when(core_ref[0] == core)
        def _(low=low, high=high):
            for ref, at in ((low, 0), (high, HALO)):
                rows = [values[f, at : at + HALO] for f in range(fields)]
                ref[...] = jnp.concatenate([*rows, pad], axis=0).astype(jnp.bfloat16)


def pick(checkpoints, checkpoint_step, core):
    _, fields, rows, lon = checkpoints.shape
    lines = jax.ShapeDtypeStruct((16, lon), jnp.bfloat16)
    return pl.pallas_call(
        pick_kernel,
        out_shape=(lines, lines, jax.ShapeDtypeStruct((fields, rows, lon), jnp.float32)),
        in_specs=[SMEM, SMEM, HBM],
        out_specs=(VMEM,) * 3,
        scratch_shapes=[pltpu.VMEM((fields, rows, lon), jnp.bfloat16), pltpu.SemaphoreType.DMA((1,))],
        compiler_params=pltpu.CompilerParams(vmem_limit_bytes=8 * MIB),
        name="pick",
    )(checkpoint_step, core, on_hbm(checkpoints))


def pack_kernel(core_ref, sketch_hbm, outer_ref, inner_ref, sketch, sems):
    chunks = sketch.shape[0] // KC
    fields = sketch.shape[1]

    def copy(c):
        at = pl.ds(c * KC, KC)
        return pltpu.make_async_copy(sketch_hbm.at[at], sketch.at[at], sems.at[c])

    for c in range(chunks):
        copy(c).start()
    def chunk_body(c, carry):
        copy(c).wait()
        at = pl.ds(c * KC, KC)
        for core in range(2):
            low, high = (outer_ref, inner_ref) if core == 0 else (inner_ref, outer_ref)

            @pl.when(core_ref[0] == core)
            def _(low=low, high=high):
                for f in range(fields):
                    part = jnp.swapaxes(sketch[at, f].astype(jnp.float32), 0, 1)
                    part = part.astype(jnp.bfloat16)
                    for ref, rows in ((low, part[:HALO]), (high, part[HALO:])):
                        ref[f * HALO : (f + 1) * HALO, at] = rows

        return carry

    lax.fori_loop(0, chunks, chunk_body, 0)


def pack(sketch, core):
    rank, fields, rows, lon = sketch.shape
    half = jax.ShapeDtypeStruct((fields * HALO, rank, lon), jnp.bfloat16)
    return pl.pallas_call(
        pack_kernel,
        out_shape=(half, half),
        in_specs=[SMEM, HBM],
        out_specs=(VMEM,) * 2,
        scratch_shapes=[pltpu.VMEM(sketch.shape, sketch.dtype), pltpu.SemaphoreType.DMA((rank // KC,))],
        compiler_params=pltpu.CompilerParams(vmem_limit_bytes=8 * MIB),
        name="pack",
    )(core, on_hbm(sketch))


def observed(scales, band, height, station_row, station_column, station_value):
    total_rows, observations, groups = scales
    rows, lon = height.shape
    count = station_row.shape[-1]
    local = station_row - band * rows
    at_column = lax.broadcasted_iota(jnp.int32, (lon, count), 0) == station_column
    at_column = jnp.where(at_column, 1.0, 0.0).astype(jnp.bfloat16)
    at_row = lax.broadcasted_iota(jnp.int32, (rows, count), 0) == local
    found = lax.dot_general(
        height.astype(jnp.bfloat16), at_column, (((1,), (0,)), ((), ())), preferred_element_type=jnp.float32
    )
    here = jnp.sum(jnp.where(at_row, found, 0.0), axis=0, keepdims=True)
    innovation = here - station_value
    weight = 1.0 + 2.0 * station_row.astype(jnp.float32) / total_rows
    weighted = weight * innovation
    cost = jnp.sum(weighted * innovation, axis=1, keepdims=True) / (2.0 * groups * observations)
    spread = jnp.where(at_row, weighted / (2.0 * math.sqrt(observations)), 0.0)
    field = jnp.zeros((rows, lon), jnp.float32)
    for piece in split3(spread):
        field += across(piece, at_column)
    pieces = [piece.astype(jnp.float32) for piece in split3(field)]
    return jnp.concatenate(pieces, axis=0).astype(jnp.bfloat16), cost


def sweep_kernel(
    scales,
    bands,
    band_ref,
    core_ref,
    test_hbm,
    base_ref,
    outer_base,
    inner_base,
    outer_ref,
    inner_ref,
    station_row_ref,
    station_column_ref,
    station_value_ref,
    back_ref,
    coef_ref,
    tail_ref,
    test,
    one,
    two,
    coef,
    sems,
):
    rank, fields, rows, lon = test.shape
    extended = rows + 2 * HALO
    band, core = band_ref[0], core_ref[0]

    def copy(c):
        at = pl.ds(c * KC, KC)
        return pltpu.make_async_copy(test_hbm.at[at], test.at[at], sems.at[c])

    for c in range(rank // KC):
        copy(c).start()

    def latitude(e):
        return band * rows - HALO + e

    def inside(e):
        at = latitude(e)
        return jnp.where((at >= 0) & (at < rows * bands), 1.0, 0.0)

    def put(f, e, line):
        line = 0.0625 + 0.015625 * line if f == 0 else (0.2 * flow_coef) * line
        line = line * inside(e)
        coef[f, e] = jnp.broadcast_to(line, (8, lon))
        coef_ref[f, pl.ds(e, 1)] = line

    def own_row(r, carry):
        for f in range(fields):
            put(f, HALO + r, base_ref[f, pl.ds(r, 1)])
        return carry

    lax.fori_loop(0, rows, own_row, 0)
    for ref, first in ((outer_base, core), (inner_base, 1 - core)):
        values = ref[...].astype(jnp.float32)
        for f in range(fields):
            for r in range(HALO):
                put(f, first * (extended - HALO) + r, values[f * HALO + r : f * HALO + r + 1])

    forced = jnp.zeros((3 * rows, rank), jnp.float32)
    line = lax.broadcasted_iota(jnp.int32, (3 * rows, rank), 0) % rows
    field, cost = observed(
        scales, band, base_ref[0], station_row_ref[...], station_column_ref[...], station_value_ref[...]
    )
    for ref, first in ((outer_ref, core), (inner_ref, 1 - core)):
        for r in range(HALO):
            forced += jnp.where(line == first * HALO + r, across(field, ref[r]), 0.0)
    lane = lax.broadcasted_iota(jnp.int32, (8, rank), 0)
    forced = jnp.sum(forced, axis=0, keepdims=True)
    tail_ref[...] = jnp.where(lane == 0, forced, jnp.where(lane == 1, cost, 0.0))

    turns = [
        0.5 * coriolis_coef * (2.0 * (latitude(e).astype(jnp.float32) + 0.5) / (rows * bands) - 1.0)
        for e in range(extended)
    ]
    insides = [inside(e) for e in range(extended)]

    def terms(source, e, at):
        depth, east, north = (coef[f, e] for f in range(3))
        h, u, v = (source[e, f, at] for f in range(3))
        deep = depth * h
        mine = (
            h + lon_difference(u + east * h),
            u - turns[e] * v + lon_difference(east * u + deep),
            v + turns[e] * u + lon_difference(east * v),
        )
        edge = v if HALO <= e < HALO + rows else insides[e] * v
        beside = (edge + north * h, north * u, north * v + deep)
        return mine, beside

    def keep(target, c, e, f, half, total):
        target[e, f, pl.ds(half * 8, 8)] = total

    def keep_parts(target, c, e, f, half, total):
        if f == 0:
            total = 0.25 * total
        upper = total.astype(jnp.bfloat16)
        lower = (total - upper.astype(jnp.float32)).astype(jnp.bfloat16)
        at = c * KC + half * 8
        back_ref[f * extended + e, pl.ds(at, 8)] = upper
        back_ref[f * extended + e, pl.ds(rank + at, 8)] = lower

    def backward_step(source, target, first, last, c, half, store):
        at = pl.ds(half * 8, 8)
        before = here = mine = None
        for e in range(first - 1, last + 2):
            after_mine, after = terms(source, e + 1, at) if e + 1 <= last else (None, None)
            for f in range(fields):
                total = mine[f] if mine is not None else None
                if after is not None:
                    total = after[f] if total is None else total + after[f]
                if before is not None:
                    total = -before[f] if total is None else total - before[f]
                store(target, c, e, f, half, total)
            before, here, mine = here, after, after_mine

    def chunk_body(c, carry):
        copy(c).wait()
        for half in range(KC // 8):
            at = pl.ds(half * 8, 8)
            for f in range(fields):
                part = test[pl.ds(c * KC + half * 8, 8), f].astype(jnp.float32)
                part = jnp.swapaxes(part, 0, 1)
                for r in range(rows):
                    one[HALO + r, f, at] = 4.0 * part[r] if f == 0 else part[r]
            source, target = one, two
            for step in range(STEPS):
                store = keep if step < STEPS - 1 else keep_parts
                backward_step(source, target, HALO - step, HALO + rows - 1 + step, c, half, store)
                source, target = target, source
        return carry

    lax.fori_loop(0, rank // KC, chunk_body, 0)


def sweep(band, core, test_sketch, base, outer_base, inner_base, outer, inner, stations, scales, bands):
    rank, fields, rows, lon = test_sketch.shape
    extended = rows + 2 * HALO
    return pl.pallas_call(
        functools.partial(sweep_kernel, scales, bands),
        out_shape=(
            jax.ShapeDtypeStruct((fields * extended, 2 * rank, lon), jnp.bfloat16),
            jax.ShapeDtypeStruct((fields, extended, lon), jnp.float32),
            jax.ShapeDtypeStruct((8, rank), jnp.float32),
        ),
        in_specs=[SMEM, SMEM, HBM] + [VMEM] * 8,
        out_specs=(VMEM,) * 3,
        scratch_shapes=[
            pltpu.VMEM(test_sketch.shape, jnp.bfloat16),
            pltpu.VMEM((extended, fields, KC, lon), jnp.float32),
            pltpu.VMEM((extended, fields, KC, lon), jnp.float32),
            pltpu.VMEM((fields, extended, 8, lon), jnp.float32),
            pltpu.SemaphoreType.DMA((rank // KC,)),
        ],
        compiler_params=pltpu.CompilerParams(vmem_limit_bytes=24 * MIB),
        cost_estimate=pl.CostEstimate(flops=2_000_000_000, bytes_accessed=30_000_000, transcendentals=0),
        name="sweep",
    )(band, core, on_hbm(test_sketch), base, outer_base, inner_base, outer, inner, *stations)


def join_kernel(
    scale, core_ref, back_ref, tail_ref, outer_ref, inner_ref, outer_hbm, inner_hbm, share_ref, outer, inner, sums, sems
):
    rank = tail_ref.shape[1]
    extended = back_ref.shape[0] // 3
    core = core_ref[0]
    pieces = 3
    step = outer.shape[0] // pieces
    sides = ((inner_hbm, inner, 1 - core), (outer_hbm, outer, core))

    def copy(s, n):
        at = pl.ds(n * step, step)
        return pltpu.make_async_copy(sides[s][0].at[at], sides[s][1].at[at], sems.at[s * pieces + n])

    for s in range(2):
        for n in range(pieces):
            copy(s, n).start()
    def products(places):
        total = jnp.zeros((2 * rank, rank), jnp.float32)
        for ref, first in places:
            for i in range(ref.shape[0]):
                total += across(back_ref[i // HALO * extended + first + i % HALO], ref[i])
        return total

    for at in range(2):

        @pl.when(core == at)
        def _(at=at):
            sums[...] = products(((outer_ref, HALO + at * HALO), (inner_ref, 2 * HALO - at * HALO)))

    for s in range(2):
        for n in range(pieces):
            copy(s, n).wait()
    for at in range(2):

        @pl.when(core == at)
        def _(at=at):
            sums[...] += products(
                ((inner, (1 - at) * (extended - HALO)), (outer, at * (extended - HALO)))
            )

    share = sums[...]
    share = (share[:rank] + share[rank:]) * scale
    half = rank // 2
    share_ref[:half] = jnp.concatenate([share[:half], share[half:]], axis=1)
    tail = tail_ref[...]
    share_ref[half:] = jnp.concatenate([tail, tail], axis=1)


def join(core, back, tail, outer, inner, far_outer, far_inner, scale):
    rank = tail.shape[1]
    return pl.pallas_call(
        functools.partial(join_kernel, scale),
        out_shape=jax.ShapeDtypeStruct((rank // 2 + 8, 2 * rank), jnp.float32),
        in_specs=[SMEM, VMEM, VMEM, VMEM, VMEM, HBM, HBM],
        out_specs=VMEM,
        scratch_shapes=[
            pltpu.VMEM(outer.shape, outer.dtype),
            pltpu.VMEM(inner.shape, inner.dtype),
            pltpu.VMEM((2 * rank, rank), jnp.float32),
            pltpu.SemaphoreType.DMA((6,)),
        ],
        compiler_params=pltpu.CompilerParams(vmem_limit_bytes=8 * MIB),
        name="join",
    )(core, back, tail, outer, inner, on_hbm(far_outer), on_hbm(far_inner))


def fetch_kernel(outer_hbm, inner_hbm, share_ref, outer_ref, inner_ref, sems):
    copies = [
        pltpu.make_async_copy(outer_hbm, outer_ref, sems.at[0]),
        pltpu.make_async_copy(inner_hbm, inner_ref, sems.at[1]),
    ]
    for copy in copies:
        copy.start()
    for copy in copies:
        copy.wait()


def fetch(outer, inner, share):
    received = jax.ShapeDtypeStruct(outer.shape, outer.dtype)
    return pl.pallas_call(
        fetch_kernel,
        out_shape=(received, received),
        in_specs=[HBM, HBM, VMEM],
        out_specs=(VMEM, VMEM),
        scratch_shapes=[pltpu.SemaphoreType.DMA((2,))],
        compiler_params=pltpu.CompilerParams(vmem_limit_bytes=4 * MIB),
        cost_estimate=pl.CostEstimate(flops=0, bytes_accessed=6_300_000, transcendentals=0),
        name="fetch",
    )(on_hbm(outer), on_hbm(inner), share)


def combine_kernel(
    scale,
    groups,
    bands,
    group_ref,
    band_ref,
    core_ref,
    *refs,
):
    shares = refs[:groups]
    (
        outer_ref,
        inner_ref,
        far_outer_ref,
        far_inner_ref,
        coef_ref,
        increment_hbm,
        adjoint_hbm,
        cost_hbm,
        increment,
        adjoint,
        cost_out,
        combined,
        sems,
    ) = refs[groups:]
    half = shares[0].shape[0] - 8
    rank = 2 * half
    fields, extended, lon = coef_ref.shape
    rows = extended - 2 * HALO
    core = core_ref[0]

    line = lax.broadcasted_iota(jnp.int32, (half, 2 * rank), 0)
    lane = lax.broadcasted_iota(jnp.int32, (half, 2 * rank), 1)
    left = lane < rank
    row = jnp.zeros((1, 2 * rank), jnp.float32)
    cost = jnp.zeros((1, 2 * rank), jnp.float32)
    places = dict(zip((0, *nearest_first(groups)), shares))
    for ahead in reversed(range(groups)):
        share = places[ahead][...]
        cost += share[half + 1 : half + 2]
        upper = jnp.sum(jnp.where(lane == line, row, 0.0), axis=1, keepdims=True)
        lower = jnp.sum(jnp.where(lane == line + half, row, 0.0), axis=1, keepdims=True)
        product = jnp.sum(share[:half] * jnp.where(left, upper, lower), axis=0, keepdims=True)
        row = product + pltpu.roll(product, rank, 1) + share[half : half + 1]
        if ahead:
            row = jnp.where(group_ref[0] + ahead < groups, row, 0.0)
    adjoint[...] = row[:, :rank]
    cost_out[...] = cost
    copies = [
        pltpu.make_async_copy(adjoint, adjoint_hbm, sems.at[0]),
        pltpu.make_async_copy(cost_out, cost_hbm, sems.at[1]),
    ]
    for copy in copies:
        copy.start()

    pick = lax.broadcasted_iota(jnp.int32, (8, rank), 0)
    factor = jnp.zeros((8, rank), jnp.float32)
    for n, piece in enumerate(split3(row[:, :rank] * scale)):
        factor = jnp.where(pick == n, piece.astype(jnp.float32), factor)
    factor = factor.astype(jnp.bfloat16)
    places = (
        (outer_ref, HALO + core * HALO),
        (inner_ref, 2 * HALO - core * HALO),
        (far_outer_ref, core * (extended - HALO)),
        (far_inner_ref, (1 - core) * (extended - HALO)),
    )

    def one_field(f, carry):
        for ref, first in places:
            for r in range(HALO):
                part = lax.dot_general(
                    factor, ref[f * HALO + r], (((1,), (0,)), ((), ())), preferred_element_type=jnp.float32
                )
                combined[f, pl.ds(first + r, 1)] = jnp.sum(part, axis=0, keepdims=True)
        return carry

    lax.fori_loop(0, fields, one_field, 0)

    latitude = band_ref[0] * rows - HALO + lax.broadcasted_iota(jnp.int32, (extended, lon), 0)
    present = (latitude >= 0) & (latitude < rows * bands)
    turn = 0.5 * coriolis_coef * (2.0 * (latitude.astype(jnp.float32) + 0.5) / (rows * bands) - 1.0)
    combined[0] = 0.25 * combined[0]

    def lat_difference(x):
        return pltpu.roll(x, extended - 1, 0) - pltpu.roll(x, 1, 0)

    def step(_, carry):
        depth, east, north = (coef_ref[f] for f in range(3))
        h, u, v = (combined[f] for f in range(3))
        dxh, dxu, dxv = (lon_difference(x) for x in (h, u, v))
        dyh, dyu, dyv = (lat_difference(x) for x in (h, u, v))
        new_u = (u + turn * v) - dxh - east * dxu - north * dyu
        new_v = (v - turn * u) - dyh - east * dxv - north * dyv
        new_h = h - depth * (dxu + dyv) - east * dxh - north * dyh
        for f, x in enumerate((new_h, new_u, new_v)):
            combined[f] = jnp.where(present, x, 0.0)
        return carry

    lax.fori_loop(0, STEPS, step, 0)
    for f in range(fields):
        value = combined[f, HALO : HALO + rows]
        increment[0, f] = 4.0 * value if f == 0 else value
    copies.append(pltpu.make_async_copy(increment, increment_hbm, sems.at[2]))
    copies[-1].start()
    for copy in copies:
        copy.wait()


def combine(group, band, core, shares, halves, coef, scale, bands):
    fields, extended, lon = coef.shape
    rows = extended - 2 * HALO
    rank = halves[0].shape[1]
    return pl.pallas_call(
        functools.partial(combine_kernel, scale, len(shares), bands),
        out_shape=(
            jax.ShapeDtypeStruct((1, fields, rows, lon), jnp.float32),
            jax.ShapeDtypeStruct((1, rank), jnp.float32),
            jax.ShapeDtypeStruct((1, 2 * rank), jnp.float32),
        ),
        in_specs=[SMEM] * 3 + [VMEM] * (len(shares) + 5),
        out_specs=(HBM,) * 3,
        scratch_shapes=[
            pltpu.VMEM((1, fields, rows, lon), jnp.float32),
            pltpu.VMEM((1, rank), jnp.float32),
            pltpu.VMEM((1, 2 * rank), jnp.float32),
            pltpu.VMEM((fields, extended, lon), jnp.float32),
            pltpu.SemaphoreType.DMA((3,)),
        ],
        compiler_params=pltpu.CompilerParams(vmem_limit_bytes=8 * MIB),
        name="combine",
    )(group, band, core, *shares, *halves, coef)


def from_ahead(x, axis, by):
    count = lax.axis_size(axis)
    return lax.ppermute(x, axis, [((i + by) % count, i) for i in range(count)])


def nearest_first(count):
    return sorted(range(1, count), key=lambda by: min(by, count - by))


def added_over(x, axis):
    others = [from_ahead(x, axis, by) for by in nearest_first(lax.axis_size(axis))]
    return functools.reduce(jnp.add, others, x)


def body(
    sketch, test_sketch, checkpoints, checkpoint_step, station_row, station_column, station_value
):
    rank, fields, rows, lon = sketch.shape
    bands = lax.axis_size(LAT)
    groups = lax.axis_size("tm")
    total_rows = rows * bands
    band = lax.axis_index(LAT).astype(jnp.int32).reshape(1)
    core = lax.axis_index("lat_2").astype(jnp.int32).reshape(1)
    group = lax.axis_index("tm").astype(jnp.int32).reshape(1)

    outer_base, inner_base, base = pick(checkpoints, checkpoint_step, core)
    across_chips = [pair for i in range(1, bands - 1, 2) for pair in ((i, i + 1), (i + 1, i))]
    inside_chip = [(0, 1), (1, 0)]
    far_outer_base = lax.ppermute(outer_base, LAT, across_chips)
    far_inner_base = lax.ppermute(inner_base, "lat_2", inside_chip)
    outer, inner = pack(sketch, core)
    outer, inner, far_outer_base, far_inner_base = lax.optimization_barrier(
        (outer, inner, far_outer_base, far_inner_base)
    )
    far_outer = lax.ppermute(outer, LAT, across_chips)
    far_inner = lax.ppermute(inner, "lat_2", inside_chip)
    stations = (station_row, station_column, station_value)
    scales = (total_rows, station_row.shape[1] * bands, groups)
    scale = map_scale / math.sqrt(rank * fields * total_rows * lon)
    back, coef, tail = sweep(
        band, core, test_sketch, base, far_outer_base, far_inner_base, outer, inner, stations, scales, bands
    )
    share = join(core, back, tail, outer, inner, far_outer, far_inner, scale)
    for axis in ("lat_2", "lat_1", "lat_0"):
        share = added_over(share, axis)
    far_outer, far_inner = fetch(far_outer, far_inner, share)
    order = nearest_first(groups)
    shares = [share] + [from_ahead(share, "tm", by) for by in order]
    increment, adjoint, total_cost = combine(
        group, band, core, shares, (outer, inner, far_outer, far_inner), coef, 1.0 / math.sqrt(rank), bands
    )
    return (increment, adjoint, total_cost[0, 0])


def solution(mesh):
    torus = Mesh(mesh.devices.reshape(mesh.shape["tm"], 4, 4, 2), ("tm", "lat_0", "lat_1", "lat_2"))
    in_specs = (
        P("tm", None, LAT, None),
        P("tm", None, LAT, None),
        P("tm", None, LAT, None),
        P("tm"),
        P("tm", LAT),
        P("tm", LAT),
        P("tm", LAT),
    )
    out_specs = (P("tm", None, LAT, None), P("tm", None), P())
    return jax.shard_map(body, mesh=torus, in_specs=in_specs, out_specs=out_specs, check_vma=False)
```

```python
import functools
import math

import jax
import jax.numpy as jnp
from jax import lax
from jax.experimental import pallas as pl
from jax.experimental.pallas import tpu as pltpu
from jax.sharding import Mesh
from jax.sharding import PartitionSpec as P

STEPS = 4
LAT = ("lat_0", "lat_1", "lat_2")
KC = 16
HALO = STEPS

flow_coef = 0.4
coriolis_coef = 0.5
map_scale = 0.5
MIB = 1 << 20

VMEM = pl.BlockSpec(memory_space=pltpu.VMEM)
SMEM = pl.BlockSpec(memory_space=pltpu.SMEM)
HBM = pl.BlockSpec(memory_space=pltpu.HBM)


def lon_difference(x):
    lon = x.shape[-1]
    return pltpu.roll(x, lon - 1, 1) - pltpu.roll(x, 1, 1)


def split3(x):
    high = x.astype(jnp.bfloat16)
    rest = x - high.astype(jnp.float32)
    middle = rest.astype(jnp.bfloat16)
    low = (rest - middle.astype(jnp.float32)).astype(jnp.bfloat16)
    return high, middle, low


def across(a, b):
    return lax.dot_general(a, b, (((1,), (1,)), ((), ())), preferred_element_type=jnp.float32)


def on_hbm(x):
    return pltpu.with_memory_space_constraint(x, pltpu.HBM)


def pick_kernel(step_ref, core_ref, base_hbm, outer_base, inner_base, base_ref, base, sems):
    fields = base.shape[0]
    copy = pltpu.make_async_copy(base_hbm.at[step_ref[0]], base, sems.at[0])
    copy.start()
    copy.wait()
    values = base[...].astype(jnp.float32)
    base_ref[...] = values
    pad = jnp.zeros((16 - fields * HALO, values.shape[-1]), jnp.float32)
    for core in range(2):
        low, high = (outer_base, inner_base) if core == 0 else (inner_base, outer_base)

        @pl.when(core_ref[0] == core)
        def _(low=low, high=high):
            for ref, at in ((low, 0), (high, HALO)):
                rows = [values[f, at : at + HALO] for f in range(fields)]
                ref[...] = jnp.concatenate([*rows, pad], axis=0).astype(jnp.bfloat16)


def pick(checkpoints, checkpoint_step, core):
    _, fields, rows, lon = checkpoints.shape
    lines = jax.ShapeDtypeStruct((16, lon), jnp.bfloat16)
    return pl.pallas_call(
        pick_kernel,
        out_shape=(lines, lines, jax.ShapeDtypeStruct((fields, rows, lon), jnp.float32)),
        in_specs=[SMEM, SMEM, HBM],
        out_specs=(VMEM,) * 3,
        scratch_shapes=[pltpu.VMEM((fields, rows, lon), jnp.bfloat16), pltpu.SemaphoreType.DMA((1,))],
        compiler_params=pltpu.CompilerParams(vmem_limit_bytes=8 * MIB),
        name="pick",
    )(checkpoint_step, core, on_hbm(checkpoints))


def pack_kernel(core_ref, sketch_hbm, outer_ref, inner_ref, sketch, sems):
    chunks = sketch.shape[0] // KC
    fields = sketch.shape[1]

    def copy(c):
        at = pl.ds(c * KC, KC)
        return pltpu.make_async_copy(sketch_hbm.at[at], sketch.at[at], sems.at[c])

    for c in range(chunks):
        copy(c).start()
    def chunk_body(c, carry):
        copy(c).wait()
        at = pl.ds(c * KC, KC)
        for core in range(2):
            low, high = (outer_ref, inner_ref) if core == 0 else (inner_ref, outer_ref)

            @pl.when(core_ref[0] == core)
            def _(low=low, high=high):
                for f in range(fields):
                    part = jnp.swapaxes(sketch[at, f].astype(jnp.float32), 0, 1)
                    part = part.astype(jnp.bfloat16)
                    for ref, rows in ((low, part[:HALO]), (high, part[HALO:])):
                        ref[f * HALO : (f + 1) * HALO, at] = rows

        return carry

    lax.fori_loop(0, chunks, chunk_body, 0)


def pack(sketch, core):
    rank, fields, rows, lon = sketch.shape
    half = jax.ShapeDtypeStruct((fields * HALO, rank, lon), jnp.bfloat16)
    return pl.pallas_call(
        pack_kernel,
        out_shape=(half, half),
        in_specs=[SMEM, HBM],
        out_specs=(VMEM,) * 2,
        scratch_shapes=[pltpu.VMEM(sketch.shape, sketch.dtype), pltpu.SemaphoreType.DMA((rank // KC,))],
        compiler_params=pltpu.CompilerParams(vmem_limit_bytes=8 * MIB),
        name="pack",
    )(core, on_hbm(sketch))


def observed(scales, band, height, station_row, station_column, station_value):
    total_rows, observations, groups = scales
    rows, lon = height.shape
    count = station_row.shape[-1]
    local = station_row - band * rows
    at_column = lax.broadcasted_iota(jnp.int32, (lon, count), 0) == station_column
    at_column = jnp.where(at_column, 1.0, 0.0).astype(jnp.bfloat16)
    at_row = lax.broadcasted_iota(jnp.int32, (rows, count), 0) == local
    found = lax.dot_general(
        height.astype(jnp.bfloat16), at_column, (((1,), (0,)), ((), ())), preferred_element_type=jnp.float32
    )
    here = jnp.sum(jnp.where(at_row, found, 0.0), axis=0, keepdims=True)
    innovation = here - station_value
    weight = 1.0 + 2.0 * station_row.astype(jnp.float32) / total_rows
    weighted = weight * innovation
    cost = jnp.sum(weighted * innovation, axis=1, keepdims=True) / (2.0 * groups * observations)
    spread = jnp.where(at_row, weighted / (2.0 * math.sqrt(observations)), 0.0)
    field = jnp.zeros((rows, lon), jnp.float32)
    for piece in split3(spread):
        field += across(piece, at_column)
    pieces = [piece.astype(jnp.float32) for piece in split3(field)]
    return jnp.concatenate(pieces, axis=0).astype(jnp.bfloat16), cost


def sweep_kernel(
    scales,
    bands,
    band_ref,
    core_ref,
    test_hbm,
    base_ref,
    outer_base,
    inner_base,
    outer_ref,
    inner_ref,
    station_row_ref,
    station_column_ref,
    station_value_ref,
    back_ref,
    coef_ref,
    tail_ref,
    test,
    one,
    two,
    coef,
    sems,
):
    rank, fields, rows, lon = test.shape
    extended = rows + 2 * HALO
    band, core = band_ref[0], core_ref[0]

    def copy(c):
        at = pl.ds(c * KC, KC)
        return pltpu.make_async_copy(test_hbm.at[at], test.at[at], sems.at[c])

    for c in range(rank // KC):
        copy(c).start()

    def latitude(e):
        return band * rows - HALO + e

    def inside(e):
        at = latitude(e)
        return jnp.where((at >= 0) & (at < rows * bands), 1.0, 0.0)

    def put(f, e, line):
        line = 0.0625 + 0.015625 * line if f == 0 else (0.2 * flow_coef) * line
        line = line * inside(e)
        coef[f, e] = jnp.broadcast_to(line, (8, lon))
        coef_ref[f, pl.ds(e, 1)] = line

    def own_row(r, carry):
        for f in range(fields):
            put(f, HALO + r, base_ref[f, pl.ds(r, 1)])
        return carry

    lax.fori_loop(0, rows, own_row, 0)
    for ref, first in ((outer_base, core), (inner_base, 1 - core)):
        values = ref[...].astype(jnp.float32)
        for f in range(fields):
            for r in range(HALO):
                put(f, first * (extended - HALO) + r, values[f * HALO + r : f * HALO + r + 1])

    forced = jnp.zeros((3 * rows, rank), jnp.float32)
    line = lax.broadcasted_iota(jnp.int32, (3 * rows, rank), 0) % rows
    field, cost = observed(
        scales, band, base_ref[0], station_row_ref[...], station_column_ref[...], station_value_ref[...]
    )
    for ref, first in ((outer_ref, core), (inner_ref, 1 - core)):
        for r in range(HALO):
            forced += jnp.where(line == first * HALO + r, across(field, ref[r]), 0.0)
    lane = lax.broadcasted_iota(jnp.int32, (8, rank), 0)
    forced = jnp.sum(forced, axis=0, keepdims=True)
    tail_ref[...] = jnp.where(lane == 0, forced, jnp.where(lane == 1, cost, 0.0))

    turns = [
        0.5 * coriolis_coef * (2.0 * (latitude(e).astype(jnp.float32) + 0.5) / (rows * bands) - 1.0)
        for e in range(extended)
    ]
    insides = [inside(e) for e in range(extended)]

    def terms(source, e, at):
        depth, east, north = (coef[f, e] for f in range(3))
        h, u, v = (source[e, f, at] for f in range(3))
        deep = depth * h
        mine = (
            h + lon_difference(u + east * h),
            u - turns[e] * v + lon_difference(east * u + deep),
            v + turns[e] * u + lon_difference(east * v),
        )
        edge = v if HALO <= e < HALO + rows else insides[e] * v
        beside = (edge + north * h, north * u, north * v + deep)
        return mine, beside

    def keep(target, c, e, f, half, total):
        target[e, f, pl.ds(half * 8, 8)] = total

    def keep_parts(target, c, e, f, half, total):
        if f == 0:
            total = 0.25 * total
        upper = total.astype(jnp.bfloat16)
        lower = (total - upper.astype(jnp.float32)).astype(jnp.bfloat16)
        at = c * KC + half * 8
        back_ref[f * extended + e, pl.ds(at, 8)] = upper
        back_ref[f * extended + e, pl.ds(rank + at, 8)] = lower

    def backward_step(source, target, first, last, c, half, store):
        at = pl.ds(half * 8, 8)
        before = here = mine = None
        for e in range(first - 1, last + 2):
            after_mine, after = terms(source, e + 1, at) if e + 1 <= last else (None, None)
            for f in range(fields):
                total = mine[f] if mine is not None else None
                if after is not None:
                    total = after[f] if total is None else total + after[f]
                if before is not None:
                    total = -before[f] if total is None else total - before[f]
                store(target, c, e, f, half, total)
            before, here, mine = here, after, after_mine

    def chunk_body(c, carry):
        copy(c).wait()
        for half in range(KC // 8):
            at = pl.ds(half * 8, 8)
            for f in range(fields):
                part = test[pl.ds(c * KC + half * 8, 8), f].astype(jnp.float32)
                part = jnp.swapaxes(part, 0, 1)
                for r in range(rows):
                    one[HALO + r, f, at] = 4.0 * part[r] if f == 0 else part[r]
            source, target = one, two
            for step in range(STEPS):
                store = keep if step < STEPS - 1 else keep_parts
                backward_step(source, target, HALO - step, HALO + rows - 1 + step, c, half, store)
                source, target = target, source
        return carry

    lax.fori_loop(0, rank // KC, chunk_body, 0)


def sweep(band, core, test_sketch, base, outer_base, inner_base, outer, inner, stations, scales, bands):
    rank, fields, rows, lon = test_sketch.shape
    extended = rows + 2 * HALO
    return pl.pallas_call(
        functools.partial(sweep_kernel, scales, bands),
        out_shape=(
            jax.ShapeDtypeStruct((fields * extended, 2 * rank, lon), jnp.bfloat16),
            jax.ShapeDtypeStruct((fields, extended, lon), jnp.float32),
            jax.ShapeDtypeStruct((8, rank), jnp.float32),
        ),
        in_specs=[SMEM, SMEM, HBM] + [VMEM] * 8,
        out_specs=(VMEM,) * 3,
        scratch_shapes=[
            pltpu.VMEM(test_sketch.shape, jnp.bfloat16),
            pltpu.VMEM((extended, fields, KC, lon), jnp.float32),
            pltpu.VMEM((extended, fields, KC, lon), jnp.float32),
            pltpu.VMEM((fields, extended, 8, lon), jnp.float32),
            pltpu.SemaphoreType.DMA((rank // KC,)),
        ],
        compiler_params=pltpu.CompilerParams(vmem_limit_bytes=24 * MIB),
        cost_estimate=pl.CostEstimate(flops=2_000_000_000, bytes_accessed=30_000_000, transcendentals=0),
        name="sweep",
    )(band, core, on_hbm(test_sketch), base, outer_base, inner_base, outer, inner, *stations)


def join_kernel(
    scale, core_ref, back_ref, tail_ref, outer_ref, inner_ref, outer_hbm, inner_hbm, share_ref, outer, inner, sums, sems
):
    rank = tail_ref.shape[1]
    extended = back_ref.shape[0] // 3
    core = core_ref[0]
    pieces = 3
    step = outer.shape[0] // pieces
    sides = ((inner_hbm, inner, 1 - core), (outer_hbm, outer, core))

    def copy(s, n):
        at = pl.ds(n * step, step)
        return pltpu.make_async_copy(sides[s][0].at[at], sides[s][1].at[at], sems.at[s * pieces + n])

    for s in range(2):
        for n in range(pieces):
            copy(s, n).start()
    def products(places):
        total = jnp.zeros((2 * rank, rank), jnp.float32)
        for ref, first in places:
            for i in range(ref.shape[0]):
                total += across(back_ref[i // HALO * extended + first + i % HALO], ref[i])
        return total

    for at in range(2):

        @pl.when(core == at)
        def _(at=at):
            sums[...] = products(((outer_ref, HALO + at * HALO), (inner_ref, 2 * HALO - at * HALO)))

    for s in range(2):
        for n in range(pieces):
            copy(s, n).wait()
    for at in range(2):

        @pl.when(core == at)
        def _(at=at):
            sums[...] += products(
                ((inner, (1 - at) * (extended - HALO)), (outer, at * (extended - HALO)))
            )

    share = sums[...]
    share = (share[:rank] + share[rank:]) * scale
    half = rank // 2
    share_ref[:half] = jnp.concatenate([share[:half], share[half:]], axis=1)
    tail = tail_ref[...]
    share_ref[half:] = jnp.concatenate([tail, tail], axis=1)


def join(core, back, tail, outer, inner, far_outer, far_inner, scale):
    rank = tail.shape[1]
    return pl.pallas_call(
        functools.partial(join_kernel, scale),
        out_shape=jax.ShapeDtypeStruct((rank // 2 + 8, 2 * rank), jnp.float32),
        in_specs=[SMEM, VMEM, VMEM, VMEM, VMEM, HBM, HBM],
        out_specs=VMEM,
        scratch_shapes=[
            pltpu.VMEM(outer.shape, outer.dtype),
            pltpu.VMEM(inner.shape, inner.dtype),
            pltpu.VMEM((2 * rank, rank), jnp.float32),
            pltpu.SemaphoreType.DMA((6,)),
        ],
        compiler_params=pltpu.CompilerParams(vmem_limit_bytes=8 * MIB),
        name="join",
    )(core, back, tail, outer, inner, on_hbm(far_outer), on_hbm(far_inner))


def fetch_kernel(outer_hbm, inner_hbm, share_ref, outer_ref, inner_ref, sems):
    copies = [
        pltpu.make_async_copy(outer_hbm, outer_ref, sems.at[0]),
        pltpu.make_async_copy(inner_hbm, inner_ref, sems.at[1]),
    ]
    for copy in copies:
        copy.start()
    for copy in copies:
        copy.wait()


def fetch(outer, inner, share):
    received = jax.ShapeDtypeStruct(outer.shape, outer.dtype)
    return pl.pallas_call(
        fetch_kernel,
        out_shape=(received, received),
        in_specs=[HBM, HBM, VMEM],
        out_specs=(VMEM, VMEM),
        scratch_shapes=[pltpu.SemaphoreType.DMA((2,))],
        compiler_params=pltpu.CompilerParams(vmem_limit_bytes=4 * MIB),
        cost_estimate=pl.CostEstimate(flops=0, bytes_accessed=6_300_000, transcendentals=0),
        name="fetch",
    )(on_hbm(outer), on_hbm(inner), share)


def combine_kernel(
    scale,
    groups,
    bands,
    group_ref,
    band_ref,
    core_ref,
    *refs,
):
    shares = refs[:groups]
    (
        outer_ref,
        inner_ref,
        far_outer_ref,
        far_inner_ref,
        coef_ref,
        increment_hbm,
        adjoint_hbm,
        cost_hbm,
        increment,
        adjoint,
        cost_out,
        combined,
        sems,
    ) = refs[groups:]
    half = shares[0].shape[0] - 8
    rank = 2 * half
    fields, extended, lon = coef_ref.shape
    rows = extended - 2 * HALO
    core = core_ref[0]

    line = lax.broadcasted_iota(jnp.int32, (half, 2 * rank), 0)
    lane = lax.broadcasted_iota(jnp.int32, (half, 2 * rank), 1)
    left = lane < rank
    row = jnp.zeros((1, 2 * rank), jnp.float32)
    cost = jnp.zeros((1, 2 * rank), jnp.float32)
    for ahead in reversed(range(groups)):
        share = shares[ahead][...]
        cost += share[half + 1 : half + 2]
        upper = jnp.sum(jnp.where(lane == line, row, 0.0), axis=1, keepdims=True)
        lower = jnp.sum(jnp.where(lane == line + half, row, 0.0), axis=1, keepdims=True)
        product = jnp.sum(share[:half] * jnp.where(left, upper, lower), axis=0, keepdims=True)
        row = product + pltpu.roll(product, rank, 1) + share[half : half + 1]
        if ahead:
            row = jnp.where(group_ref[0] + ahead < groups, row, 0.0)
    adjoint[...] = row[:, :rank]
    cost_out[...] = cost
    copies = [
        pltpu.make_async_copy(adjoint, adjoint_hbm, sems.at[0]),
        pltpu.make_async_copy(cost_out, cost_hbm, sems.at[1]),
    ]
    for copy in copies:
        copy.start()

    pick = lax.broadcasted_iota(jnp.int32, (8, rank), 0)
    factor = jnp.zeros((8, rank), jnp.float32)
    for n, piece in enumerate(split3(row[:, :rank] * scale)):
        factor = jnp.where(pick == n, piece.astype(jnp.float32), factor)
    factor = factor.astype(jnp.bfloat16)
    places = (
        (outer_ref, HALO + core * HALO),
        (inner_ref, 2 * HALO - core * HALO),
        (far_outer_ref, core * (extended - HALO)),
        (far_inner_ref, (1 - core) * (extended - HALO)),
    )

    def one_field(f):
        for ref, first in places:
            for r in range(HALO):
                part = lax.dot_general(
                    factor, ref[f * HALO + r], (((1,), (0,)), ((), ())), preferred_element_type=jnp.float32
                )
                combined[f, pl.ds(first + r, 1)] = jnp.sum(part, axis=0, keepdims=True)

    for f in range(fields):
        one_field(f)

    latitude = band_ref[0] * rows - HALO + lax.broadcasted_iota(jnp.int32, (extended, lon), 0)
    present = (latitude >= 0) & (latitude < rows * bands)
    turn = 0.5 * coriolis_coef * (2.0 * (latitude.astype(jnp.float32) + 0.5) / (rows * bands) - 1.0)
    combined[0] = 0.25 * combined[0]

    def lat_difference(x):
        return pltpu.roll(x, extended - 1, 0) - pltpu.roll(x, 1, 0)

    def step():
        depth, east, north = (coef_ref[f] for f in range(3))
        h, u, v = (combined[f] for f in range(3))
        dxh, dxu, dxv = (lon_difference(x) for x in (h, u, v))
        dyh, dyu, dyv = (lat_difference(x) for x in (h, u, v))
        new_u = (u + turn * v) - dxh - east * dxu - north * dyu
        new_v = (v - turn * u) - dyh - east * dxv - north * dyv
        new_h = h - depth * (dxu + dyv) - east * dxh - north * dyh
        for f, x in enumerate((new_h, new_u, new_v)):
            combined[f] = jnp.where(present, x, 0.0)

    for _ in range(STEPS):
        step()
    for f in range(fields):
        value = combined[f, HALO : HALO + rows]
        increment[0, f] = 4.0 * value if f == 0 else value
    copies.append(pltpu.make_async_copy(increment, increment_hbm, sems.at[2]))
    copies[-1].start()
    for copy in copies:
        copy.wait()


def combine(group, band, core, shares, halves, coef, scale, bands):
    fields, extended, lon = coef.shape
    rows = extended - 2 * HALO
    rank = halves[0].shape[1]
    return pl.pallas_call(
        functools.partial(combine_kernel, scale, len(shares), bands),
        out_shape=(
            jax.ShapeDtypeStruct((1, fields, rows, lon), jnp.float32),
            jax.ShapeDtypeStruct((1, rank), jnp.float32),
            jax.ShapeDtypeStruct((1, 2 * rank), jnp.float32),
        ),
        in_specs=[SMEM] * 3 + [VMEM] * (len(shares) + 5),
        out_specs=(HBM,) * 3,
        scratch_shapes=[
            pltpu.VMEM((1, fields, rows, lon), jnp.float32),
            pltpu.VMEM((1, rank), jnp.float32),
            pltpu.VMEM((1, 2 * rank), jnp.float32),
            pltpu.VMEM((fields, extended, lon), jnp.float32),
            pltpu.SemaphoreType.DMA((3,)),
        ],
        compiler_params=pltpu.CompilerParams(vmem_limit_bytes=8 * MIB),
        name="combine",
    )(group, band, core, *shares, *halves, coef)


def from_ahead(x, axis, by):
    count = lax.axis_size(axis)
    return lax.ppermute(x, axis, [((i + by) % count, i) for i in range(count)])


def added_over(x, axis):
    others = [from_ahead(x, axis, by) for by in range(1, lax.axis_size(axis))]
    return functools.reduce(jnp.add, others, x)


def body(
    sketch, test_sketch, checkpoints, checkpoint_step, station_row, station_column, station_value
):
    rank, fields, rows, lon = sketch.shape
    bands = lax.axis_size(LAT)
    groups = lax.axis_size("tm")
    total_rows = rows * bands
    band = lax.axis_index(LAT).astype(jnp.int32).reshape(1)
    core = lax.axis_index("lat_2").astype(jnp.int32).reshape(1)
    group = lax.axis_index("tm").astype(jnp.int32).reshape(1)

    outer_base, inner_base, base = pick(checkpoints, checkpoint_step, core)
    across_chips = [pair for i in range(1, bands - 1, 2) for pair in ((i, i + 1), (i + 1, i))]
    inside_chip = [(0, 1), (1, 0)]
    far_outer_base = lax.ppermute(outer_base, LAT, across_chips)
    far_inner_base = lax.ppermute(inner_base, "lat_2", inside_chip)
    outer, inner = pack(sketch, core)
    outer, inner, far_outer_base, far_inner_base = lax.optimization_barrier(
        (outer, inner, far_outer_base, far_inner_base)
    )
    far_outer = lax.ppermute(outer, LAT, across_chips)
    far_inner = lax.ppermute(inner, "lat_2", inside_chip)
    stations = (station_row, station_column, station_value)
    scales = (total_rows, station_row.shape[1] * bands, groups)
    scale = map_scale / math.sqrt(rank * fields * total_rows * lon)
    back, coef, tail = sweep(
        band, core, test_sketch, base, far_outer_base, far_inner_base, outer, inner, stations, scales, bands
    )
    share = join(core, back, tail, outer, inner, far_outer, far_inner, scale)
    for axis in ("lat_2", "lat_1", "lat_0"):
        share = added_over(share, axis)
    far_outer, far_inner = fetch(far_outer, far_inner, share)
    shares = [share] + [from_ahead(share, "tm", by) for by in range(1, groups)]
    increment, adjoint, total_cost = combine(
        group, band, core, shares, (outer, inner, far_outer, far_inner), coef, 1.0 / math.sqrt(rank), bands
    )
    return (increment, adjoint, total_cost[0, 0])


def solution(mesh):
    torus = Mesh(mesh.devices.reshape(mesh.shape["tm"], 4, 4, 2), ("tm", "lat_0", "lat_1", "lat_2"))
    in_specs = (
        P("tm", None, LAT, None),
        P("tm", None, LAT, None),
        P("tm", None, LAT, None),
        P("tm"),
        P("tm", LAT),
        P("tm", LAT),
        P("tm", LAT),
    )
    out_specs = (P("tm", None, LAT, None), P("tm", None), P())
    return jax.shard_map(body, mesh=torus, in_specs=in_specs, out_specs=out_specs, check_vma=False)
```
